256 devices in a mesh: grp: 8 (over z), blk: 32 (over x, y, core).
Axes of the slice: x: 4, y: 4, z: 8, core: 2. Of those that a mesh axis runs over, the one named last changes fastest.
Arguments:
- tokens: bfloat16 [8, 4096, 1024], P('grp', 'blk'), may hold values from -40 to 40
- lengths: int32 [8, 16], P('grp'), may hold values from 1 to 2176, 4096 in all within a row
- owners: int32 [8], P('grp'), may hold values from 0 to 7
- prefix_cache: bfloat16 [8, 2048, 1024], P('grp', 'blk'), may hold values from -52 to 52
- routes: int32 [8, 4096, 2], P('grp', 'blk'), may hold values from 0 to 7, all different within a row; in each aligned block of 128 rows (0 to 127, 128 to 255, ..., all dimensions but the last counted through in order) at most 40 rows name the same one
- gates: float32 [8, 4096, 2], P('grp', 'blk'), may hold values from 0.2 to 1
- attn_gain: float32 [1024], replicated, may hold values from 0.5 to 1.5
- w_query: bfloat16 [1024, 512], replicated, may hold values from -0.5 to 0.5
- w_keyval: bfloat16 [1024, 1024], replicated, may hold values from -0.1875 to 0.1875
- w_out: bfloat16 [512, 1024], replicated, may hold values from -0.25 to 0.25
- moe_gain: float32 [1024], replicated, may hold values from 0.5 to 1.5
- w_gate: bfloat16 [32, 1024, 704], P('blk'), may hold values from -0.1875 to 0.1875
- w_up: bfloat16 [32, 1024, 704], P('blk'), may hold values from -0.1875 to 0.1875
- w_down: bfloat16 [32, 704, 1024], P('blk'), may hold values from -0.109375 to 0.109375
- final_gain: float32 [1024], replicated, may hold values from 0.5 to 1.5
- unembed: bfloat16 [1024, 32128], P(None, 'blk'), may hold values from -0.5 to 0.5
Outputs:
- hidden: bfloat16 [8, 4096, 1024], P('grp', 'blk')
- suffix_cache: bfloat16 [8, 4096, 1024], P('grp', 'blk')
- request_norm: float32 [8, 16], P('grp')
- greatest: float32 [8, 16], P('grp')
The draws below stay inside these ranges and needn't reach their ends.
Inputs may be any that keep to these rules, and one draw needn't show every extreme that they name: In each group the lengths sum to 4096, and the longest request has exactly 2176 tokens. `routes`: the two experts of a token differ. Within the 128 rows of one device no expert is named more than 40 times, and in some device's rows an expert is named exactly 40 times.
All inputs are finite; a program needn't handle non-finite values.
Results may differ from the reference program's by a relative error of at most 0.0052.
The reference program's roundings to bfloat16 on the way count: a program that leaves them out, or rounds other values in their place, can miss the bound.
Values may be sent and summed in bfloat16 or wider, within the bound.
No kernel may reach another device: no remote copies, remote signals or barrier semaphores. Data moves between devices by JAX's collectives and lax.ppermute only.
A program may use at most 128 MiB of HBM per device.

```python
import math
import jax
import jax.numpy as jnp
import numpy as np
from jax import lax

D = 1024
HEADS = 8
HEAD = 64
EXPERTS = 8
FF = 2816
VOCAB = 32128
REQS = 16
TOK_DEV = 128
CAP = 40
SPLIT = 4
TOK_GRP = 4096
PREFIX = 2048
MOST_LEN = 2176
N_GRP = 8
N_BLK = 32


def draw_tokens(key, part):
    base_key, row_key, col_key = jax.random.split(key, 3)
    full_shape = (N_GRP, TOK_GRP, D)
    base_values = jax.random.truncated_normal(base_key, -4.0, 4.0, full_shape, jnp.float32)
    row_spread = jnp.exp(jax.random.uniform(row_key, (N_GRP, TOK_GRP, 1), jnp.float32, -0.35, 0.35))
    rising = 1.0 + 2.0 * jnp.arange(TOK_GRP, dtype=jnp.float32)[None, :, None] / TOK_GRP
    column_spread = jnp.exp(jax.random.uniform(col_key, (1, 1, D), jnp.float32, -0.8, 0.8))
    return (base_values * row_spread * rising * column_spread).astype(jnp.bfloat16)


def draw_owners(key, part):
    offset_key, order_key = jax.random.split(jax.random.fold_in(key, 17), 2)
    group_ids = jnp.arange(N_GRP, dtype=jnp.int32)
    offsets = jax.random.randint(offset_key, (N_GRP,), 0, N_GRP, dtype=jnp.int32)
    owner_ids = ((group_ids - offsets + N_GRP) % N_GRP).astype(jnp.int32)
    order = jax.random.permutation(order_key, N_GRP).astype(jnp.int32)
    first_group = order[0]
    second_group = order[1]
    third_group = order[2]
    fourth_group = order[3]
    owner_ids = jnp.where(group_ids == first_group, (group_ids - 1 + N_GRP) % N_GRP, owner_ids)
    owner_ids = jnp.where(group_ids == second_group, (group_ids - N_GRP // 2 + N_GRP) % N_GRP, owner_ids)
    owner_ids = jnp.where(group_ids == third_group, N_GRP - 1, owner_ids)
    owner_ids = jnp.where(group_ids == fourth_group, 0, owner_ids)
    return owner_ids.astype(jnp.int32)


def draw_prefix_cache(key, part):
    base_key = jax.random.fold_in(key, 0)
    width_keys = HEADS * HEAD
    full_shape = (N_GRP, PREFIX, 2 * width_keys)
    values = jax.random.truncated_normal(base_key, -4.0, 4.0, full_shape, jnp.float32)
    return values.astype(jnp.bfloat16)


def block_levels(own_key, dims, shards, least, high):
    loudness, own = 1.0, jax.random.fold_in(own_key, 6)
    for axis_at, shards_of in shards:
        heights = jnp.exp(jax.random.uniform(jax.random.fold_in(own, axis_at), (shards_of,), jnp.float32, least / len(shards), high / len(shards)))
        loudness = loudness * jnp.repeat(heights, dims[axis_at] // shards_of).reshape([-1 if axis == axis_at else 1 for axis in range(len(dims))])
    return loudness


def length_profile(amount, total, most, skew):
    weights = [(1 << 20) // math.isqrt(grade ** skew) + 1 for grade in range(2, amount + 1)]
    rest, holding = total - most - (amount - 1), [1] * (amount - 1)
    while rest > 0:
        candidates = [i for i in range(amount - 1) if holding[i] < most]
        mass, remaining = sum([weights[i] for i in candidates]), rest
        for i in candidates:
            addition = min(most - holding[i], max(1, remaining * weights[i] // mass), rest)
            holding[i] = holding[i] + addition
            rest = rest - addition
    return np.array([most] + holding)


def ragged_sizes(rng, number_of, total, bound, lean):
    if number_of == 2:
        one = jax.random.randint(rng, (), max(1, total - bound), min(bound, total - 1) + 1)
        return jnp.stack([one, total - one])
    tallies = jnp.asarray(length_profile(number_of, total, bound, lean), jnp.int32)
    pairs = (number_of - 1) // 2
    donor, sink = tallies[1:1 + 2 * pairs:2], tallies[2:2 + 2 * pairs:2]
    room = jnp.minimum(donor - 1, bound - sink)
    shifted = jax.random.randint(jax.random.fold_in(rng, 1), (pairs,), 0, 1 << 20) % (room + 1)
    tallies = tallies.at[1:1 + 2 * pairs:2].set(donor - shifted).at[2:2 + 2 * pairs:2].set(sink + shifted)
    return tallies[jax.random.permutation(jax.random.fold_in(rng, 2), number_of)]


def shared_out(rng, own, number, rows, count, top, limit, skew):
    ranking = jax.random.permutation(rng, count)
    crowded, usual = portions_of(count, rows * top, limit, skew, True), portions_of(count, rows * top, limit, skew, False)
    places = jnp.arange(count)

    def named(sizes, rotation):
        used = int((sizes > 0).sum())
        fixed = max(1, used // 4)
        moved = fixed + (places - fixed + rotation * (used - fixed)) % max(1, count - fixed)
        return jnp.zeros((count,), jnp.int32).at[ranking[jnp.where(places < fixed, places, moved)]].set(jnp.asarray(sizes, jnp.int32))

    sizes = jnp.where(number % 4 == 0, named(crowded, number // 4), named(usual, number - number // 4 - 1))
    mixed = jax.random.permutation(jax.random.fold_in(own, 3), count)
    source_of, sink = mixed[0:count // 2 * 2:2], mixed[1:count // 2 * 2:2]
    slack = jnp.minimum(sizes[source_of] - 1, limit - sizes[sink]) // 2
    slack = jnp.where((source_of == ranking[0]) | (sink == ranking[0]) | (sizes[sink] == 0), 0, jnp.maximum(slack, 0))
    moved = jax.random.randint(jax.random.fold_in(own, 4), (count // 2,), 0, 1 << 20) % (slack + 1)
    sizes = sizes.at[source_of].add(-moved).at[sink].add(moved)
    items = jnp.searchsorted(jnp.cumsum(sizes), jnp.arange(rows * top), side="right").astype(jnp.int32)
    table = items.reshape(top, rows).T
    table = table[jax.random.permutation(jax.random.fold_in(own, 1), rows)]
    rotation = jax.random.randint(jax.random.fold_in(own, 2), (rows, 1), 0, top)
    return jnp.take_along_axis(table, (jnp.arange(top)[None, :] + rotation) % top, axis=1)


def portions_of(amount, total, reach, slope, full):
    weights = [(1 << 20) // math.isqrt(grade ** slope) + 1 for grade in range(1, amount + 1)]
    largest = reach if full else min(reach, max(-(-total // amount), total * weights[0] // sum(weights)))
    least = 1 if total - largest >= amount - 1 else 0
    counts, surplus = [largest] + [least] * (amount - 1), total - largest - least * (amount - 1)
    while surplus > 0:
        candidates = [i for i in range(1, amount) if counts[i] < largest] or [i for i in range(1, amount) if counts[i] < reach]
        whole, left = sum([weights[i] for i in candidates]), surplus
        for i in candidates:
            extra = min(reach - counts[i], max(1, left * weights[i] // whole), surplus)
            counts[i] = counts[i] + extra
            surplus = surplus - extra
    return np.array(counts)


def centred(own_key, shape, width, most, pieces=(), kind=jnp.bfloat16):
    entries = width * jax.random.normal(own_key, shape, jnp.float32)
    if pieces:
        entries = entries * block_levels(own_key, shape, pieces, -0.22, 0.18)
    return jnp.clip(entries, -most, most).astype(kind)


def setup_inputs(seed: int = 0) -> dict:
    arg_keys = jax.random.split(jax.random.key(seed), 17)
    tokens = draw_tokens(jax.random.fold_in(arg_keys[16], 71), 0)
    lengths = jax.vmap(lambda own: ragged_sizes(own, REQS, TOK_GRP, MOST_LEN, 2))(jax.random.split(arg_keys[1], N_GRP)).reshape((N_GRP, REQS)).astype(jnp.int32)
    owners = draw_owners(jax.random.fold_in(arg_keys[16], 71), 0)
    prefix_cache = draw_prefix_cache(jax.random.fold_in(arg_keys[16], 71), 0)
    routes_keys = jax.random.split(jax.random.fold_in(arg_keys[4], 1), N_GRP * TOK_GRP // TOK_DEV)
    routes_turns = jax.random.permutation(jax.random.fold_in(arg_keys[4], 3), N_GRP * TOK_GRP // TOK_DEV)
    routes = jax.vmap(lambda own, number: shared_out(jax.random.fold_in(arg_keys[4], 2), own, number, TOK_DEV, EXPERTS, 2, CAP, 2))(routes_keys, routes_turns).reshape((N_GRP, TOK_GRP, 2))
    gates = jnp.clip(0.2 + 0.8 * jax.random.uniform(arg_keys[5], (N_GRP, TOK_GRP, 2), jnp.float32) ** block_levels(arg_keys[5], (N_GRP, TOK_GRP, 2), ((0, 8), (1, 32)), -0.2, 0.2), 0.2, 1.0)
    attn_gain = jnp.clip(1.0 + 0.1 * jax.random.normal(arg_keys[6], (D,), jnp.float32), 0.5, 1.5)
    w_query = centred(arg_keys[7], (D, HEADS * HEAD), (D // 9) ** -0.5, 0.5)
    w_keyval = centred(arg_keys[8], (D, 2 * HEADS * HEAD), D ** -0.5, 0.1875)
    w_out = centred(arg_keys[9], (HEADS * HEAD, D), (HEADS * HEAD) ** -0.5, 0.25)
    moe_gain = jnp.clip(1.0 + 0.1 * jax.random.normal(arg_keys[10], (D,), jnp.float32), 0.5, 1.5)
    w_gate = centred(arg_keys[11], (EXPERTS * SPLIT, D, FF // SPLIT), D ** -0.5, 0.1875, ((0, 32),))
    w_up = centred(arg_keys[12], (EXPERTS * SPLIT, D, FF // SPLIT), D ** -0.5, 0.1875, ((0, 32),))
    w_down = centred(arg_keys[13], (EXPERTS * SPLIT, FF // SPLIT, D), FF ** -0.5, 0.109375, ((0, 32),))
    final_gain = jnp.clip(1.0 + 0.1 * jax.random.normal(arg_keys[14], (D,), jnp.float32), 0.5, 1.5)
    unembed = centred(arg_keys[15], (D, VOCAB), (D // 9) ** -0.5, 0.5, ((1, 32),))
    return {"tokens": tokens, "lengths": lengths, "owners": owners, "prefix_cache": prefix_cache, "routes": routes, "gates": gates, "attn_gain": attn_gain, "w_query": w_query, "w_keyval": w_keyval, "w_out": w_out, "moe_gain": moe_gain, "w_gate": w_gate, "w_up": w_up, "w_down": w_down, "final_gain": final_gain, "unembed": unembed}


epsilon = 1e-06
neg_big = -1e+30

def rms_scale(values, gain_vector):
    values = values.astype(jnp.float32)
    return values * lax.rsqrt(lax.optimization_barrier(jnp.mean(values * values, axis=-1, keepdims=True)) + epsilon) * gain_vector

def request_of(positions, end_points):
    return lax.optimization_barrier(jnp.sum((positions[:, None] >= end_points[None, :]).astype(jnp.int32), axis=1)).astype(jnp.int32)

def slot_targets(block_routes):
    flat_routes = block_routes.reshape(-1)
    onehot = (flat_routes[:, None] == jnp.arange(EXPERTS, dtype=jnp.int32)[None, :]).astype(jnp.int32)
    before = (jnp.cumsum(onehot, axis=0) - onehot).astype(jnp.int32)
    slot_index = lax.optimization_barrier(jnp.sum(before * onehot, axis=1)).astype(jnp.int32)
    return (flat_routes * CAP + slot_index).reshape(block_routes.shape)

def dispatch_matrix(targets):
    slot_ids = jnp.arange(EXPERTS * CAP, dtype=jnp.int32)
    matches = (targets[:, 0][None, :] == slot_ids[:, None]) | (targets[:, 1][None, :] == slot_ids[:, None])
    return matches.astype(jnp.bfloat16)

def reference(tokens, lengths, owners, prefix_cache, routes, gates, attn_gain, w_query, w_keyval, w_out, moe_gain, w_gate, w_up, w_down, final_gain, unembed):
    attn_width = HEADS * HEAD
    query_block = math.gcd(TOK_GRP, 512)
    positions = jnp.arange(TOK_GRP, dtype=jnp.int32)

    def one_group(group_inputs):
        stream, group_lengths, owner_id = group_inputs
        normed = rms_scale(stream, attn_gain).astype(jnp.bfloat16)
        queries = jnp.dot(normed, w_query, preferred_element_type=jnp.float32).astype(jnp.bfloat16)
        suffix_kv = jnp.dot(normed, w_keyval, preferred_element_type=jnp.float32).astype(jnp.bfloat16)
        end_points = jnp.cumsum(group_lengths).astype(jnp.int32)
        requests = request_of(positions, end_points)
        owner_prefix = lax.dynamic_index_in_dim(prefix_cache, owner_id, 0, keepdims=False)
        every_kv = jnp.concatenate([owner_prefix, suffix_kv], axis=0).astype(jnp.float32)
        key_heads = every_kv[:, :attn_width].reshape(-1, HEADS, HEAD)
        value_heads = every_kv[:, attn_width:].reshape(-1, HEADS, HEAD)

        def attend_block(block_number):
            first_row = block_number * query_block
            query_heads = lax.dynamic_slice_in_dim(queries, first_row, query_block, 0).astype(jnp.float32).reshape(query_block, HEADS, HEAD)
            query_pos = first_row + jnp.arange(query_block, dtype=jnp.int32)
            query_req = lax.dynamic_slice_in_dim(requests, first_row, query_block, 0)
            scores = jnp.einsum('qhd,khd->hqk', query_heads, key_heads) * HEAD ** (-0.5)
            own_rows = (query_req[:, None] == requests[None, :]) & (positions[None, :] <= query_pos[:, None])
            allowed = jnp.concatenate([jnp.ones((query_block, PREFIX), dtype=bool), own_rows], axis=1)
            scores = jnp.where(allowed[None], scores, neg_big)
            row_max = lax.optimization_barrier(jnp.max(scores, axis=-1, keepdims=True))
            probs_full = jnp.exp(scores - row_max)
            row_total = lax.optimization_barrier(jnp.sum(probs_full, axis=-1))
            probs_low = lax.optimization_barrier(probs_full.astype(jnp.bfloat16))
            weighted = jnp.einsum('hqk,khd->hqd', probs_low.astype(jnp.float32), value_heads)
            context = weighted / row_total[..., None]
            return jnp.transpose(context, (1, 0, 2)).reshape(query_block, attn_width).astype(jnp.bfloat16)
        context = lax.map(attend_block, jnp.arange(TOK_GRP // query_block, dtype=jnp.int32)).reshape(TOK_GRP, attn_width)
        mixed_stream = stream.astype(jnp.float32) + jnp.dot(context, w_out, preferred_element_type=jnp.float32)
        return (mixed_stream, suffix_kv)
    mixed_stream, suffix_cache = lax.map(one_group, (tokens, lengths, owners))
    routed_in = rms_scale(mixed_stream, moe_gain).astype(jnp.bfloat16)
    block_count = N_GRP * N_BLK
    block_rows = routed_in.reshape(block_count, TOK_DEV, D)
    block_routes = routes.reshape(block_count, TOK_DEV, 2)
    block_gates = gates.reshape(block_count, TOK_DEV, 2)
    targets = jax.vmap(slot_targets)(block_routes)
    dispatch = jax.vmap(dispatch_matrix)(targets)
    packed = jnp.einsum('bst,btd->bsd', dispatch.astype(jnp.float32), block_rows.astype(jnp.float32)).astype(jnp.bfloat16)
    packed = packed.reshape(block_count, EXPERTS, CAP, D)
    part_width = FF // SPLIT
    gate_all = w_gate.reshape(EXPERTS, SPLIT, D, part_width)
    up_all = w_up.reshape(EXPERTS, SPLIT, D, part_width)
    down_all = w_down.reshape(EXPERTS, SPLIT, part_width, D)
    slot_index = (targets % CAP).astype(jnp.int32)

    def one_expert(moe_sum, expert):
        expert_rows = lax.dynamic_index_in_dim(packed, expert, 1, keepdims=False).reshape(block_count * CAP, D)
        gate_weight = jnp.transpose(lax.dynamic_index_in_dim(gate_all, expert, 0, keepdims=False), (1, 0, 2)).reshape(D, FF)
        up_weight = jnp.transpose(lax.dynamic_index_in_dim(up_all, expert, 0, keepdims=False), (1, 0, 2)).reshape(D, FF)
        down_weight = lax.dynamic_index_in_dim(down_all, expert, 0, keepdims=False)
        gate_value = jnp.dot(expert_rows, gate_weight, preferred_element_type=jnp.float32)
        up_value = jnp.dot(expert_rows, up_weight, preferred_element_type=jnp.float32)
        expert_hidden = (jax.nn.gelu(gate_value, approximate=True) * up_value).astype(jnp.bfloat16)
        expert_out = jnp.zeros((block_count * CAP, D), jnp.float32)
        for part_number in range(SPLIT):
            partial_value = jnp.dot(expert_hidden[:, part_number * part_width:(part_number + 1) * part_width], down_weight[part_number], preferred_element_type=jnp.float32)
            partial_value = lax.optimization_barrier(partial_value.astype(jnp.bfloat16))
            expert_out = expert_out + partial_value.astype(jnp.float32)
        expert_out = expert_out.reshape(block_count, CAP, D)
        for pick_number in range(2):
            picked = jnp.take_along_axis(expert_out, slot_index[:, :, pick_number:pick_number + 1], axis=1)
            chosen = (block_routes[:, :, pick_number] == expert)[..., None]
            moe_sum = moe_sum + jnp.where(chosen, block_gates[:, :, pick_number:pick_number + 1] * picked, 0.0)
        return (moe_sum, expert)
    moe_total = lax.scan(one_expert, jnp.zeros((block_count, TOK_DEV, D), jnp.float32), jnp.arange(EXPERTS, dtype=jnp.int32))[0]
    hidden = (mixed_stream + moe_total.reshape(N_GRP, TOK_GRP, D)).astype(jnp.bfloat16)
    request_ends = jnp.cumsum(lengths, axis=1).astype(jnp.int32)
    requests = jax.vmap(request_of, in_axes=(None, 0))(positions, request_ends)
    squares = lax.optimization_barrier(jnp.sum(jnp.square(hidden.astype(jnp.float32)), axis=2))
    member = requests[:, :, None] == jnp.arange(REQS, dtype=jnp.int32)[None, None, :]
    norm_sums = lax.optimization_barrier(jnp.sum(jnp.where(member, squares[:, :, None], 0.0), axis=1))
    request_norm = jnp.sqrt(norm_sums / (lengths.astype(jnp.float32) * D))
    last_rows = jnp.take_along_axis(hidden, (request_ends - 1)[:, :, None], axis=1)
    final_rows = rms_scale(last_rows, final_gain).astype(jnp.bfloat16).reshape(N_GRP * REQS, D)
    logits = jnp.dot(final_rows, unembed, preferred_element_type=jnp.float32)
    greatest = lax.optimization_barrier(jnp.max(logits, axis=1)).reshape(N_GRP, REQS)
    return (hidden, suffix_cache, request_norm, greatest)
```

```python
import jax
import jax.numpy as jnp
from jax import lax
from jax.experimental import pallas as pl
from jax.experimental.pallas import tpu as pltpu
from jax.sharding import PartitionSpec as P

HEADS = 8
EXPERTS = 8
QUARTERS = 4
CAP = 40
SLOT_ROWS = 48
REQS = 16
ROWS = 128
HALF = 64
LANES = 128
KEY_TILE = 1024
QUERY_TILE = 256

epsilon = 1e-06
neg_big = -1e30
bf16 = jnp.bfloat16
f32 = jnp.float32


def rms_scale(values, gain_vector):
    return (
        values * lax.rsqrt(jnp.mean(values * values, axis=-1, keepdims=True) + epsilon) * gain_vector
    )


def lane_of(shape):
    return lax.broadcasted_iota(jnp.int32, shape, len(shape) - 1)


def head_split(first, second):
    low = lane_of(first.shape) < HALF
    axis = len(first.shape) - 1
    even = jnp.where(low, first, pltpu.roll(second, HALF, axis))
    odd = jnp.where(low, pltpu.roll(first, HALF, axis), second)
    return even, odd


def project_kernel(tok_ref, gain_ref, wq_ref, wk_ref, wv_ref, kv_ref, send_ref, normed_ref):
    pair = pl.program_id(0)

    @pl.when(pair == 0)
    def _():
        normed_ref[...] = rms_scale(tok_ref[...].astype(f32), gain_ref[...]).astype(bf16)

    normed = normed_ref[...]
    query = jnp.dot(normed, wq_ref[...], preferred_element_type=f32).astype(bf16)
    key = jnp.dot(normed, wk_ref[...], preferred_element_type=f32).astype(bf16)
    value = jnp.dot(normed, wv_ref[...], preferred_element_type=f32).astype(bf16)
    column = pl.multiple_of(pair * LANES, LANES)
    kv_ref[:, pl.ds(column, LANES)] = key
    kv_ref[:, pl.ds(HEADS * HALF + column, LANES)] = value
    even, odd = head_split(key.astype(f32), value.astype(f32))
    even = even.astype(bf16)
    odd = odd.astype(bf16)
    scaled = query.astype(f32) * (HALF**-0.5)
    for quarter in range(QUARTERS):
        first = scaled[quarter * 32 : quarter * 32 + 16]
        second = scaled[quarter * 32 + 16 : quarter * 32 + 32]
        query_even, query_odd = head_split(first, second)
        send_ref[0, quarter, 0:ROWS, :] = even
        send_ref[1, quarter, 0:ROWS, :] = odd
        send_ref[0, quarter, ROWS : ROWS + 16, :] = query_even.astype(bf16)
        send_ref[1, quarter, ROWS : ROWS + 16, :] = query_odd.astype(bf16)


def project(stream, gain, w_query, w_keyval):
    width = stream.shape[1]
    return pl.pallas_call(
        project_kernel,
        grid=(HEADS // 2,),
        in_specs=[
            pl.BlockSpec((ROWS, width), lambda i: (0, 0)),
            pl.BlockSpec((1, width), lambda i: (0, 0)),
            pl.BlockSpec((width, LANES), lambda i: (0, i)),
            pl.BlockSpec((width, LANES), lambda i: (0, i)),
            pl.BlockSpec((width, LANES), lambda i: (0, i + HEADS // 2)),
        ],
        out_specs=[
            pl.BlockSpec((ROWS, 2 * HEADS * HALF), lambda i: (0, 0)),
            pl.BlockSpec((2, QUARTERS, ROWS + 16, LANES), lambda i: (i, 0, 0, 0)),
        ],
        out_shape=[
            jax.ShapeDtypeStruct((ROWS, 2 * HEADS * HALF), bf16),
            jax.ShapeDtypeStruct((HEADS, QUARTERS, ROWS + 16, LANES), bf16),
        ],
        scratch_shapes=[pltpu.VMEM((ROWS, width), bf16)],
        name="project",
    )(stream, gain, w_query, w_keyval, w_keyval)


def prefix_pack_kernel(owner_ref, in_ref, out_ref):
    for pair in range(HEADS // 2):
        key = in_ref[0, :, pair * LANES : (pair + 1) * LANES].astype(f32)
        base = HEADS * HALF + pair * LANES
        value = in_ref[0, :, base : base + LANES].astype(f32)
        even, odd = head_split(key, value)
        for quarter in range(QUARTERS):
            out_ref[2 * pair, quarter] = even.astype(bf16)
            out_ref[2 * pair + 1, quarter] = odd.astype(bf16)


def prefix_pack(arrived, owners):
    _, rows, width = arrived.shape
    return pl.pallas_call(
        prefix_pack_kernel,
        grid_spec=pltpu.PrefetchScalarGridSpec(
            num_scalar_prefetch=1,
            grid=(1,),
            in_specs=[pl.BlockSpec((1, rows, width), lambda i, owner: (owner[0], 0, 0))],
            out_specs=pl.BlockSpec((HEADS, QUARTERS, rows, LANES), lambda i, owner: (0, 0, 0, 0)),
        ),
        out_shape=jax.ShapeDtypeStruct((HEADS, QUARTERS, rows, LANES), bf16),
        name="prefix_pack",
    )(owners, arrived)


def query_tile(got_ref, tile):
    blocks = QUERY_TILE // 32
    packed = got_ref[pl.ds(tile * blocks, blocks), ROWS : ROWS + 16, :]
    packed = packed.reshape(QUERY_TILE // 2, LANES).astype(f32)
    low = lane_of(packed.shape) < HALF
    first = jnp.where(low, packed, 0.0)
    second = jnp.where(low, pltpu.roll(packed, HALF, 1), 0.0)
    return jnp.concatenate([first, second], axis=0).astype(bf16)


def start_of(position, lengths_ref, zero):
    end = jnp.int32(0)
    start = zero
    for request in range(REQS):
        end = end + lengths_ref[request]
        start = jnp.where(position >= end, end, start)
    return start


def suffix_kernel(quarter_ref, lengths_ref, got_ref, out_ref):
    tile = pl.program_id(0)
    blocks = QUERY_TILE // 32
    key_blocks = KEY_TILE // ROWS
    query = query_tile(got_ref, tile)
    row = lax.broadcasted_iota(jnp.int32, (QUERY_TILE, 1), 0)
    half_rows = QUERY_TILE // 2
    second = (row >= half_rows).astype(jnp.int32)
    within = row - second * half_rows
    first_position = tile * blocks * ROWS + quarter_ref[0] * 32
    position = first_position + (within // 16) * ROWS + second * 16 + within % 16
    start = start_of(position, lengths_ref, jnp.zeros_like(position))
    lowest = start_of(first_position, lengths_ref, jnp.int32(0))
    span = blocks * ROWS
    last_tile = (tile * span + span - 1) // KEY_TILE

    def step(j, carry):
        acc, top, total = carry
        keys = got_ref[pl.ds(j * key_blocks, key_blocks), 0:ROWS, :].reshape(KEY_TILE, LANES)
        scores = lax.dot_general(
            query, keys, (((1,), (1,)), ((), ())), preferred_element_type=f32
        )
        key_position = j * KEY_TILE + lane_of(scores.shape)
        allowed = (key_position >= start) & (key_position <= position)
        scores = jnp.where(allowed, scores, neg_big)
        new_top = jnp.maximum(top, jnp.max(scores, axis=1, keepdims=True))
        shrink = jnp.exp(top - new_top)
        probs = jnp.exp(scores - new_top)
        total = total * shrink + jnp.sum(probs, axis=1, keepdims=True)
        acc = acc * shrink + jnp.dot(probs.astype(bf16), keys, preferred_element_type=f32)
        return acc, new_top, total

    acc, top, total = lax.fori_loop(
        lowest // KEY_TILE,
        last_tile + 1,
        step,
        (
            jnp.zeros((QUERY_TILE, LANES), f32),
            jnp.full((QUERY_TILE, 1), neg_big, f32),
            jnp.zeros((QUERY_TILE, 1), f32),
        ),
    )
    lane = lane_of(acc.shape)
    out_ref[...] = jnp.where(lane == 0, top, jnp.where(lane == 1, total, acc))


def suffix_attention(quarter, lengths, got):
    blocks = got.shape[0]
    queries = blocks * 32
    return pl.pallas_call(
        suffix_kernel,
        grid_spec=pltpu.PrefetchScalarGridSpec(
            num_scalar_prefetch=2,
            grid=(queries // QUERY_TILE,),
            in_specs=[pl.BlockSpec(got.shape, lambda i, q, l: (0, 0, 0))],
            out_specs=pl.BlockSpec((QUERY_TILE, LANES), lambda i, q, l: (i, 0)),
        ),
        out_shape=jax.ShapeDtypeStruct((queries, LANES), f32),
        compiler_params=pltpu.CompilerParams(vmem_limit_bytes=32 << 20),
        name="suffix_attention",
    )(quarter, lengths, got)


def prefix_kernel(got_ref, keys_ref, part_ref, out_ref):
    tile = pl.program_id(0)
    query = query_tile(got_ref, tile)
    keys = keys_ref[...].reshape(-1, LANES)
    scores = lax.dot_general(query, keys, (((1,), (1,)), ((), ())), preferred_element_type=f32)
    part = part_ref[...]
    part_top = part[:, 0:1]
    part_total = part[:, 1:2]
    top = jnp.maximum(part_top, jnp.max(scores, axis=1, keepdims=True))
    probs = jnp.exp(scores - top)
    shrink = jnp.exp(part_top - top)
    total = part_total * shrink + jnp.sum(probs, axis=1, keepdims=True)
    acc = part * shrink + jnp.dot(probs.astype(bf16), keys, preferred_element_type=f32)
    context = acc / total
    half_rows = QUERY_TILE // 2
    low = lane_of((half_rows, LANES)) < HALF
    packed = jnp.where(low, pltpu.roll(context[:half_rows], HALF, 1), context[half_rows:])
    out_ref[...] = packed.astype(bf16).reshape(out_ref.shape)


def prefix_attention(got, keys, part):
    blocks = got.shape[0]
    queries = blocks * 32
    tile_blocks = QUERY_TILE // 32
    return pl.pallas_call(
        prefix_kernel,
        grid=(queries // QUERY_TILE,),
        in_specs=[
            pl.BlockSpec(got.shape, lambda i: (0, 0, 0)),
            pl.BlockSpec(keys.shape, lambda i: (0, 0, 0)),
            pl.BlockSpec((QUERY_TILE, LANES), lambda i: (i, 0)),
        ],
        out_specs=pl.BlockSpec((tile_blocks, 16, LANES), lambda i: (i, 0, 0)),
        out_shape=jax.ShapeDtypeStruct((blocks, 16, LANES), bf16),
        compiler_params=pltpu.CompilerParams(vmem_limit_bytes=32 << 20),
        name="prefix_attention",
    )(got, keys, part)


def mix_kernel(ctx_ref, tok_ref, wout_ref, gain_ref, routes_ref, mixed_ref, send_ref):
    tiles = []
    for pair in range(HEADS // 2):
        even = ctx_ref[2 * pair].astype(f32)
        odd = ctx_ref[2 * pair + 1].astype(f32)
        first, second = head_split(even, odd)
        both = jnp.stack([first, second], axis=1)
        tiles.append(both.reshape(ROWS, LANES).astype(bf16))
    context = jnp.concatenate(tiles, axis=1)
    mixed = tok_ref[...].astype(f32) + jnp.dot(
        context, wout_ref[...], preferred_element_type=f32
    )
    mixed_ref[...] = mixed
    routed = rms_scale(mixed, gain_ref[...]).astype(bf16)
    expert = lax.broadcasted_iota(jnp.int32, (EXPERTS, ROWS), 0)
    named = (routes_ref[0:1, :] == expert) | (routes_ref[1:2, :] == expert)
    named_f = named.astype(f32)
    earlier = (
        lax.broadcasted_iota(jnp.int32, (ROWS, ROWS), 0)
        < lax.broadcasted_iota(jnp.int32, (ROWS, ROWS), 1)
    ).astype(bf16)
    slots = jnp.dot(named_f.astype(bf16), earlier, preferred_element_type=f32)
    slots = jnp.where(named, slots, -1.0).astype(jnp.int32)
    slot_id = lax.broadcasted_iota(jnp.int32, (SLOT_ROWS, ROWS), 0)
    for e in range(EXPERTS):
        pick = (slots[e : e + 1, :] == slot_id).astype(f32).astype(bf16)
        rows = jnp.dot(pick, routed, preferred_element_type=f32).astype(bf16)
        send_ref[e, 0] = rows
        send_ref[e, 1] = rows


def mix(ctx, stream, w_out, gain, routes_t):
    width = stream.shape[1]
    return pl.pallas_call(
        mix_kernel,
        out_shape=[
            jax.ShapeDtypeStruct((ROWS, width), f32),
            jax.ShapeDtypeStruct((EXPERTS, 2, SLOT_ROWS, width), bf16),
        ],
        compiler_params=pltpu.CompilerParams(vmem_limit_bytes=32 << 20),
        name="mix",
    )(ctx, stream, w_out, gain, routes_t)


def gelu(v):
    return 0.5 * v * (1.0 + jnp.tanh(0.7978845608028654 * (v + 0.044715 * v * v * v)))


FFN_TILE = 256


def expert_kernel(x_ref, g0, u0, d0, g1, u1, d1, out_ref, gate_v, up_v, down_v, acc_v, sems):
    sources = ((g0, u0, d0), (g1, u1, d1))
    places = (gate_v, up_v, down_v)
    copies = [
        [
            pltpu.make_async_copy(sources[part][kind], places[kind].at[part], sems.at[part, kind])
            for kind in range(3)
        ]
        for part in range(2)
    ]
    for part in range(2):
        for kind in range(3):
            copies[part][kind].start()
    for part in range(2):
        for tile in range(x_ref.shape[0] // FFN_TILE):
            rows = slice(tile * FFN_TILE, (tile + 1) * FFN_TILE)
            if tile == 0:
                copies[part][0].wait()
                copies[part][1].wait()
            x = x_ref[rows, :]
            gate = jnp.dot(x, gate_v[part], preferred_element_type=f32)
            up = jnp.dot(x, up_v[part], preferred_element_type=f32)
            hidden = (gelu(gate) * up).astype(bf16)
            if tile == 0:
                copies[part][2].wait()
            down = jnp.dot(hidden, down_v[part], preferred_element_type=f32)
            if part == 0:
                acc_v[rows, :] = down
            else:
                out_ref[rows, :] = (acc_v[rows, :] + down).astype(bf16)


def expert(rows, own, other):
    count, width = rows.shape
    units = own[0].shape[1]
    hbm = pl.BlockSpec(memory_space=pl.ANY)
    vmem = pl.BlockSpec(memory_space=pltpu.VMEM)
    return pl.pallas_call(
        expert_kernel,
        in_specs=[vmem] + [hbm] * 6,
        out_specs=vmem,
        out_shape=jax.ShapeDtypeStruct((count, width), bf16),
        scratch_shapes=[
            pltpu.VMEM((2, width, units), bf16),
            pltpu.VMEM((2, width, units), bf16),
            pltpu.VMEM((2, units, width), bf16),
            pltpu.VMEM((count, width), f32),
            pltpu.SemaphoreType.DMA((2, 3)),
        ],
        compiler_params=pltpu.CompilerParams(vmem_limit_bytes=48 << 20),
        name="expert",
    )(rows, *own, *other)


def combine_kernel(
    block_ref, lengths_ref, mixed_ref, got_ref, routes_ref, gates_ref, gain_ref, hidden_ref, last_ref, norm_ref
):
    routes = routes_ref[...]
    first = routes[:, 0:1]
    second = routes[:, 1:2]
    lane = lane_of((ROWS, LANES))
    named = ((first == lane) | (second == lane)).astype(f32).astype(bf16)
    earlier = (
        lax.broadcasted_iota(jnp.int32, (ROWS, ROWS), 1)
        < lax.broadcasted_iota(jnp.int32, (ROWS, ROWS), 0)
    ).astype(bf16)
    slots = jnp.dot(earlier, named, preferred_element_type=f32)
    got = got_ref[...]
    column = lane_of((ROWS, got.shape[0]))
    gates = gates_ref[...]
    hidden = mixed_ref[...]
    moe = None
    for which, chosen in enumerate((first, second)):
        slot = jnp.sum(jnp.where(chosen == lane, slots, 0.0), axis=1, keepdims=True)
        target = chosen * (2 * SLOT_ROWS) + slot.astype(jnp.int32)
        pick = ((column == target) | (column == target + SLOT_ROWS)).astype(f32).astype(bf16)
        picked = jnp.dot(pick, got, preferred_element_type=f32)
        term = gates[:, which : which + 1] * picked
        moe = term if moe is None else moe + term
    hidden = (hidden + moe).astype(bf16)
    hidden_ref[...] = hidden
    wide = hidden.astype(f32)
    squares = jnp.sum(wide * wide, axis=1, keepdims=True)
    position = block_ref[0] * ROWS + lax.broadcasted_iota(jnp.int32, (ROWS, LANES), 0)
    starts = jnp.zeros((1, LANES), jnp.int32)
    ends = jnp.zeros((1, LANES), jnp.int32)
    lasts = jnp.full((REQS, LANES), -1, jnp.int32)
    request = lax.broadcasted_iota(jnp.int32, (REQS, LANES), 0)
    lane_row = lane_of((1, LANES))
    end = jnp.int32(0)
    for r in range(REQS):
        starts = jnp.where(lane_row == r, end, starts)
        end = end + lengths_ref[r]
        ends = jnp.where(lane_row == r, end, ends)
        lasts = jnp.where(request == r, end - 1, lasts)
    member = (position >= starts) & (position < ends)
    norm_ref[...] = jnp.sum(jnp.where(member, squares, 0.0), axis=0, keepdims=True)
    final = rms_scale(wide, gain_ref[...]).astype(bf16)
    is_last = (lasts == block_ref[0] * ROWS + lane_of((REQS, LANES))).astype(f32).astype(bf16)
    last_ref[...] = jnp.dot(is_last, final, preferred_element_type=f32).astype(bf16)


def combine(block, lengths, mixed, got, routes, gates, gain):
    width = mixed.shape[1]
    vmem = pl.BlockSpec(memory_space=pltpu.VMEM)
    smem = pl.BlockSpec(memory_space=pltpu.SMEM)
    return pl.pallas_call(
        combine_kernel,
        in_specs=[smem, smem] + [vmem] * 5,
        out_specs=[vmem] * 3,
        out_shape=[
            jax.ShapeDtypeStruct((ROWS, width), bf16),
            jax.ShapeDtypeStruct((REQS, width), bf16),
            jax.ShapeDtypeStruct((1, LANES), f32),
        ],
        compiler_params=pltpu.CompilerParams(vmem_limit_bytes=32 << 20),
        name="combine",
    )(block, lengths, mixed, got, routes, gates, gain)


def exchange(rows):
    return lax.all_to_all(rows, "blk", split_axis=0, concat_axis=0, tiled=True)


def local(
    tokens,
    lengths,
    owners,
    prefix_cache,
    routes,
    gates,
    attn_gain,
    w_query,
    w_keyval,
    w_out,
    moe_gain,
    w_gate,
    w_up,
    w_down,
    final_gain,
    unembed,
):
    blocks = lax.axis_size("blk")
    block_index = lax.axis_index("blk")
    width = tokens.shape[2]
    stream = tokens[0]
    block = block_index.astype(jnp.int32).reshape(1)
    quarter = block % QUARTERS
    swap = [(i, i ^ 1) for i in range(blocks)]
    with jax.named_scope("prefix_gather"):
        arrived = lax.all_gather(prefix_cache, "grp", axis=0, tiled=True)
    with jax.named_scope("weight_swap"):
        own = (w_gate[0], w_up[0], w_down[0])
        other = tuple(lax.ppermute(one, "blk", swap) for one in own)
    suffix_kv, send = project(stream, attn_gain.reshape(1, -1), w_query, w_keyval)
    with jax.named_scope("qkv_exchange"):
        got = exchange(send.reshape(blocks, ROWS + 16, LANES))
    part = suffix_attention(quarter, lengths[0], got)
    packed = prefix_pack(arrived, owners)
    with jax.named_scope("prefix_exchange"):
        prefix_keys = exchange(packed.reshape(blocks, packed.shape[2], LANES))
    context = prefix_attention(got, prefix_keys, part)
    with jax.named_scope("context_exchange"):
        ctx = exchange(context).reshape(HEADS, QUARTERS, 16, LANES)
    mixed, outgoing = mix(ctx, stream, w_out, moe_gain.reshape(1, -1), routes[0].T)
    with jax.named_scope("dispatch_exchange"):
        rows = exchange(outgoing.reshape(blocks, SLOT_ROWS // 2, width))
    results = expert(rows.reshape(-1, width), own, other)
    with jax.named_scope("return_exchange"):
        returned = exchange(results.reshape(blocks, SLOT_ROWS // 2, width)).reshape(-1, width)
    hidden, last_terms, norm_terms = combine(
        block, lengths[0], mixed, returned, routes[0], gates[0], final_gain.reshape(1, -1)
    )
    with jax.named_scope("last_exchange"):
        spread = jnp.broadcast_to(last_terms[None], (blocks,) + last_terms.shape)
        last_rows = jnp.sum(exchange(spread).astype(f32), axis=0).astype(bf16)
    logits = jnp.dot(last_rows, unembed, preferred_element_type=f32)
    best = jnp.max(logits, axis=1)
    with jax.named_scope("final_exchange"):
        final = jnp.concatenate([norm_terms[:, :REQS], best[None, :]], axis=1)
        final = jnp.pad(final, ((0, 0), (0, LANES - 2 * REQS)))
        final = exchange(jnp.broadcast_to(final[None], (blocks, 1, LANES)))[:, 0, :]
    norm_sums = jnp.sum(final[:, :REQS], axis=0)
    greatest = jnp.max(final[:, REQS : 2 * REQS], axis=0)
    request_norm = jnp.sqrt(norm_sums / (lengths[0].astype(f32) * width))
    return (hidden[None], suffix_kv[None], request_norm[None], greatest[None])


def solution(mesh):
    placed = (
        P("grp", "blk", None),
        P("grp", None),
        P("grp"),
        P("grp", "blk", None),
        P("grp", "blk", None),
        P("grp", "blk", None),
        P(),
        P(),
        P(),
        P(),
        P(),
        P("blk", None, None),
        P("blk", None, None),
        P("blk", None, None),
        P(),
        P(None, "blk"),
    )
    return jax.shard_map(
        local,
        mesh=mesh,
        in_specs=placed,
        out_specs=(P("grp", "blk", None), P("grp", "blk", None), P("grp", None), P("grp", None)),
        check_vma=False,
    )
```

```python
import jax
import jax.numpy as jnp
from jax import lax
from jax.experimental import pallas as pl
from jax.experimental.pallas import tpu as pltpu
from jax.sharding import PartitionSpec as P

HEADS = 8
EXPERTS = 8
QUARTERS = 4
CAP = 40
SLOT_ROWS = 48
PART_ROWS = 24
PART_SLOTS = 20
SEND_ROWS = 176
REQS = 16
ROWS = 128
HALF = 64
LANES = 128
KEY_TILE = 1024
QUERY_TILE = 256

epsilon = 1e-06
neg_big = -1e30
bf16 = jnp.bfloat16
f32 = jnp.float32


def rms_scale(values, gain_vector):
    return (
        values * lax.rsqrt(jnp.mean(values * values, axis=-1, keepdims=True) + epsilon) * gain_vector
    )


def lane_of(shape):
    return lax.broadcasted_iota(jnp.int32, shape, len(shape) - 1)


def head_split(first, second):
    low = lane_of(first.shape) < HALF
    axis = len(first.shape) - 1
    even = jnp.where(low, first, pltpu.roll(second, HALF, axis))
    odd = jnp.where(low, pltpu.roll(first, HALF, axis), second)
    return even, odd


def last_matrix(lengths_ref, positions):
    request = lax.broadcasted_iota(jnp.int32, positions.shape, 0)
    lasts = jnp.full(positions.shape, -1, jnp.int32)
    end = jnp.int32(0)
    for r in range(REQS):
        end = end + lengths_ref[r]
        lasts = jnp.where(request == r, end - 1, lasts)
    return (lasts == positions).astype(f32).astype(bf16)


def three_parts(values):
    high = values.astype(bf16).astype(f32)
    middle = (values - high).astype(bf16).astype(f32)
    low = (values - high - middle).astype(bf16).astype(f32)
    return high, middle, low


def project_kernel(
    block_ref, lengths_ref, tok_ref, gain_ref, wq_ref, wk_ref, wv_ref, routes_ref, gates_ref,
    kv_ref, send_ref, normed_ref, gate_ref,
):
    pair = pl.program_id(0)
    is_last = last_matrix(lengths_ref, block_ref[0] * ROWS + lane_of((REQS, ROWS)))

    @pl.when(pair == 0)
    def _():
        normed_ref[...] = rms_scale(tok_ref[...].astype(f32), gain_ref[...]).astype(bf16)
        row = lax.broadcasted_iota(jnp.int32, (LANES, ROWS), 0)
        named = row % EXPERTS
        weight = jnp.where(
            routes_ref[0:1, :] == named,
            gates_ref[0:1, :],
            jnp.where(routes_ref[1:2, :] == named, gates_ref[1:2, :], 0.0),
        )
        high, middle, low = three_parts(weight)
        piece = row // EXPERTS
        pieces = jnp.where(
            piece == 0, high, jnp.where(piece == 1, middle, jnp.where(piece == 2, low, 0.0))
        )
        gate_ref[...] = lax.dot_general(
            is_last, pieces.astype(bf16), (((1,), (1,)), ((), ())), preferred_element_type=f32
        ).astype(bf16)

    normed = normed_ref[...]
    query = jnp.dot(normed, wq_ref[...], preferred_element_type=f32).astype(bf16)
    key = jnp.dot(normed, wk_ref[...], preferred_element_type=f32).astype(bf16)
    value = jnp.dot(normed, wv_ref[...], preferred_element_type=f32).astype(bf16)
    column = pl.multiple_of(pair * LANES, LANES)
    kv_ref[:, pl.ds(column, LANES)] = key
    kv_ref[:, pl.ds(HEADS * HALF + column, LANES)] = value
    even, odd = head_split(key.astype(f32), value.astype(f32))
    even = even.astype(bf16)
    odd = odd.astype(bf16)
    wide = pl.multiple_of(pair * 2 * LANES, 2 * LANES)
    ends = jnp.dot(
        is_last, tok_ref[:, pl.ds(wide, 2 * LANES)], preferred_element_type=f32
    ).astype(bf16)
    scaled = query.astype(f32) * (HALF**-0.5)
    for quarter in range(QUARTERS):
        first = scaled[quarter * 32 : quarter * 32 + 16]
        second = scaled[quarter * 32 + 16 : quarter * 32 + 32]
        query_even, query_odd = head_split(first, second)
        send_ref[0, quarter, 0:ROWS, :] = even
        send_ref[1, quarter, 0:ROWS, :] = odd
        send_ref[0, quarter, ROWS : ROWS + 16, :] = query_even.astype(bf16)
        send_ref[1, quarter, ROWS : ROWS + 16, :] = query_odd.astype(bf16)
        for which in range(2):
            send_ref[which, quarter, ROWS + 16 : ROWS + 32, :] = ends[
                :, which * LANES : (which + 1) * LANES
            ]
            send_ref[which, quarter, ROWS + 32 : ROWS + 48, :] = gate_ref[...]


def project(block, lengths, stream, gain, w_query, w_keyval, routes_t, gates_t):
    width = stream.shape[1]
    return pl.pallas_call(
        project_kernel,
        grid_spec=pltpu.PrefetchScalarGridSpec(
            num_scalar_prefetch=2,
            grid=(HEADS // 2,),
            in_specs=[
                pl.BlockSpec((ROWS, width), lambda i, b, l: (0, 0)),
                pl.BlockSpec((1, width), lambda i, b, l: (0, 0)),
                pl.BlockSpec((width, LANES), lambda i, b, l: (0, i)),
                pl.BlockSpec((width, LANES), lambda i, b, l: (0, i)),
                pl.BlockSpec((width, LANES), lambda i, b, l: (0, i + HEADS // 2)),
                pl.BlockSpec((2, ROWS), lambda i, b, l: (0, 0)),
                pl.BlockSpec((2, ROWS), lambda i, b, l: (0, 0)),
            ],
            out_specs=[
                pl.BlockSpec((ROWS, 2 * HEADS * HALF), lambda i, b, l: (0, 0)),
                pl.BlockSpec((2, QUARTERS, SEND_ROWS, LANES), lambda i, b, l: (i, 0, 0, 0)),
            ],
            scratch_shapes=[pltpu.VMEM((ROWS, width), bf16), pltpu.VMEM((REQS, LANES), bf16)],
        ),
        out_shape=[
            jax.ShapeDtypeStruct((ROWS, 2 * HEADS * HALF), bf16),
            jax.ShapeDtypeStruct((HEADS, QUARTERS, SEND_ROWS, LANES), bf16),
        ],
        name="project",
    )(block, lengths, stream, gain, w_query, w_keyval, w_keyval, routes_t, gates_t)


def prefix_pack_kernel(owner_ref, in_ref, ends_ref, out_ref):
    rows = in_ref.shape[1]
    for pair in range(HEADS // 2):
        key = in_ref[0, :, pair * LANES : (pair + 1) * LANES].astype(f32)
        base = HEADS * HALF + pair * LANES
        value = in_ref[0, :, base : base + LANES].astype(f32)
        even, odd = head_split(key, value)
        for quarter in range(QUARTERS):
            out_ref[2 * pair, quarter, 0:rows, :] = even.astype(bf16)
            out_ref[2 * pair + 1, quarter, 0:rows, :] = odd.astype(bf16)
    ends = jnp.sum(ends_ref[...].astype(f32), axis=0).astype(bf16)
    for head in range(HEADS):
        for quarter in range(QUARTERS):
            out_ref[head, quarter, rows : rows + REQS, :] = ends


def prefix_pack(arrived, owners, got):
    _, rows, width = arrived.shape
    return pl.pallas_call(
        prefix_pack_kernel,
        grid_spec=pltpu.PrefetchScalarGridSpec(
            num_scalar_prefetch=1,
            grid=(1,),
            in_specs=[
                pl.BlockSpec((1, rows, width), lambda i, owner: (owner[0], 0, 0)),
                pl.BlockSpec((got.shape[0], REQS, LANES), lambda i, owner: (0, 9, 0)),
            ],
            out_specs=pl.BlockSpec(
                (HEADS, QUARTERS, rows + REQS, LANES), lambda i, owner: (0, 0, 0, 0)
            ),
        ),
        out_shape=jax.ShapeDtypeStruct((HEADS, QUARTERS, rows + REQS, LANES), bf16),
        name="prefix_pack",
    )(owners, arrived, got)


def query_tile(got_ref, tile):
    blocks = QUERY_TILE // 32
    packed = got_ref[pl.ds(tile * blocks, blocks), ROWS : ROWS + 16, :]
    packed = packed.reshape(QUERY_TILE // 2, LANES).astype(f32)
    low = lane_of(packed.shape) < HALF
    first = jnp.where(low, packed, 0.0)
    second = jnp.where(low, pltpu.roll(packed, HALF, 1), 0.0)
    return jnp.concatenate([first, second], axis=0).astype(bf16)


def offset_of(row):
    half_rows = QUERY_TILE // 2
    second = (row >= half_rows).astype(jnp.int32)
    within = row - second * half_rows
    return (within // 16) * ROWS + second * 16 + within % 16


def start_of(position, lengths_ref, zero):
    end = jnp.int32(0)
    start = zero
    for request in range(REQS):
        end = end + lengths_ref[request]
        start = jnp.where(position >= end, end, start)
    return start


def suffix_kernel(quarter_ref, lengths_ref, got_ref, out_ref):
    tile = pl.program_id(0)
    blocks = QUERY_TILE // 32
    key_blocks = KEY_TILE // ROWS
    query = query_tile(got_ref, tile)
    first_position = tile * blocks * ROWS + quarter_ref[0] * 32
    position = first_position + offset_of(lax.broadcasted_iota(jnp.int32, (QUERY_TILE, 1), 0))
    start = start_of(position, lengths_ref, jnp.zeros_like(position))
    lowest = start_of(first_position, lengths_ref, jnp.int32(0))
    span = blocks * ROWS
    last_tile = (tile * span + span - 1) // KEY_TILE

    def step(j, carry):
        acc, top, total = carry
        keys = got_ref[pl.ds(j * key_blocks, key_blocks), 0:ROWS, :].reshape(KEY_TILE, LANES)
        scores = lax.dot_general(
            query, keys, (((1,), (1,)), ((), ())), preferred_element_type=f32
        )
        key_position = j * KEY_TILE + lane_of(scores.shape)
        allowed = (key_position >= start) & (key_position <= position)
        scores = jnp.where(allowed, scores, neg_big)
        new_top = jnp.maximum(top, jnp.max(scores, axis=1, keepdims=True))
        shrink = jnp.exp(top - new_top)
        probs = jnp.exp(scores - new_top)
        total = total * shrink + jnp.sum(probs, axis=1, keepdims=True)
        acc = acc * shrink + jnp.dot(probs.astype(bf16), keys, preferred_element_type=f32)
        return acc, new_top, total

    acc, top, total = lax.fori_loop(
        lowest // KEY_TILE,
        last_tile + 1,
        step,
        (
            jnp.zeros((QUERY_TILE, LANES), f32),
            jnp.full((QUERY_TILE, 1), neg_big, f32),
            jnp.zeros((QUERY_TILE, 1), f32),
        ),
    )
    lane = lane_of(acc.shape)
    out_ref[...] = jnp.where(lane == 0, top, jnp.where(lane == 1, total, acc))


def suffix_attention(quarter, lengths, got):
    blocks = got.shape[0]
    queries = blocks * 32
    return pl.pallas_call(
        suffix_kernel,
        grid_spec=pltpu.PrefetchScalarGridSpec(
            num_scalar_prefetch=2,
            grid=(queries // QUERY_TILE,),
            in_specs=[pl.BlockSpec(got.shape, lambda i, q, l: (0, 0, 0))],
            out_specs=pl.BlockSpec((QUERY_TILE, LANES), lambda i, q, l: (i, 0)),
        ),
        out_shape=jax.ShapeDtypeStruct((queries, LANES), f32),
        compiler_params=pltpu.CompilerParams(vmem_limit_bytes=24 << 20),
        name="suffix_attention",
    )(quarter, lengths, got)


def prefix_kernel(quarter_ref, lengths_ref, got_ref, keys_ref, part_ref, out_ref, last_ref):
    tile = pl.program_id(0)
    query = query_tile(got_ref, tile)
    keys = keys_ref[...].reshape(-1, LANES)
    scores = lax.dot_general(query, keys, (((1,), (1,)), ((), ())), preferred_element_type=f32)
    part = part_ref[...]
    part_top = part[:, 0:1]
    part_total = part[:, 1:2]
    top = jnp.maximum(part_top, jnp.max(scores, axis=1, keepdims=True))
    probs = jnp.exp(scores - top)
    shrink = jnp.exp(part_top - top)
    total = part_total * shrink + jnp.sum(probs, axis=1, keepdims=True)
    acc = part * shrink + jnp.dot(probs.astype(bf16), keys, preferred_element_type=f32)
    context = acc / total
    half_rows = QUERY_TILE // 2
    tile_blocks = QUERY_TILE // 32
    low = lane_of((half_rows, LANES)) < HALF
    packed = jnp.where(low, pltpu.roll(context[:half_rows], HALF, 1), context[half_rows:])
    out_ref[pl.ds(tile * tile_blocks, tile_blocks), 0:16, :] = packed.astype(bf16).reshape(
        tile_blocks, 16, LANES
    )
    positions = tile * tile_blocks * ROWS + quarter_ref[0] * 32
    positions = positions + offset_of(lane_of((REQS, QUERY_TILE)))
    is_last = last_matrix(lengths_ref, positions)
    ends = jnp.where(lane_of(context.shape) < HALF, 0.0, context).astype(bf16)
    ends = jnp.dot(is_last, ends, preferred_element_type=f32)

    @pl.when(tile == 0)
    def _():
        last_ref[...] = ends

    @pl.when(tile > 0)
    def _():
        last_ref[...] = last_ref[...] + ends

    @pl.when(tile == pl.num_programs(0) - 1)
    def _():
        every = last_ref[...].astype(bf16)
        for block in range(out_ref.shape[0]):
            out_ref[block, 16:32, :] = every


def prefix_attention(quarter, lengths, got, keys, part):
    blocks = got.shape[0]
    queries = blocks * 32
    rows = keys.shape[1] - REQS
    return pl.pallas_call(
        prefix_kernel,
        grid_spec=pltpu.PrefetchScalarGridSpec(
            num_scalar_prefetch=2,
            grid=(queries // QUERY_TILE,),
            in_specs=[
                pl.BlockSpec(got.shape, lambda i, q, l: (0, 0, 0)),
                pl.BlockSpec((blocks, rows, LANES), lambda i, q, l: (0, 0, 0)),
                pl.BlockSpec((QUERY_TILE, LANES), lambda i, q, l: (i, 0)),
            ],
            out_specs=pl.BlockSpec((blocks, 32, LANES), lambda i, q, l: (0, 0, 0)),
            scratch_shapes=[pltpu.VMEM((REQS, LANES), f32)],
        ),
        out_shape=jax.ShapeDtypeStruct((blocks, 32, LANES), bf16),
        compiler_params=pltpu.CompilerParams(vmem_limit_bytes=24 << 20),
        name="prefix_attention",
    )(quarter, lengths, got, keys, part)


def gelu(v):
    return 0.5 * v * (1.0 + jnp.tanh(0.7978845608028654 * (v + 0.044715 * v * v * v)))


def dot_nt(a, b):
    return lax.dot_general(a, b, (((1,), (1,)), ((), ())), preferred_element_type=f32)


def mix_kernel(
    block_ref, ctx_ref, tok_ref, tok_last_ref, gate_last_ref, wout_ref, gain_ref, routes_ref, g_ref, u_ref, d_ref,
    mixed_ref, mixed_last_ref, send_ref, g_v, u_v, d_v, send_v, sems, out_sems,
):
    copies = [
        pltpu.make_async_copy(source, place, sems.at[kind])
        for kind, (source, place) in enumerate(((g_ref, g_v), (u_ref, u_v), (d_ref, d_v)))
    ]
    for copy in copies:
        copy.start()
    tiles = []
    for pair in range(HEADS // 2):
        even = ctx_ref[2 * pair].astype(f32)
        odd = ctx_ref[2 * pair + 1].astype(f32)
        first, second = head_split(even[:, 0:16], odd[:, 0:16])
        both = jnp.stack([first, second], axis=1).reshape(ROWS, LANES)
        even_last = jnp.sum(even[:, 16:32], axis=0)
        odd_last = jnp.sum(odd[:, 16:32], axis=0)
        low = lane_of(even_last.shape) < HALF
        ends = jnp.where(low, pltpu.roll(even_last, HALF, 1), odd_last)
        tiles.append(jnp.concatenate([both, ends], axis=0).astype(bf16))
    context = jnp.concatenate(tiles, axis=1)
    lift = jnp.dot(context, wout_ref[...], preferred_element_type=f32)
    mixed = tok_ref[...].astype(f32) + lift[:ROWS]
    mixed_ref[...] = mixed
    routed = rms_scale(mixed, gain_ref[...]).astype(bf16)
    tok_last = jnp.concatenate([tok_last_ref[QUARTERS * j] for j in range(8)], axis=1)
    mixed_last = tok_last.astype(f32) + lift[ROWS:]
    mixed_last_ref[...] = mixed_last
    routed_last = rms_scale(mixed_last, gain_ref[...]).astype(bf16)
    expert_id = block_ref[0] // QUARTERS
    weights = jnp.sum(gate_last_ref[...].astype(f32), axis=0)
    lane = lane_of(weights.shape)
    mine = (lane % EXPERTS == expert_id) & (lane < 3 * EXPERTS)
    weight = jnp.sum(jnp.where(mine, weights, 0.0), axis=1, keepdims=True)
    copies[0].wait()
    copies[1].wait()
    act = (gelu(dot_nt(routed_last, g_v[...])) * dot_nt(routed_last, u_v[...])).astype(bf16)
    copies[2].wait()
    partial_last = weight * jnp.dot(act, d_v[...], preferred_element_type=f32)
    high = partial_last.astype(bf16)
    low_part = (partial_last - high.astype(f32)).astype(bf16)
    source = jnp.concatenate([routed, high, low_part], axis=0)
    columns = ROWS + 2 * REQS
    expert = lax.broadcasted_iota(jnp.int32, (EXPERTS, ROWS), 0)
    named = (routes_ref[0:1, :] == expert) | (routes_ref[1:2, :] == expert)
    earlier = (
        lax.broadcasted_iota(jnp.int32, (ROWS, ROWS), 0)
        < lax.broadcasted_iota(jnp.int32, (ROWS, ROWS), 1)
    ).astype(bf16)
    slots = jnp.dot(named.astype(f32).astype(bf16), earlier, preferred_element_type=f32)
    slots = jnp.where(named, slots, -1.0).astype(jnp.int32)
    place = slots + jnp.where(slots >= PART_SLOTS, PART_ROWS - PART_SLOTS, 0)
    place_id = lax.broadcasted_iota(jnp.int32, (SLOT_ROWS, ROWS), 0)
    extra_row = lax.broadcasted_iota(jnp.int32, (SLOT_ROWS, 2 * REQS), 0) % PART_ROWS
    extra_column = lane_of((SLOT_ROWS, 2 * REQS))
    sends = []
    for e in range(EXPERTS):
        pick = (place[e : e + 1, :] == place_id).astype(f32)
        for chip in range(2):
            row_last = 2 * e + chip
            extra = ((extra_row == PART_SLOTS) & (extra_column == row_last)) | (
                (extra_row == PART_SLOTS + 1) & (extra_column == REQS + row_last)
            )
            both = jnp.concatenate([pick, extra.astype(f32)], axis=1).astype(bf16)
            send_v[e, chip] = jnp.dot(both, source, preferred_element_type=f32).astype(bf16)
        send = pltpu.make_async_copy(send_v.at[e], send_ref.at[e], out_sems.at[e])
        send.start()
        sends.append(send)
    for send in sends:
        send.wait()


def mix(block, ctx, stream, prefix_got, got, w_out, gain, routes_t, own):
    width = stream.shape[1]
    blocks = got.shape[0]
    units = own[0].shape[0]
    hbm = pl.BlockSpec(memory_space=pl.ANY)

    def whole(shape):
        return pl.BlockSpec(shape, lambda i, b: (0,) * len(shape))

    return pl.pallas_call(
        mix_kernel,
        grid_spec=pltpu.PrefetchScalarGridSpec(
            num_scalar_prefetch=1,
            grid=(1,),
            in_specs=[
                whole(ctx.shape),
                whole(stream.shape),
                pl.BlockSpec((blocks, REQS, LANES), lambda i, b: (0, 4, 0)),
                pl.BlockSpec((blocks, REQS, LANES), lambda i, b: (0, 10, 0)),
                whole(w_out.shape),
                whole(gain.shape),
                whole(routes_t.shape),
                hbm,
                hbm,
                hbm,
            ],
            out_specs=[
                whole((ROWS, width)),
                whole((REQS, width)),
                pl.BlockSpec(memory_space=pltpu.HBM),
            ],
            scratch_shapes=[
                pltpu.VMEM((units, width), bf16),
                pltpu.VMEM((units, width), bf16),
                pltpu.VMEM((units, width), bf16),
                pltpu.VMEM((EXPERTS, 2, SLOT_ROWS, width), bf16),
                pltpu.SemaphoreType.DMA((3,)),
                pltpu.SemaphoreType.DMA((EXPERTS,)),
            ],
        ),
        out_shape=[
            jax.ShapeDtypeStruct((ROWS, width), f32),
            jax.ShapeDtypeStruct((REQS, width), f32),
            jax.ShapeDtypeStruct((EXPERTS, 2, SLOT_ROWS, width), bf16),
        ],
        compiler_params=pltpu.CompilerParams(vmem_limit_bytes=28 << 20),
        name="mix",
    )(block, ctx, stream, prefix_got, got, w_out, gain, routes_t, *own)


FFN_TILE = 256


def expert_kernel(
    x_ref, g0, u0, d0, g1, u1, d1, out_ref, gate_v, up_v, down_v, acc_v, out_v, sems, out_sems
):
    sources = ((g0, u0, d0), (g1, u1, d1))
    places = (gate_v, up_v, down_v)
    copies = [
        [
            pltpu.make_async_copy(sources[part][kind], places[kind].at[part], sems.at[part, kind])
            for kind in range(3)
        ]
        for part in range(2)
    ]
    for part in range(2):
        for kind in range(3):
            copies[part][kind].start()
    count = x_ref.shape[0]
    within = lane_of((16, count)) % PART_ROWS
    extra = ((within == PART_SLOTS) | (within == PART_SLOTS + 1)).astype(f32).astype(bf16)
    total = jnp.dot(extra, x_ref[...], preferred_element_type=f32)[0:1]
    high = total.astype(bf16).astype(f32)
    low = (total - high).astype(bf16).astype(f32)
    sends = []
    for part in range(2):
        for tile in range(count // FFN_TILE):
            rows = slice(tile * FFN_TILE, (tile + 1) * FFN_TILE)
            if tile == 0:
                copies[part][0].wait()
                copies[part][1].wait()
            x = x_ref[rows, :]
            hidden = (gelu(dot_nt(x, gate_v[part])) * dot_nt(x, up_v[part])).astype(bf16)
            if tile == 0:
                copies[part][2].wait()
            down = jnp.dot(hidden, down_v[part], preferred_element_type=f32)
            if part == 0:
                acc_v[rows, :] = down
            else:
                row = tile * FFN_TILE + lax.broadcasted_iota(jnp.int32, (FFN_TILE, 1), 0)
                row = row % PART_ROWS
                result = acc_v[rows, :] + down
                result = jnp.where(row == PART_SLOTS, high, result)
                result = jnp.where(row == PART_SLOTS + 1, low, result)
                out_v[rows, :] = result.astype(bf16)
                send = pltpu.make_async_copy(
                    out_v.at[pl.ds(tile * FFN_TILE, FFN_TILE), :],
                    out_ref.at[pl.ds(tile * FFN_TILE, FFN_TILE), :],
                    out_sems.at[tile],
                )
                send.start()
                sends.append(send)
    for send in sends:
        send.wait()


def expert(rows, own, other):
    count, width = rows.shape
    units = own[0].shape[0]
    hbm = pl.BlockSpec(memory_space=pl.ANY)
    vmem = pl.BlockSpec(memory_space=pltpu.VMEM)
    return pl.pallas_call(
        expert_kernel,
        in_specs=[vmem] + [hbm] * 6,
        out_specs=pl.BlockSpec(memory_space=pltpu.HBM),
        out_shape=jax.ShapeDtypeStruct((count, width), bf16),
        scratch_shapes=[
            pltpu.VMEM((2, units, width), bf16),
            pltpu.VMEM((2, units, width), bf16),
            pltpu.VMEM((2, units, width), bf16),
            pltpu.VMEM((count, width), f32),
            pltpu.VMEM((count, width), bf16),
            pltpu.SemaphoreType.DMA((2, 3)),
            pltpu.SemaphoreType.DMA((count // FFN_TILE,)),
        ],
        compiler_params=pltpu.CompilerParams(vmem_limit_bytes=48 << 20),
        name="expert",
    )(rows, *own, *other)


def combine_kernel(
    block_ref, lengths_ref, mixed_ref, mixed_last_ref, got_ref, routes_ref, gates_ref, gain_ref,
    hidden_ref, last_ref, norm_ref,
):
    got = got_ref[...]
    count = got.shape[0]
    request_row = lax.broadcasted_iota(jnp.int32, (REQS, count), 0)
    wanted = request_row * (2 * PART_ROWS) + PART_SLOTS
    source = lane_of((REQS, count))
    pick_last = ((source == wanted) | (source == wanted + 1)).astype(f32).astype(bf16)
    moe_last = jnp.dot(pick_last, got, preferred_element_type=f32)
    hidden_last = (mixed_last_ref[...] + moe_last).astype(bf16).astype(f32)
    last_ref[...] = rms_scale(hidden_last, gain_ref[...]).astype(bf16)
    routes = routes_ref[...]
    first = routes[:, 0:1]
    second = routes[:, 1:2]
    lane = lane_of((ROWS, LANES))
    named = ((first == lane) | (second == lane)).astype(f32).astype(bf16)
    earlier = (
        lax.broadcasted_iota(jnp.int32, (ROWS, ROWS), 1)
        < lax.broadcasted_iota(jnp.int32, (ROWS, ROWS), 0)
    ).astype(bf16)
    slots = jnp.dot(earlier, named, preferred_element_type=f32)
    column = lane_of((ROWS, count))
    gates = gates_ref[...]
    moe = None
    for which, chosen in enumerate((first, second)):
        slot = jnp.sum(jnp.where(chosen == lane, slots, 0.0), axis=1, keepdims=True)
        slot = slot.astype(jnp.int32)
        place = slot + jnp.where(slot >= PART_SLOTS, PART_ROWS - PART_SLOTS, 0)
        target = chosen * (2 * SLOT_ROWS) + place
        pick = ((column == target) | (column == target + SLOT_ROWS)).astype(f32).astype(bf16)
        picked = jnp.dot(pick, got, preferred_element_type=f32)
        term = gates[:, which : which + 1] * picked
        moe = term if moe is None else moe + term
    hidden = (mixed_ref[...] + moe).astype(bf16)
    hidden_ref[...] = hidden
    wide = hidden.astype(f32)
    squares = jnp.sum(wide * wide, axis=1, keepdims=True)
    position = block_ref[0] * ROWS + lax.broadcasted_iota(jnp.int32, (ROWS, LANES), 0)
    starts = jnp.zeros((1, LANES), jnp.int32)
    ends = jnp.zeros((1, LANES), jnp.int32)
    lane_row = lane_of((1, LANES))
    end = jnp.int32(0)
    for r in range(REQS):
        starts = jnp.where(lane_row == r, end, starts)
        end = end + lengths_ref[r]
        ends = jnp.where(lane_row == r, end, ends)
    member = (position >= starts) & (position < ends)
    norm_ref[...] = jnp.sum(jnp.where(member, squares, 0.0), axis=0, keepdims=True)


def combine(block, lengths, mixed, mixed_last, got, routes, gates, gain):
    width = mixed.shape[1]
    vmem = pl.BlockSpec(memory_space=pltpu.VMEM)
    smem = pl.BlockSpec(memory_space=pltpu.SMEM)
    return pl.pallas_call(
        combine_kernel,
        in_specs=[smem, smem] + [vmem] * 6,
        out_specs=[vmem] * 3,
        out_shape=[
            jax.ShapeDtypeStruct((ROWS, width), bf16),
            jax.ShapeDtypeStruct((REQS, width), bf16),
            jax.ShapeDtypeStruct((1, LANES), f32),
        ],
        compiler_params=pltpu.CompilerParams(vmem_limit_bytes=24 << 20),
        name="combine",
    )(block, lengths, mixed, mixed_last, got, routes, gates, gain)


def exchange(rows):
    return lax.all_to_all(rows, "blk", split_axis=0, concat_axis=0, tiled=True)


def local(
    tokens,
    lengths,
    owners,
    prefix_cache,
    routes,
    gates,
    attn_gain,
    w_query,
    w_keyval,
    w_out,
    moe_gain,
    w_gate,
    w_up,
    w_down,
    final_gain,
    unembed,
):
    blocks = lax.axis_size("blk")
    block_index = lax.axis_index("blk")
    width = tokens.shape[2]
    stream = tokens[0]
    block = block_index.astype(jnp.int32).reshape(1)
    quarter = block % QUARTERS
    swap = [(i, i ^ 1) for i in range(blocks)]
    with jax.named_scope("prefix_gather"):
        arrived = lax.all_gather(prefix_cache, "grp", axis=0, tiled=True)
    with jax.named_scope("weight_swap"):
        own = (w_gate[0].T, w_up[0].T, w_down[0])
        other = tuple(lax.ppermute(one, "blk", swap) for one in own)
    routes_t = routes[0].T
    suffix_kv, send = project(
        block, lengths[0], stream, attn_gain.reshape(1, -1), w_query, w_keyval, routes_t, gates[0].T
    )
    with jax.named_scope("qkv_exchange"):
        got = exchange(send.reshape(blocks, SEND_ROWS, LANES))
    part = suffix_attention(quarter, lengths[0], got)
    packed = prefix_pack(arrived, owners, got)
    with jax.named_scope("prefix_exchange"):
        prefix_got = exchange(packed.reshape(blocks, packed.shape[2], LANES))
    context = prefix_attention(quarter, lengths[0], got, prefix_got, part)
    with jax.named_scope("context_exchange"):
        ctx = exchange(context).reshape(HEADS, QUARTERS, 32, LANES)
    mixed, mixed_last, outgoing = mix(
        block, ctx, stream, prefix_got, got, w_out, moe_gain.reshape(1, -1), routes_t, own
    )
    with jax.named_scope("dispatch_exchange"):
        rows = exchange(outgoing.reshape(blocks, PART_ROWS, width))
    results = expert(rows.reshape(-1, width), own, other)
    with jax.named_scope("return_exchange"):
        returned = exchange(results.reshape(blocks, PART_ROWS, width)).reshape(-1, width)
    hidden, last_rows, norm_terms = combine(
        block, lengths[0], mixed, mixed_last, returned, routes[0], gates[0], final_gain.reshape(1, -1)
    )
    logits = jnp.dot(last_rows, unembed, preferred_element_type=f32)
    best = jnp.max(logits, axis=1)
    with jax.named_scope("final_exchange"):
        final = jnp.concatenate([norm_terms[:, :REQS], best[None, :]], axis=1)
        final = jnp.pad(final, ((0, 0), (0, LANES - 2 * REQS)))
        final = exchange(jnp.broadcast_to(final[None], (blocks, 1, LANES)))[:, 0, :]
    norm_sums = jnp.sum(final[:, :REQS], axis=0)
    greatest = jnp.max(final[:, REQS : 2 * REQS], axis=0)
    request_norm = jnp.sqrt(norm_sums / (lengths[0].astype(f32) * width))
    return (hidden[None], suffix_kv[None], request_norm[None], greatest[None])


def solution(mesh):
    placed = (
        P("grp", "blk", None),
        P("grp", None),
        P("grp"),
        P("grp", "blk", None),
        P("grp", "blk", None),
        P("grp", "blk", None),
        P(),
        P(),
        P(),
        P(),
        P(),
        P("blk", None, None),
        P("blk", None, None),
        P("blk", None, None),
        P(),
        P(None, "blk"),
    )
    return jax.shard_map(
        local,
        mesh=mesh,
        in_specs=placed,
        out_specs=(P("grp", "blk", None), P("grp", "blk", None), P("grp", None), P("grp", None)),
        check_vma=False,
    )
```

```python
import jax
import jax.numpy as jnp
from jax import lax
from jax.experimental import pallas as pl
from jax.experimental.pallas import tpu as pltpu
from jax.sharding import PartitionSpec as P

HEADS = 8
EXPERTS = 8
QUARTERS = 4
CAP = 40
SLOT_ROWS = 48
PART_ROWS = 24
PART_SLOTS = 20
SEND_ROWS = 176
REQS = 16
ROWS = 128
HALF = 64
LANES = 128
KEY_TILE = 1024
QUERY_TILE = 256

epsilon = 1e-06
neg_big = -1e30
bf16 = jnp.bfloat16
f32 = jnp.float32


def rms_scale(values, gain_vector):
    return (
        values * lax.rsqrt(jnp.mean(values * values, axis=-1, keepdims=True) + epsilon) * gain_vector
    )


def lane_of(shape):
    return lax.broadcasted_iota(jnp.int32, shape, len(shape) - 1)


def head_split(first, second):
    low = lane_of(first.shape) < HALF
    axis = len(first.shape) - 1
    even = jnp.where(low, first, pltpu.roll(second, HALF, axis))
    odd = jnp.where(low, pltpu.roll(first, HALF, axis), second)
    return even, odd


def last_matrix(lengths_ref, positions):
    request = lax.broadcasted_iota(jnp.int32, positions.shape, 0)
    lasts = jnp.full(positions.shape, -1, jnp.int32)
    end = jnp.int32(0)
    for r in range(REQS):
        end = end + lengths_ref[r]
        lasts = jnp.where(request == r, end - 1, lasts)
    return (lasts == positions).astype(f32).astype(bf16)


def three_parts(values):
    high = values.astype(bf16).astype(f32)
    middle = (values - high).astype(bf16).astype(f32)
    low = (values - high - middle).astype(bf16).astype(f32)
    return high, middle, low


def in_hbm(*arrays):
    return tuple(pltpu.with_memory_space_constraint(one, pltpu.HBM) for one in arrays)


def project_kernel(
    block_ref, lengths_ref, tok_ref, gain_ref, wq_ref, wk_ref, wv_ref, routes_ref, gates_ref,
    kv_ref, send_ref, normed_ref, gate_ref,
):
    pair = pl.program_id(0)
    is_last = last_matrix(lengths_ref, block_ref[0] * ROWS + lane_of((REQS, ROWS)))

    @pl.when(pair == 0)
    def _():
        normed_ref[...] = rms_scale(tok_ref[...].astype(f32), gain_ref[...]).astype(bf16)
        row = lax.broadcasted_iota(jnp.int32, (LANES, ROWS), 0)
        named = row % EXPERTS
        weight = jnp.where(
            routes_ref[0:1, :] == named,
            gates_ref[0:1, :],
            jnp.where(routes_ref[1:2, :] == named, gates_ref[1:2, :], 0.0),
        )
        high, middle, low = three_parts(weight)
        piece = row // EXPERTS
        pieces = jnp.where(
            piece == 0, high, jnp.where(piece == 1, middle, jnp.where(piece == 2, low, 0.0))
        )
        gate_ref[...] = lax.dot_general(
            is_last, pieces.astype(bf16), (((1,), (1,)), ((), ())), preferred_element_type=f32
        ).astype(bf16)

    normed = normed_ref[...]
    query = jnp.dot(normed, wq_ref[...], preferred_element_type=f32).astype(bf16)
    key = jnp.dot(normed, wk_ref[...], preferred_element_type=f32).astype(bf16)
    value = jnp.dot(normed, wv_ref[...], preferred_element_type=f32).astype(bf16)
    column = pl.multiple_of(pair * LANES, LANES)
    kv_ref[:, pl.ds(column, LANES)] = key
    kv_ref[:, pl.ds(HEADS * HALF + column, LANES)] = value
    even, odd = head_split(key.astype(f32), value.astype(f32))
    even = even.astype(bf16)
    odd = odd.astype(bf16)
    wide = pl.multiple_of(pair * 2 * LANES, 2 * LANES)
    ends = jnp.dot(
        is_last, tok_ref[:, pl.ds(wide, 2 * LANES)], preferred_element_type=f32
    ).astype(bf16)
    scaled = query.astype(f32) * (HALF**-0.5)
    for quarter in range(QUARTERS):
        first = scaled[quarter * 32 : quarter * 32 + 16]
        second = scaled[quarter * 32 + 16 : quarter * 32 + 32]
        query_even, query_odd = head_split(first, second)
        send_ref[0, quarter, 0:ROWS, :] = even
        send_ref[1, quarter, 0:ROWS, :] = odd
        send_ref[0, quarter, ROWS : ROWS + 16, :] = query_even.astype(bf16)
        send_ref[1, quarter, ROWS : ROWS + 16, :] = query_odd.astype(bf16)
        for which in range(2):
            send_ref[which, quarter, ROWS + 16 : ROWS + 32, :] = ends[
                :, which * LANES : (which + 1) * LANES
            ]
            send_ref[which, quarter, ROWS + 32 : ROWS + 48, :] = gate_ref[...]


def project(block, lengths, stream, gain, w_query, w_keyval, routes_t, gates_t):
    width = stream.shape[1]
    return pl.pallas_call(
        project_kernel,
        grid_spec=pltpu.PrefetchScalarGridSpec(
            num_scalar_prefetch=2,
            grid=(HEADS // 2,),
            in_specs=[
                pl.BlockSpec((ROWS, width), lambda i, b, l: (0, 0)),
                pl.BlockSpec((1, width), lambda i, b, l: (0, 0)),
                pl.BlockSpec((width, LANES), lambda i, b, l: (0, i)),
                pl.BlockSpec((width, LANES), lambda i, b, l: (0, i)),
                pl.BlockSpec((width, LANES), lambda i, b, l: (0, i + HEADS // 2)),
                pl.BlockSpec((2, ROWS), lambda i, b, l: (0, 0)),
                pl.BlockSpec((2, ROWS), lambda i, b, l: (0, 0)),
            ],
            out_specs=[
                pl.BlockSpec((ROWS, 2 * HEADS * HALF), lambda i, b, l: (0, 0)),
                pl.BlockSpec((2, QUARTERS, SEND_ROWS, LANES), lambda i, b, l: (i, 0, 0, 0)),
            ],
            scratch_shapes=[pltpu.VMEM((ROWS, width), bf16), pltpu.VMEM((REQS, LANES), bf16)],
        ),
        out_shape=[
            jax.ShapeDtypeStruct((ROWS, 2 * HEADS * HALF), bf16),
            jax.ShapeDtypeStruct((HEADS, QUARTERS, SEND_ROWS, LANES), bf16),
        ],
        name="project",
    )(block, lengths, stream, gain, w_query, w_keyval, w_keyval, routes_t, gates_t)


def prefix_pack_kernel(owner_ref, in_ref, ends_ref, out_ref):
    rows = in_ref.shape[1]
    for pair in range(HEADS // 2):
        key = in_ref[0, :, pair * LANES : (pair + 1) * LANES].astype(f32)
        base = HEADS * HALF + pair * LANES
        value = in_ref[0, :, base : base + LANES].astype(f32)
        even, odd = head_split(key, value)
        for quarter in range(QUARTERS):
            out_ref[2 * pair, quarter, 0:rows, :] = even.astype(bf16)
            out_ref[2 * pair + 1, quarter, 0:rows, :] = odd.astype(bf16)
    ends = jnp.sum(ends_ref[...].astype(f32), axis=0).astype(bf16)
    for head in range(HEADS):
        for quarter in range(QUARTERS):
            out_ref[head, quarter, rows : rows + REQS, :] = ends


def prefix_pack(arrived, owners, got):
    _, rows, width = arrived.shape
    return pl.pallas_call(
        prefix_pack_kernel,
        grid_spec=pltpu.PrefetchScalarGridSpec(
            num_scalar_prefetch=1,
            grid=(1,),
            in_specs=[
                pl.BlockSpec((1, rows, width), lambda i, owner: (owner[0], 0, 0)),
                pl.BlockSpec((got.shape[0], REQS, LANES), lambda i, owner: (0, 9, 0)),
            ],
            out_specs=pl.BlockSpec(
                (HEADS, QUARTERS, rows + REQS, LANES), lambda i, owner: (0, 0, 0, 0)
            ),
        ),
        out_shape=jax.ShapeDtypeStruct((HEADS, QUARTERS, rows + REQS, LANES), bf16),
        name="prefix_pack",
    )(owners, *in_hbm(arrived, got))


def query_tile(query_ref):
    packed = query_ref[...].reshape(QUERY_TILE // 2, LANES).astype(f32)
    low = lane_of(packed.shape) < HALF
    first = jnp.where(low, packed, 0.0)
    second = jnp.where(low, pltpu.roll(packed, HALF, 1), 0.0)
    return jnp.concatenate([first, second], axis=0).astype(bf16)


def offset_of(row):
    half_rows = QUERY_TILE // 2
    second = (row >= half_rows).astype(jnp.int32)
    within = row - second * half_rows
    return (within // 16) * ROWS + second * 16 + within % 16


def start_of(position, lengths_ref, zero):
    end = jnp.int32(0)
    start = zero
    for request in range(REQS):
        end = end + lengths_ref[request]
        start = jnp.where(position >= end, end, start)
    return start


def suffix_kernel(quarter_ref, lengths_ref, query_ref, got_ref, out_ref):
    tile = pl.program_id(0)
    blocks = QUERY_TILE // 32
    key_blocks = KEY_TILE // ROWS
    query = query_tile(query_ref)
    first_position = tile * blocks * ROWS + quarter_ref[0] * 32
    position = first_position + offset_of(lax.broadcasted_iota(jnp.int32, (QUERY_TILE, 1), 0))
    start = start_of(position, lengths_ref, jnp.zeros_like(position))
    lowest = start_of(first_position, lengths_ref, jnp.int32(0))
    span = blocks * ROWS
    last_tile = (tile * span + span - 1) // KEY_TILE

    def step(j, carry):
        acc, top, total = carry
        keys = got_ref[pl.ds(j * key_blocks, key_blocks), :, :].reshape(KEY_TILE, LANES)
        scores = lax.dot_general(
            query, keys, (((1,), (1,)), ((), ())), preferred_element_type=f32
        )
        key_position = j * KEY_TILE + lane_of(scores.shape)
        allowed = (key_position >= start) & (key_position <= position)
        scores = jnp.where(allowed, scores, neg_big)
        new_top = jnp.maximum(top, jnp.max(scores, axis=1, keepdims=True))
        shrink = jnp.exp(top - new_top)
        probs = jnp.exp(scores - new_top)
        total = total * shrink + jnp.sum(probs, axis=1, keepdims=True)
        acc = acc * shrink + jnp.dot(probs.astype(bf16), keys, preferred_element_type=f32)
        return acc, new_top, total

    acc, top, total = lax.fori_loop(
        lowest // KEY_TILE,
        last_tile + 1,
        step,
        (
            jnp.zeros((QUERY_TILE, LANES), f32),
            jnp.full((QUERY_TILE, 1), neg_big, f32),
            jnp.zeros((QUERY_TILE, 1), f32),
        ),
    )
    lane = lane_of(acc.shape)
    out_ref[...] = jnp.where(lane == 0, top, jnp.where(lane == 1, total, acc))


def suffix_attention(quarter, lengths, got):
    blocks = got.shape[0]
    queries = blocks * 32
    return pl.pallas_call(
        suffix_kernel,
        grid_spec=pltpu.PrefetchScalarGridSpec(
            num_scalar_prefetch=2,
            grid=(queries // QUERY_TILE,),
            in_specs=[
                pl.BlockSpec((QUERY_TILE // 32, 16, LANES), lambda i, q, l: (i, ROWS // 16, 0)),
                pl.BlockSpec((blocks, ROWS, LANES), lambda i, q, l: (0, 0, 0)),
            ],
            out_specs=pl.BlockSpec((QUERY_TILE, LANES), lambda i, q, l: (i, 0)),
        ),
        out_shape=pltpu.HBM((queries, LANES), f32),
        compiler_params=pltpu.CompilerParams(vmem_limit_bytes=14 << 20),
        name="suffix_attention",
    )(quarter, lengths, *in_hbm(got, got))


def prefix_kernel(quarter_ref, lengths_ref, query_ref, keys_ref, part_ref, out_ref, last_ref):
    tile = pl.program_id(0)
    query = query_tile(query_ref)
    keys = keys_ref[...].reshape(-1, LANES)
    scores = lax.dot_general(query, keys, (((1,), (1,)), ((), ())), preferred_element_type=f32)
    part = part_ref[...]
    part_top = part[:, 0:1]
    part_total = part[:, 1:2]
    top = jnp.maximum(part_top, jnp.max(scores, axis=1, keepdims=True))
    probs = jnp.exp(scores - top)
    shrink = jnp.exp(part_top - top)
    total = part_total * shrink + jnp.sum(probs, axis=1, keepdims=True)
    acc = part * shrink + jnp.dot(probs.astype(bf16), keys, preferred_element_type=f32)
    context = acc / total
    half_rows = QUERY_TILE // 2
    tile_blocks = QUERY_TILE // 32
    low = lane_of((half_rows, LANES)) < HALF
    packed = jnp.where(low, pltpu.roll(context[:half_rows], HALF, 1), context[half_rows:])
    out_ref[pl.ds(tile * tile_blocks, tile_blocks), 0:16, :] = packed.astype(bf16).reshape(
        tile_blocks, 16, LANES
    )
    positions = tile * tile_blocks * ROWS + quarter_ref[0] * 32
    positions = positions + offset_of(lane_of((REQS, QUERY_TILE)))
    is_last = last_matrix(lengths_ref, positions)
    ends = jnp.where(lane_of(context.shape) < HALF, 0.0, context).astype(bf16)
    ends = jnp.dot(is_last, ends, preferred_element_type=f32)

    @pl.when(tile == 0)
    def _():
        last_ref[...] = ends

    @pl.when(tile > 0)
    def _():
        last_ref[...] = last_ref[...] + ends

    @pl.when(tile == pl.num_programs(0) - 1)
    def _():
        every = last_ref[...].astype(bf16)
        for block in range(out_ref.shape[0]):
            out_ref[block, 16:32, :] = every


def prefix_attention(quarter, lengths, got, keys, part):
    blocks = got.shape[0]
    queries = blocks * 32
    rows = keys.shape[1] - REQS
    return pl.pallas_call(
        prefix_kernel,
        grid_spec=pltpu.PrefetchScalarGridSpec(
            num_scalar_prefetch=2,
            grid=(queries // QUERY_TILE,),
            in_specs=[
                pl.BlockSpec((QUERY_TILE // 32, 16, LANES), lambda i, q, l: (i, ROWS // 16, 0)),
                pl.BlockSpec((blocks, rows, LANES), lambda i, q, l: (0, 0, 0)),
                pl.BlockSpec((QUERY_TILE, LANES), lambda i, q, l: (i, 0)),
            ],
            out_specs=pl.BlockSpec((blocks, 32, LANES), lambda i, q, l: (0, 0, 0)),
            scratch_shapes=[pltpu.VMEM((REQS, LANES), f32)],
        ),
        out_shape=jax.ShapeDtypeStruct((blocks, 32, LANES), bf16),
        compiler_params=pltpu.CompilerParams(vmem_limit_bytes=18 << 20),
        name="prefix_attention",
    )(quarter, lengths, *in_hbm(got, keys, part))


def gelu(v):
    return 0.5 * v * (1.0 + jnp.tanh(0.7978845608028654 * (v + 0.044715 * v * v * v)))


def dot_nt(a, b):
    return lax.dot_general(a, b, (((1,), (1,)), ((), ())), preferred_element_type=f32)


def mix_kernel(
    block_ref, ctx_ref, tok_ref, tok_last_ref, gate_last_ref, wout_ref, gain_ref, routes_ref, g_ref, u_ref, d_ref,
    mixed_ref, mixed_last_ref, send_ref, g_v, u_v, d_v, send_v, sems, out_sems,
):
    copies = [
        pltpu.make_async_copy(source, place, sems.at[kind])
        for kind, (source, place) in enumerate(((g_ref, g_v), (u_ref, u_v), (d_ref, d_v)))
    ]
    for copy in copies:
        copy.start()
    tiles = []
    for pair in range(HEADS // 2):
        even = ctx_ref[2 * pair].astype(f32)
        odd = ctx_ref[2 * pair + 1].astype(f32)
        first, second = head_split(even[:, 0:16], odd[:, 0:16])
        both = jnp.stack([first, second], axis=1).reshape(ROWS, LANES)
        even_last = jnp.sum(even[:, 16:32], axis=0)
        odd_last = jnp.sum(odd[:, 16:32], axis=0)
        low = lane_of(even_last.shape) < HALF
        ends = jnp.where(low, pltpu.roll(even_last, HALF, 1), odd_last)
        tiles.append(jnp.concatenate([both, ends], axis=0).astype(bf16))
    context = jnp.concatenate(tiles, axis=1)
    lift = jnp.dot(context, wout_ref[...], preferred_element_type=f32)
    mixed = tok_ref[...].astype(f32) + lift[:ROWS]
    mixed_ref[...] = mixed
    routed = rms_scale(mixed, gain_ref[...]).astype(bf16)
    tok_last = jnp.concatenate([tok_last_ref[QUARTERS * j] for j in range(8)], axis=1)
    mixed_last = tok_last.astype(f32) + lift[ROWS:]
    mixed_last_ref[...] = mixed_last
    routed_last = rms_scale(mixed_last, gain_ref[...]).astype(bf16)
    expert_id = block_ref[0] // QUARTERS
    weights = jnp.sum(gate_last_ref[...].astype(f32), axis=0)
    lane = lane_of(weights.shape)
    mine = (lane % EXPERTS == expert_id) & (lane < 3 * EXPERTS)
    weight = jnp.sum(jnp.where(mine, weights, 0.0), axis=1, keepdims=True)
    copies[0].wait()
    copies[1].wait()
    act = (gelu(dot_nt(routed_last, g_v[...])) * dot_nt(routed_last, u_v[...])).astype(bf16)
    copies[2].wait()
    partial_last = weight * jnp.dot(act, d_v[...], preferred_element_type=f32)
    high = partial_last.astype(bf16)
    low_part = (partial_last - high.astype(f32)).astype(bf16)
    source = jnp.concatenate([routed, high, low_part], axis=0)
    columns = ROWS + 2 * REQS
    expert = lax.broadcasted_iota(jnp.int32, (EXPERTS, ROWS), 0)
    named = (routes_ref[0:1, :] == expert) | (routes_ref[1:2, :] == expert)
    earlier = (
        lax.broadcasted_iota(jnp.int32, (ROWS, ROWS), 0)
        < lax.broadcasted_iota(jnp.int32, (ROWS, ROWS), 1)
    ).astype(bf16)
    slots = jnp.dot(named.astype(f32).astype(bf16), earlier, preferred_element_type=f32)
    slots = jnp.where(named, slots, -1.0).astype(jnp.int32)
    place = slots + jnp.where(slots >= PART_SLOTS, PART_ROWS - PART_SLOTS, 0)
    place_id = lax.broadcasted_iota(jnp.int32, (SLOT_ROWS, ROWS), 0)
    extra_row = lax.broadcasted_iota(jnp.int32, (SLOT_ROWS, 2 * REQS), 0) % PART_ROWS
    extra_column = lane_of((SLOT_ROWS, 2 * REQS))
    sends = []
    for e in range(EXPERTS):
        pick = (place[e : e + 1, :] == place_id).astype(f32)
        for chip in range(2):
            row_last = 2 * e + chip
            extra = ((extra_row == PART_SLOTS) & (extra_column == row_last)) | (
                (extra_row == PART_SLOTS + 1) & (extra_column == REQS + row_last)
            )
            both = jnp.concatenate([pick, extra.astype(f32)], axis=1).astype(bf16)
            send_v[e, chip] = jnp.dot(both, source, preferred_element_type=f32).astype(bf16)
        send = pltpu.make_async_copy(send_v.at[e], send_ref.at[e], out_sems.at[e])
        send.start()
        sends.append(send)
    for send in sends:
        send.wait()


def mix(block, ctx, stream, prefix_got, got, w_out, gain, routes_t, own):
    width = stream.shape[1]
    blocks = got.shape[0]
    units = own[0].shape[0]
    hbm = pl.BlockSpec(memory_space=pl.ANY)

    def whole(shape):
        return pl.BlockSpec(shape, lambda i, b: (0,) * len(shape))

    return pl.pallas_call(
        mix_kernel,
        grid_spec=pltpu.PrefetchScalarGridSpec(
            num_scalar_prefetch=1,
            grid=(1,),
            in_specs=[
                whole(ctx.shape),
                whole(stream.shape),
                pl.BlockSpec((blocks, REQS, LANES), lambda i, b: (0, 4, 0)),
                pl.BlockSpec((blocks, REQS, LANES), lambda i, b: (0, 10, 0)),
                whole(w_out.shape),
                whole(gain.shape),
                whole(routes_t.shape),
                hbm,
                hbm,
                hbm,
            ],
            out_specs=[
                whole((ROWS, width)),
                whole((REQS, width)),
                pl.BlockSpec(memory_space=pltpu.HBM),
            ],
            scratch_shapes=[
                pltpu.VMEM((units, width), bf16),
                pltpu.VMEM((units, width), bf16),
                pltpu.VMEM((units, width), bf16),
                pltpu.VMEM((EXPERTS, 2, SLOT_ROWS, width), bf16),
                pltpu.SemaphoreType.DMA((3,)),
                pltpu.SemaphoreType.DMA((EXPERTS,)),
            ],
        ),
        out_shape=[
            pltpu.HBM((ROWS, width), f32),
            pltpu.HBM((REQS, width), f32),
            pltpu.HBM((EXPERTS, 2, SLOT_ROWS, width), bf16),
        ],
        compiler_params=pltpu.CompilerParams(vmem_limit_bytes=18 << 20),
        name="mix",
    )(block, ctx, stream, *in_hbm(prefix_got, got), w_out, gain, routes_t, *in_hbm(*own))


FFN_TILE = 256


def expert_kernel(
    x_ref, g0, u0, d0, g1, u1, d1, out_ref, gate_v, up_v, down_v, acc_v, out_v, sems, out_sems
):
    sources = ((g0, u0, d0), (g1, u1, d1))
    places = (gate_v, up_v, down_v)
    copies = [
        [
            pltpu.make_async_copy(sources[part][kind], places[kind].at[part], sems.at[part, kind])
            for kind in range(3)
        ]
        for part in range(2)
    ]
    for part in range(2):
        for kind in range(3):
            copies[part][kind].start()
    count = x_ref.shape[0]
    within = lane_of((16, count)) % PART_ROWS
    extra = ((within == PART_SLOTS) | (within == PART_SLOTS + 1)).astype(f32).astype(bf16)
    total = jnp.dot(extra, x_ref[...], preferred_element_type=f32)[0:1]
    high = total.astype(bf16).astype(f32)
    low = (total - high).astype(bf16).astype(f32)
    sends = []
    for part in range(2):
        for tile in range(count // FFN_TILE):
            rows = slice(tile * FFN_TILE, (tile + 1) * FFN_TILE)
            if tile == 0:
                copies[part][0].wait()
                copies[part][1].wait()
            x = x_ref[rows, :]
            hidden = (gelu(dot_nt(x, gate_v[part])) * dot_nt(x, up_v[part])).astype(bf16)
            if tile == 0:
                copies[part][2].wait()
            down = jnp.dot(hidden, down_v[part], preferred_element_type=f32)
            if part == 0:
                acc_v[rows, :] = down
            else:
                row = tile * FFN_TILE + lax.broadcasted_iota(jnp.int32, (FFN_TILE, 1), 0)
                row = row % PART_ROWS
                result = acc_v[rows, :] + down
                result = jnp.where(row == PART_SLOTS, high, result)
                result = jnp.where(row == PART_SLOTS + 1, low, result)
                out_v[rows, :] = result.astype(bf16)
                send = pltpu.make_async_copy(
                    out_v.at[pl.ds(tile * FFN_TILE, FFN_TILE), :],
                    out_ref.at[pl.ds(tile * FFN_TILE, FFN_TILE), :],
                    out_sems.at[tile],
                )
                send.start()
                sends.append(send)
    for send in sends:
        send.wait()


def expert(rows, own, other):
    count, width = rows.shape
    units = own[0].shape[0]
    hbm = pl.BlockSpec(memory_space=pl.ANY)
    vmem = pl.BlockSpec(memory_space=pltpu.VMEM)
    return pl.pallas_call(
        expert_kernel,
        in_specs=[vmem] + [hbm] * 6,
        out_specs=pl.BlockSpec(memory_space=pltpu.HBM),
        out_shape=pltpu.HBM((count, width), bf16),
        scratch_shapes=[
            pltpu.VMEM((2, units, width), bf16),
            pltpu.VMEM((2, units, width), bf16),
            pltpu.VMEM((2, units, width), bf16),
            pltpu.VMEM((count, width), f32),
            pltpu.VMEM((count, width), bf16),
            pltpu.SemaphoreType.DMA((2, 3)),
            pltpu.SemaphoreType.DMA((count // FFN_TILE,)),
        ],
        compiler_params=pltpu.CompilerParams(vmem_limit_bytes=26 << 20),
        name="expert",
    )(rows, *in_hbm(*own, *other))


def column_of(row):
    return jnp.transpose(jnp.broadcast_to(row, (ROWS, LANES)))


def combine_kernel(
    block_ref, lengths_ref, mixed_ref, mixed_last_ref, got_ref, routes_ref, gates_ref, gain_ref,
    hidden_ref, last_ref, norm_ref,
):
    got = got_ref[...]
    count = got.shape[0]
    request_row = lax.broadcasted_iota(jnp.int32, (REQS, count), 0)
    wanted = request_row * (2 * PART_ROWS) + PART_SLOTS
    source = lane_of((REQS, count))
    pick_last = ((source == wanted) | (source == wanted + 1)).astype(f32).astype(bf16)
    moe_last = jnp.dot(pick_last, got, preferred_element_type=f32)
    hidden_last = (mixed_last_ref[...] + moe_last).astype(bf16).astype(f32)
    last_ref[...] = rms_scale(hidden_last, gain_ref[...]).astype(bf16)
    first = column_of(routes_ref[0:1, :].astype(f32)).astype(jnp.int32)
    second = column_of(routes_ref[1:2, :].astype(f32)).astype(jnp.int32)
    lane = lane_of((ROWS, LANES))
    named = ((first == lane) | (second == lane)).astype(f32).astype(bf16)
    earlier = (
        lax.broadcasted_iota(jnp.int32, (ROWS, ROWS), 1)
        < lax.broadcasted_iota(jnp.int32, (ROWS, ROWS), 0)
    ).astype(bf16)
    slots = jnp.dot(earlier, named, preferred_element_type=f32)
    column = lane_of((ROWS, count))
    moe = None
    for which, chosen in enumerate((first, second)):
        slot = jnp.sum(jnp.where(chosen == lane, slots, 0.0), axis=1, keepdims=True)
        slot = slot.astype(jnp.int32)
        place = slot + jnp.where(slot >= PART_SLOTS, PART_ROWS - PART_SLOTS, 0)
        target = chosen[:, 0:1] * (2 * SLOT_ROWS) + place
        pick = ((column == target) | (column == target + SLOT_ROWS)).astype(f32).astype(bf16)
        picked = jnp.dot(pick, got, preferred_element_type=f32)
        term = column_of(gates_ref[which : which + 1, :])[:, 0:1] * picked
        moe = term if moe is None else moe + term
    hidden = (mixed_ref[...] + moe).astype(bf16)
    hidden_ref[...] = hidden
    wide = hidden.astype(f32)
    squares = jnp.sum(wide * wide, axis=1, keepdims=True)
    position = block_ref[0] * ROWS + lax.broadcasted_iota(jnp.int32, (ROWS, LANES), 0)
    starts = jnp.zeros((1, LANES), jnp.int32)
    ends = jnp.zeros((1, LANES), jnp.int32)
    lane_row = lane_of((1, LANES))
    end = jnp.int32(0)
    for r in range(REQS):
        starts = jnp.where(lane_row == r, end, starts)
        end = end + lengths_ref[r]
        ends = jnp.where(lane_row == r, end, ends)
    member = (position >= starts) & (position < ends)
    norm_ref[...] = jnp.sum(jnp.where(member, squares, 0.0), axis=0, keepdims=True)


def combine(block, lengths, mixed, mixed_last, got, routes, gates, gain):
    width = mixed.shape[1]
    vmem = pl.BlockSpec(memory_space=pltpu.VMEM)
    smem = pl.BlockSpec(memory_space=pltpu.SMEM)
    return pl.pallas_call(
        combine_kernel,
        in_specs=[smem, smem] + [vmem] * 6,
        out_specs=[vmem] * 3,
        out_shape=[
            jax.ShapeDtypeStruct((ROWS, width), bf16),
            jax.ShapeDtypeStruct((REQS, width), bf16),
            jax.ShapeDtypeStruct((1, LANES), f32),
        ],
        compiler_params=pltpu.CompilerParams(vmem_limit_bytes=16 << 20),
        name="combine",
    )(block, lengths, mixed, mixed_last, got, routes, gates, gain)


def exchange(rows):
    return lax.all_to_all(rows, "blk", split_axis=0, concat_axis=0, tiled=True)


def local(
    tokens,
    lengths,
    owners,
    prefix_cache,
    routes,
    gates,
    attn_gain,
    w_query,
    w_keyval,
    w_out,
    moe_gain,
    w_gate,
    w_up,
    w_down,
    final_gain,
    unembed,
):
    blocks = lax.axis_size("blk")
    block_index = lax.axis_index("blk")
    width = tokens.shape[2]
    stream = tokens[0]
    block = block_index.astype(jnp.int32).reshape(1)
    quarter = block % QUARTERS
    swap = [(i, i ^ 1) for i in range(blocks)]
    with jax.named_scope("prefix_gather"):
        arrived = lax.all_gather(prefix_cache, "grp", axis=0, tiled=True)
    with jax.named_scope("weight_swap"):
        own = (w_gate[0].T, w_up[0].T, w_down[0])
        other = tuple(lax.ppermute(one, "blk", swap) for one in own)
    routes_t = routes[0].T
    gates_t = gates[0].T
    suffix_kv, send = project(
        block, lengths[0], stream, attn_gain.reshape(1, -1), w_query, w_keyval, routes_t, gates_t
    )
    with jax.named_scope("qkv_exchange"):
        got = exchange(send.reshape(blocks, SEND_ROWS, LANES))
    part = suffix_attention(quarter, lengths[0], got)
    packed = prefix_pack(arrived, owners, got)
    with jax.named_scope("prefix_exchange"):
        prefix_got = exchange(packed.reshape(blocks, packed.shape[2], LANES))
    context = prefix_attention(quarter, lengths[0], got, prefix_got, part)
    with jax.named_scope("context_exchange"):
        ctx = exchange(context).reshape(HEADS, QUARTERS, 32, LANES)
    mixed, mixed_last, outgoing = mix(
        block, ctx, stream, prefix_got, got, w_out, moe_gain.reshape(1, -1), routes_t, own
    )
    with jax.named_scope("dispatch_exchange"):
        rows = exchange(outgoing.reshape(blocks, PART_ROWS, width))
    results = expert(rows.reshape(-1, width), own, other)
    with jax.named_scope("return_exchange"):
        returned = exchange(results.reshape(blocks, PART_ROWS, width)).reshape(-1, width)
    hidden, last_rows, norm_terms = combine(
        block, lengths[0], mixed, mixed_last, returned, routes_t, gates_t, final_gain.reshape(1, -1)
    )
    logits = jnp.dot(last_rows, unembed, preferred_element_type=f32)
    best = jnp.max(logits, axis=1)
    with jax.named_scope("final_exchange"):
        final = jnp.concatenate([norm_terms[:, :REQS], best[None, :]], axis=1)
        final = jnp.pad(final, ((0, 0), (0, LANES - 2 * REQS)))
        final = exchange(jnp.broadcast_to(final[None], (blocks, 1, LANES)))[:, 0, :]
    norm_sums = jnp.sum(final[:, :REQS], axis=0)
    greatest = jnp.max(final[:, REQS : 2 * REQS], axis=0)
    request_norm = jnp.sqrt(norm_sums / (lengths[0].astype(f32) * width))
    return (hidden[None], suffix_kv[None], request_norm[None], greatest[None])


def solution(mesh):
    placed = (
        P("grp", "blk", None),
        P("grp", None),
        P("grp"),
        P("grp", "blk", None),
        P("grp", "blk", None),
        P("grp", "blk", None),
        P(),
        P(),
        P(),
        P(),
        P(),
        P("blk", None, None),
        P("blk", None, None),
        P("blk", None, None),
        P(),
        P(None, "blk"),
    )
    return jax.shard_map(
        local,
        mesh=mesh,
        in_specs=placed,
        out_specs=(P("grp", "blk", None), P("grp", "blk", None), P("grp", None), P("grp", None)),
        check_vma=False,
    )
```

```python
import jax
import jax.numpy as jnp
from jax import lax
from jax.experimental import pallas as pl
from jax.experimental.pallas import tpu as pltpu
from jax.sharding import PartitionSpec as P

HEADS = 8
EXPERTS = 8
QUARTERS = 4
CAP = 40
SLOT_ROWS = 48
PART_ROWS = 24
PART_SLOTS = 20
SEND_ROWS = 176
REQS = 16
ROWS = 128
HALF = 64
LANES = 128
KEY_TILE = 1024
QUERY_TILE = 256

epsilon = 1e-06
neg_big = -1e30
bf16 = jnp.bfloat16
f32 = jnp.float32


def rms_scale(values, gain_vector):
    return (
        values * lax.rsqrt(jnp.mean(values * values, axis=-1, keepdims=True) + epsilon) * gain_vector
    )


def lane_of(shape):
    return lax.broadcasted_iota(jnp.int32, shape, len(shape) - 1)


def head_split(first, second):
    low = lane_of(first.shape) < HALF
    axis = len(first.shape) - 1
    even = jnp.where(low, first, pltpu.roll(second, HALF, axis))
    odd = jnp.where(low, pltpu.roll(first, HALF, axis), second)
    return even, odd


def last_matrix(lengths_ref, positions):
    request = lax.broadcasted_iota(jnp.int32, positions.shape, 0)
    lasts = jnp.full(positions.shape, -1, jnp.int32)
    end = jnp.int32(0)
    for r in range(REQS):
        end = end + lengths_ref[r]
        lasts = jnp.where(request == r, end - 1, lasts)
    return (lasts == positions).astype(f32).astype(bf16)


def three_parts(values):
    high = values.astype(bf16).astype(f32)
    middle = (values - high).astype(bf16).astype(f32)
    low = (values - high - middle).astype(bf16).astype(f32)
    return high, middle, low


def in_hbm(*arrays):
    return tuple(pltpu.with_memory_space_constraint(one, pltpu.HBM) for one in arrays)


def project_kernel(
    block_ref, lengths_ref, tok_ref, gain_ref, wq_ref, wk_ref, wv_ref, routes_ref, gates_ref,
    kv_ref, send_ref, normed_ref, gate_ref,
):
    pair = pl.program_id(0)
    is_last = last_matrix(lengths_ref, block_ref[0] * ROWS + lane_of((REQS, ROWS)))

    @pl.when(pair == 0)
    def _():
        normed_ref[...] = rms_scale(tok_ref[...].astype(f32), gain_ref[...]).astype(bf16)
        row = lax.broadcasted_iota(jnp.int32, (LANES, ROWS), 0)
        named = row % EXPERTS
        weight = jnp.where(
            routes_ref[0:1, :] == named,
            gates_ref[0:1, :],
            jnp.where(routes_ref[1:2, :] == named, gates_ref[1:2, :], 0.0),
        )
        high, middle, low = three_parts(weight)
        piece = row // EXPERTS
        pieces = jnp.where(
            piece == 0, high, jnp.where(piece == 1, middle, jnp.where(piece == 2, low, 0.0))
        )
        gate_ref[...] = lax.dot_general(
            is_last, pieces.astype(bf16), (((1,), (1,)), ((), ())), preferred_element_type=f32
        ).astype(bf16)

    normed = normed_ref[...]
    query = jnp.dot(normed, wq_ref[...], preferred_element_type=f32).astype(bf16)
    key = jnp.dot(normed, wk_ref[...], preferred_element_type=f32).astype(bf16)
    value = jnp.dot(normed, wv_ref[...], preferred_element_type=f32).astype(bf16)
    column = pl.multiple_of(pair * LANES, LANES)
    kv_ref[:, pl.ds(column, LANES)] = key
    kv_ref[:, pl.ds(HEADS * HALF + column, LANES)] = value
    even, odd = head_split(key.astype(f32), value.astype(f32))
    even = even.astype(bf16)
    odd = odd.astype(bf16)
    wide = pl.multiple_of(pair * 2 * LANES, 2 * LANES)
    ends = jnp.dot(
        is_last, tok_ref[:, pl.ds(wide, 2 * LANES)], preferred_element_type=f32
    ).astype(bf16)
    scaled = query.astype(f32) * (HALF**-0.5)
    for quarter in range(QUARTERS):
        first = scaled[quarter * 32 : quarter * 32 + 16]
        second = scaled[quarter * 32 + 16 : quarter * 32 + 32]
        query_even, query_odd = head_split(first, second)
        send_ref[0, quarter, 0:ROWS, :] = even
        send_ref[1, quarter, 0:ROWS, :] = odd
        send_ref[0, quarter, ROWS : ROWS + 16, :] = query_even.astype(bf16)
        send_ref[1, quarter, ROWS : ROWS + 16, :] = query_odd.astype(bf16)
        for which in range(2):
            send_ref[which, quarter, ROWS + 16 : ROWS + 32, :] = ends[
                :, which * LANES : (which + 1) * LANES
            ]
            send_ref[which, quarter, ROWS + 32 : ROWS + 48, :] = gate_ref[...]


def project(block, lengths, stream, gain, w_query, w_keyval, routes_t, gates_t):
    width = stream.shape[1]
    return pl.pallas_call(
        project_kernel,
        grid_spec=pltpu.PrefetchScalarGridSpec(
            num_scalar_prefetch=2,
            grid=(HEADS // 2,),
            in_specs=[
                pl.BlockSpec((ROWS, width), lambda i, b, l: (0, 0)),
                pl.BlockSpec((1, width), lambda i, b, l: (0, 0)),
                pl.BlockSpec((width, LANES), lambda i, b, l: (0, i)),
                pl.BlockSpec((width, LANES), lambda i, b, l: (0, i)),
                pl.BlockSpec((width, LANES), lambda i, b, l: (0, i + HEADS // 2)),
                pl.BlockSpec((2, ROWS), lambda i, b, l: (0, 0)),
                pl.BlockSpec((2, ROWS), lambda i, b, l: (0, 0)),
            ],
            out_specs=[
                pl.BlockSpec((ROWS, 2 * HEADS * HALF), lambda i, b, l: (0, 0)),
                pl.BlockSpec((2, QUARTERS, SEND_ROWS, LANES), lambda i, b, l: (i, 0, 0, 0)),
            ],
            scratch_shapes=[pltpu.VMEM((ROWS, width), bf16), pltpu.VMEM((REQS, LANES), bf16)],
        ),
        out_shape=[
            jax.ShapeDtypeStruct((ROWS, 2 * HEADS * HALF), bf16),
            jax.ShapeDtypeStruct((HEADS, QUARTERS, SEND_ROWS, LANES), bf16),
        ],
        name="project",
    )(block, lengths, stream, gain, w_query, w_keyval, w_keyval, routes_t, gates_t)


def prefix_pack_kernel(offset_ref, ends_ref, *refs):
    pieces = refs[: len(refs) - 3]
    out_ref, prefix_v, sem = refs[len(refs) - 3 :]
    for k, piece in enumerate(pieces):

        @pl.when(offset_ref[0] == k)
        def _():
            copy = pltpu.make_async_copy(piece, prefix_v, sem)
            copy.start()
            copy.wait()

    rows = prefix_v.shape[0]
    for pair in range(HEADS // 2):
        key = prefix_v[:, pair * LANES : (pair + 1) * LANES].astype(f32)
        base = HEADS * HALF + pair * LANES
        value = prefix_v[:, base : base + LANES].astype(f32)
        even, odd = head_split(key, value)
        for quarter in range(QUARTERS):
            out_ref[2 * pair, quarter, 0:rows, :] = even.astype(bf16)
            out_ref[2 * pair + 1, quarter, 0:rows, :] = odd.astype(bf16)
    ends = jnp.sum(ends_ref[...].astype(f32), axis=0).astype(bf16)
    for head in range(HEADS):
        for quarter in range(QUARTERS):
            out_ref[head, quarter, rows : rows + REQS, :] = ends


def prefix_pack(pieces, offset, got):
    rows, width = pieces[0].shape
    return pl.pallas_call(
        prefix_pack_kernel,
        grid_spec=pltpu.PrefetchScalarGridSpec(
            num_scalar_prefetch=1,
            grid=(1,),
            in_specs=[
                pl.BlockSpec((got.shape[0], REQS, LANES), lambda i, owner: (0, 9, 0)),
            ]
            + [pl.BlockSpec(memory_space=pl.ANY)] * len(pieces),
            out_specs=pl.BlockSpec(
                (HEADS, QUARTERS, rows + REQS, LANES), lambda i, owner: (0, 0, 0, 0)
            ),
            scratch_shapes=[pltpu.VMEM((rows, width), bf16), pltpu.SemaphoreType.DMA(())],
        ),
        out_shape=jax.ShapeDtypeStruct((HEADS, QUARTERS, rows + REQS, LANES), bf16),
        name="prefix_pack",
    )(offset, *in_hbm(got, *pieces))


def query_tile(query_ref):
    packed = query_ref[...].reshape(QUERY_TILE // 2, LANES).astype(f32)
    low = lane_of(packed.shape) < HALF
    first = jnp.where(low, packed, 0.0)
    second = jnp.where(low, pltpu.roll(packed, HALF, 1), 0.0)
    return jnp.concatenate([first, second], axis=0).astype(bf16)


def offset_of(row):
    half_rows = QUERY_TILE // 2
    second = (row >= half_rows).astype(jnp.int32)
    within = row - second * half_rows
    return (within // 16) * ROWS + second * 16 + within % 16


def start_of(position, lengths_ref, zero):
    end = jnp.int32(0)
    start = zero
    for request in range(REQS):
        end = end + lengths_ref[request]
        start = jnp.where(position >= end, end, start)
    return start


def suffix_kernel(quarter_ref, lengths_ref, query_ref, got_ref, out_ref):
    tile = pl.program_id(0)
    blocks = QUERY_TILE // 32
    key_blocks = KEY_TILE // ROWS
    query = query_tile(query_ref)
    first_position = tile * blocks * ROWS + quarter_ref[0] * 32
    position = first_position + offset_of(lax.broadcasted_iota(jnp.int32, (QUERY_TILE, 1), 0))
    start = start_of(position, lengths_ref, jnp.zeros_like(position))
    lowest = start_of(first_position, lengths_ref, jnp.int32(0))
    span = blocks * ROWS
    last_tile = (tile * span + span - 1) // KEY_TILE

    def step(j, carry):
        acc, top, total = carry
        keys = got_ref[pl.ds(j * key_blocks, key_blocks), :, :].reshape(KEY_TILE, LANES)
        scores = lax.dot_general(
            query, keys, (((1,), (1,)), ((), ())), preferred_element_type=f32
        )
        key_position = j * KEY_TILE + lane_of(scores.shape)
        allowed = (key_position >= start) & (key_position <= position)
        scores = jnp.where(allowed, scores, neg_big)
        new_top = jnp.maximum(top, jnp.max(scores, axis=1, keepdims=True))
        shrink = jnp.exp(top - new_top)
        probs = jnp.exp(scores - new_top)
        total = total * shrink + jnp.sum(probs, axis=1, keepdims=True)
        acc = acc * shrink + jnp.dot(probs.astype(bf16), keys, preferred_element_type=f32)
        return acc, new_top, total

    acc, top, total = lax.fori_loop(
        lowest // KEY_TILE,
        last_tile + 1,
        step,
        (
            jnp.zeros((QUERY_TILE, LANES), f32),
            jnp.full((QUERY_TILE, 1), neg_big, f32),
            jnp.zeros((QUERY_TILE, 1), f32),
        ),
    )
    lane = lane_of(acc.shape)
    out_ref[...] = jnp.where(lane == 0, top, jnp.where(lane == 1, total, acc))


def suffix_attention(quarter, lengths, got):
    blocks = got.shape[0]
    queries = blocks * 32
    return pl.pallas_call(
        suffix_kernel,
        grid_spec=pltpu.PrefetchScalarGridSpec(
            num_scalar_prefetch=2,
            grid=(queries // QUERY_TILE,),
            in_specs=[
                pl.BlockSpec((QUERY_TILE // 32, 16, LANES), lambda i, q, l: (i, ROWS // 16, 0)),
                pl.BlockSpec((blocks, ROWS, LANES), lambda i, q, l: (0, 0, 0)),
            ],
            out_specs=pl.BlockSpec((QUERY_TILE, LANES), lambda i, q, l: (i, 0)),
        ),
        out_shape=pltpu.HBM((queries, LANES), f32),
        compiler_params=pltpu.CompilerParams(vmem_limit_bytes=14 << 20),
        name="suffix_attention",
    )(quarter, lengths, *in_hbm(got, got))


def prefix_kernel(quarter_ref, lengths_ref, query_ref, keys_ref, part_ref, out_ref, last_ref):
    tile = pl.program_id(0)
    query = query_tile(query_ref)
    keys = keys_ref[...].reshape(-1, LANES)
    scores = lax.dot_general(query, keys, (((1,), (1,)), ((), ())), preferred_element_type=f32)
    part = part_ref[...]
    part_top = part[:, 0:1]
    part_total = part[:, 1:2]
    top = jnp.maximum(part_top, jnp.max(scores, axis=1, keepdims=True))
    probs = jnp.exp(scores - top)
    shrink = jnp.exp(part_top - top)
    total = part_total * shrink + jnp.sum(probs, axis=1, keepdims=True)
    acc = part * shrink + jnp.dot(probs.astype(bf16), keys, preferred_element_type=f32)
    context = acc / total
    half_rows = QUERY_TILE // 2
    tile_blocks = QUERY_TILE // 32
    low = lane_of((half_rows, LANES)) < HALF
    packed = jnp.where(low, pltpu.roll(context[:half_rows], HALF, 1), context[half_rows:])
    out_ref[pl.ds(tile * tile_blocks, tile_blocks), 0:16, :] = packed.astype(bf16).reshape(
        tile_blocks, 16, LANES
    )
    positions = tile * tile_blocks * ROWS + quarter_ref[0] * 32
    positions = positions + offset_of(lane_of((REQS, QUERY_TILE)))
    is_last = last_matrix(lengths_ref, positions)
    ends = jnp.where(lane_of(context.shape) < HALF, 0.0, context).astype(bf16)
    ends = jnp.dot(is_last, ends, preferred_element_type=f32)

    @pl.when(tile == 0)
    def _():
        last_ref[...] = ends

    @pl.when(tile > 0)
    def _():
        last_ref[...] = last_ref[...] + ends

    @pl.when(tile == pl.num_programs(0) - 1)
    def _():
        every = last_ref[...].astype(bf16)
        for block in range(out_ref.shape[0]):
            out_ref[block, 16:32, :] = every


def prefix_attention(quarter, lengths, got, keys, part):
    blocks = got.shape[0]
    queries = blocks * 32
    rows = keys.shape[1] - REQS
    return pl.pallas_call(
        prefix_kernel,
        grid_spec=pltpu.PrefetchScalarGridSpec(
            num_scalar_prefetch=2,
            grid=(queries // QUERY_TILE,),
            in_specs=[
                pl.BlockSpec((QUERY_TILE // 32, 16, LANES), lambda i, q, l: (i, ROWS // 16, 0)),
                pl.BlockSpec((blocks, rows, LANES), lambda i, q, l: (0, 0, 0)),
                pl.BlockSpec((QUERY_TILE, LANES), lambda i, q, l: (i, 0)),
            ],
            out_specs=pl.BlockSpec((blocks, 32, LANES), lambda i, q, l: (0, 0, 0)),
            scratch_shapes=[pltpu.VMEM((REQS, LANES), f32)],
        ),
        out_shape=jax.ShapeDtypeStruct((blocks, 32, LANES), bf16),
        compiler_params=pltpu.CompilerParams(vmem_limit_bytes=18 << 20),
        name="prefix_attention",
    )(quarter, lengths, *in_hbm(got, keys, part))


def gelu(v):
    return 0.5 * v * (1.0 + jnp.tanh(0.7978845608028654 * (v + 0.044715 * v * v * v)))


def dot_nt(a, b):
    return lax.dot_general(a, b, (((1,), (1,)), ((), ())), preferred_element_type=f32)


def mix_kernel(
    block_ref, ctx_ref, tok_ref, tok_last_ref, gate_last_ref, wout_ref, gain_ref, routes_ref, g_ref, u_ref, d_ref,
    mixed_ref, mixed_last_ref, send_ref, g_v, u_v, d_v, send_v, sems, out_sems,
):
    copies = [
        pltpu.make_async_copy(source, place, sems.at[kind])
        for kind, (source, place) in enumerate(((g_ref, g_v), (u_ref, u_v), (d_ref, d_v)))
    ]
    for copy in copies:
        copy.start()
    tiles = []
    for pair in range(HEADS // 2):
        even = ctx_ref[2 * pair].astype(f32)
        odd = ctx_ref[2 * pair + 1].astype(f32)
        first, second = head_split(even[:, 0:16], odd[:, 0:16])
        both = jnp.stack([first, second], axis=1).reshape(ROWS, LANES)
        even_last = jnp.sum(even[:, 16:32], axis=0)
        odd_last = jnp.sum(odd[:, 16:32], axis=0)
        low = lane_of(even_last.shape) < HALF
        ends = jnp.where(low, pltpu.roll(even_last, HALF, 1), odd_last)
        tiles.append(jnp.concatenate([both, ends], axis=0).astype(bf16))
    context = jnp.concatenate(tiles, axis=1)
    lift = jnp.dot(context, wout_ref[...], preferred_element_type=f32)
    mixed = tok_ref[...].astype(f32) + lift[:ROWS]
    mixed_ref[...] = mixed
    routed = rms_scale(mixed, gain_ref[...]).astype(bf16)
    tok_last = jnp.concatenate([tok_last_ref[QUARTERS * j] for j in range(8)], axis=1)
    mixed_last = tok_last.astype(f32) + lift[ROWS:]
    mixed_last_ref[...] = mixed_last
    routed_last = rms_scale(mixed_last, gain_ref[...]).astype(bf16)
    expert_id = block_ref[0] // QUARTERS
    weights = jnp.sum(gate_last_ref[...].astype(f32), axis=0)
    lane = lane_of(weights.shape)
    mine = (lane % EXPERTS == expert_id) & (lane < 3 * EXPERTS)
    weight = jnp.sum(jnp.where(mine, weights, 0.0), axis=1, keepdims=True)
    copies[0].wait()
    copies[1].wait()
    act = (gelu(dot_nt(routed_last, g_v[...])) * dot_nt(routed_last, u_v[...])).astype(bf16)
    copies[2].wait()
    partial_last = weight * jnp.dot(act, d_v[...], preferred_element_type=f32)
    high = partial_last.astype(bf16)
    low_part = (partial_last - high.astype(f32)).astype(bf16)
    source = jnp.concatenate([routed, high, low_part], axis=0)
    columns = ROWS + 2 * REQS
    expert = lax.broadcasted_iota(jnp.int32, (EXPERTS, ROWS), 0)
    named = (routes_ref[0:1, :] == expert) | (routes_ref[1:2, :] == expert)
    earlier = (
        lax.broadcasted_iota(jnp.int32, (ROWS, ROWS), 0)
        < lax.broadcasted_iota(jnp.int32, (ROWS, ROWS), 1)
    ).astype(bf16)
    slots = jnp.dot(named.astype(f32).astype(bf16), earlier, preferred_element_type=f32)
    slots = jnp.where(named, slots, -1.0).astype(jnp.int32)
    place = slots + jnp.where(slots >= PART_SLOTS, PART_ROWS - PART_SLOTS, 0)
    place_id = lax.broadcasted_iota(jnp.int32, (SLOT_ROWS, ROWS), 0)
    extra_row = lax.broadcasted_iota(jnp.int32, (SLOT_ROWS, 2 * REQS), 0) % PART_ROWS
    extra_column = lane_of((SLOT_ROWS, 2 * REQS))
    sends = []
    for e in range(EXPERTS):
        pick = (place[e : e + 1, :] == place_id).astype(f32)
        for chip in range(2):
            row_last = 2 * e + chip
            extra = ((extra_row == PART_SLOTS) & (extra_column == row_last)) | (
                (extra_row == PART_SLOTS + 1) & (extra_column == REQS + row_last)
            )
            both = jnp.concatenate([pick, extra.astype(f32)], axis=1).astype(bf16)
            send_v[e, chip] = jnp.dot(both, source, preferred_element_type=f32).astype(bf16)
        send = pltpu.make_async_copy(send_v.at[e], send_ref.at[e], out_sems.at[e])
        send.start()
        sends.append(send)
    for send in sends:
        send.wait()


def mix(block, ctx, stream, prefix_got, got, w_out, gain, routes_t, own):
    width = stream.shape[1]
    blocks = got.shape[0]
    units = own[0].shape[0]
    hbm = pl.BlockSpec(memory_space=pl.ANY)

    def whole(shape):
        return pl.BlockSpec(shape, lambda i, b: (0,) * len(shape))

    return pl.pallas_call(
        mix_kernel,
        grid_spec=pltpu.PrefetchScalarGridSpec(
            num_scalar_prefetch=1,
            grid=(1,),
            in_specs=[
                whole(ctx.shape),
                whole(stream.shape),
                pl.BlockSpec((blocks, REQS, LANES), lambda i, b: (0, 4, 0)),
                pl.BlockSpec((blocks, REQS, LANES), lambda i, b: (0, 10, 0)),
                whole(w_out.shape),
                whole(gain.shape),
                whole(routes_t.shape),
                hbm,
                hbm,
                hbm,
            ],
            out_specs=[
                whole((ROWS, width)),
                whole((REQS, width)),
                pl.BlockSpec(memory_space=pltpu.HBM),
            ],
            scratch_shapes=[
                pltpu.VMEM((units, width), bf16),
                pltpu.VMEM((units, width), bf16),
                pltpu.VMEM((units, width), bf16),
                pltpu.VMEM((EXPERTS, 2, SLOT_ROWS, width), bf16),
                pltpu.SemaphoreType.DMA((3,)),
                pltpu.SemaphoreType.DMA((EXPERTS,)),
            ],
        ),
        out_shape=[
            pltpu.HBM((ROWS, width), f32),
            pltpu.HBM((REQS, width), f32),
            pltpu.HBM((EXPERTS, 2, SLOT_ROWS, width), bf16),
        ],
        compiler_params=pltpu.CompilerParams(vmem_limit_bytes=18 << 20),
        name="mix",
    )(block, ctx, stream, *in_hbm(prefix_got, got), w_out, gain, routes_t, *in_hbm(*own))


FFN_TILE = 256


def expert_kernel(
    x_ref, g0, u0, d0, g1, u1, d1, out_ref, gate_v, up_v, down_v, acc_v, out_v, sems, out_sems
):
    sources = ((g0, u0, d0), (g1, u1, d1))
    places = (gate_v, up_v, down_v)
    copies = [
        [
            pltpu.make_async_copy(sources[part][kind], places[kind].at[part], sems.at[part, kind])
            for kind in range(3)
        ]
        for part in range(2)
    ]
    for part in range(2):
        for kind in range(3):
            copies[part][kind].start()
    count = x_ref.shape[0]
    within = lane_of((16, count)) % PART_ROWS
    extra = ((within == PART_SLOTS) | (within == PART_SLOTS + 1)).astype(f32).astype(bf16)
    total = jnp.dot(extra, x_ref[...], preferred_element_type=f32)[0:1]
    high = total.astype(bf16).astype(f32)
    low = (total - high).astype(bf16).astype(f32)
    sends = []
    for part in range(2):
        for tile in range(count // FFN_TILE):
            rows = slice(tile * FFN_TILE, (tile + 1) * FFN_TILE)
            if tile == 0:
                copies[part][0].wait()
                copies[part][1].wait()
            x = x_ref[rows, :]
            hidden = (gelu(dot_nt(x, gate_v[part])) * dot_nt(x, up_v[part])).astype(bf16)
            if tile == 0:
                copies[part][2].wait()
            down = jnp.dot(hidden, down_v[part], preferred_element_type=f32)
            if part == 0:
                acc_v[rows, :] = down
            else:
                row = tile * FFN_TILE + lax.broadcasted_iota(jnp.int32, (FFN_TILE, 1), 0)
                row = row % PART_ROWS
                result = acc_v[rows, :] + down
                result = jnp.where(row == PART_SLOTS, high, result)
                result = jnp.where(row == PART_SLOTS + 1, low, result)
                out_v[rows, :] = result.astype(bf16)
                send = pltpu.make_async_copy(
                    out_v.at[pl.ds(tile * FFN_TILE, FFN_TILE), :],
                    out_ref.at[pl.ds(tile * FFN_TILE, FFN_TILE), :],
                    out_sems.at[tile],
                )
                send.start()
                sends.append(send)
    for send in sends:
        send.wait()


def expert(rows, own, other):
    count, width = rows.shape
    units = own[0].shape[0]
    hbm = pl.BlockSpec(memory_space=pl.ANY)
    vmem = pl.BlockSpec(memory_space=pltpu.VMEM)
    return pl.pallas_call(
        expert_kernel,
        in_specs=[vmem] + [hbm] * 6,
        out_specs=pl.BlockSpec(memory_space=pltpu.HBM),
        out_shape=pltpu.HBM((count, width), bf16),
        scratch_shapes=[
            pltpu.VMEM((2, units, width), bf16),
            pltpu.VMEM((2, units, width), bf16),
            pltpu.VMEM((2, units, width), bf16),
            pltpu.VMEM((count, width), f32),
            pltpu.VMEM((count, width), bf16),
            pltpu.SemaphoreType.DMA((2, 3)),
            pltpu.SemaphoreType.DMA((count // FFN_TILE,)),
        ],
        compiler_params=pltpu.CompilerParams(vmem_limit_bytes=26 << 20),
        name="expert",
    )(rows, *in_hbm(*own, *other))


def column_of(row):
    return jnp.transpose(jnp.broadcast_to(row, (ROWS, LANES)))


def combine_kernel(
    block_ref, lengths_ref, mixed_ref, mixed_last_ref, got_ref, routes_ref, gates_ref, gain_ref,
    hidden_ref, last_ref, norm_ref,
):
    got = got_ref[...]
    count = got.shape[0]
    request_row = lax.broadcasted_iota(jnp.int32, (REQS, count), 0)
    wanted = request_row * (2 * PART_ROWS) + PART_SLOTS
    source = lane_of((REQS, count))
    pick_last = ((source == wanted) | (source == wanted + 1)).astype(f32).astype(bf16)
    moe_last = jnp.dot(pick_last, got, preferred_element_type=f32)
    hidden_last = (mixed_last_ref[...] + moe_last).astype(bf16).astype(f32)
    last_ref[...] = rms_scale(hidden_last, gain_ref[...]).astype(bf16)
    first = column_of(routes_ref[0:1, :].astype(f32)).astype(jnp.int32)
    second = column_of(routes_ref[1:2, :].astype(f32)).astype(jnp.int32)
    lane = lane_of((ROWS, LANES))
    named = ((first == lane) | (second == lane)).astype(f32).astype(bf16)
    earlier = (
        lax.broadcasted_iota(jnp.int32, (ROWS, ROWS), 1)
        < lax.broadcasted_iota(jnp.int32, (ROWS, ROWS), 0)
    ).astype(bf16)
    slots = jnp.dot(earlier, named, preferred_element_type=f32)
    column = lane_of((ROWS, count))
    moe = None
    for which, chosen in enumerate((first, second)):
        slot = jnp.sum(jnp.where(chosen == lane, slots, 0.0), axis=1, keepdims=True)
        slot = slot.astype(jnp.int32)
        place = slot + jnp.where(slot >= PART_SLOTS, PART_ROWS - PART_SLOTS, 0)
        target = chosen[:, 0:1] * (2 * SLOT_ROWS) + place
        pick = ((column == target) | (column == target + SLOT_ROWS)).astype(f32).astype(bf16)
        picked = jnp.dot(pick, got, preferred_element_type=f32)
        term = column_of(gates_ref[which : which + 1, :])[:, 0:1] * picked
        moe = term if moe is None else moe + term
    hidden = (mixed_ref[...] + moe).astype(bf16)
    hidden_ref[...] = hidden
    wide = hidden.astype(f32)
    squares = jnp.sum(wide * wide, axis=1, keepdims=True)
    position = block_ref[0] * ROWS + lax.broadcasted_iota(jnp.int32, (ROWS, LANES), 0)
    starts = jnp.zeros((1, LANES), jnp.int32)
    ends = jnp.zeros((1, LANES), jnp.int32)
    lane_row = lane_of((1, LANES))
    end = jnp.int32(0)
    for r in range(REQS):
        starts = jnp.where(lane_row == r, end, starts)
        end = end + lengths_ref[r]
        ends = jnp.where(lane_row == r, end, ends)
    member = (position >= starts) & (position < ends)
    norm_ref[...] = jnp.sum(jnp.where(member, squares, 0.0), axis=0, keepdims=True)


def combine(block, lengths, mixed, mixed_last, got, routes, gates, gain):
    width = mixed.shape[1]
    vmem = pl.BlockSpec(memory_space=pltpu.VMEM)
    smem = pl.BlockSpec(memory_space=pltpu.SMEM)
    return pl.pallas_call(
        combine_kernel,
        in_specs=[smem, smem] + [vmem] * 6,
        out_specs=[vmem] * 3,
        out_shape=[
            jax.ShapeDtypeStruct((ROWS, width), bf16),
            jax.ShapeDtypeStruct((REQS, width), bf16),
            jax.ShapeDtypeStruct((1, LANES), f32),
        ],
        compiler_params=pltpu.CompilerParams(vmem_limit_bytes=16 << 20),
        name="combine",
    )(block, lengths, mixed, mixed_last, got, routes, gates, gain)


def exchange(rows):
    return lax.all_to_all(rows, "blk", split_axis=0, concat_axis=0, tiled=True)


def ring_pieces(piece):
    size = lax.axis_size("grp")

    def shift(one, by):
        return lax.ppermute(one, "grp", [(i, (i + by) % size) for i in range(size)])

    pieces = {0: piece}
    for by in (1, 2, -1, -2):
        pieces[by % size] = shift(piece, by)
    pieces[3] = shift(pieces[1], 2)
    pieces[4] = shift(pieces[2], 2)
    pieces[5] = shift(pieces[7], -2)
    return [pieces[k] for k in range(size)]


def local(
    tokens,
    lengths,
    owners,
    prefix_cache,
    routes,
    gates,
    attn_gain,
    w_query,
    w_keyval,
    w_out,
    moe_gain,
    w_gate,
    w_up,
    w_down,
    final_gain,
    unembed,
):
    blocks = lax.axis_size("blk")
    block_index = lax.axis_index("blk")
    width = tokens.shape[2]
    stream = tokens[0]
    block = block_index.astype(jnp.int32).reshape(1)
    quarter = block % QUARTERS
    swap = [(i, i ^ 1) for i in range(blocks)]
    with jax.named_scope("prefix_gather"):
        pieces = ring_pieces(prefix_cache[0])
        offset = (lax.axis_index("grp").astype(jnp.int32) - owners) % len(pieces)
    with jax.named_scope("weight_swap"):
        own = (w_gate[0].T, w_up[0].T, w_down[0])
        other = tuple(lax.ppermute(one, "blk", swap) for one in own)
    routes_t = routes[0].T
    gates_t = gates[0].T
    suffix_kv, send = project(
        block, lengths[0], stream, attn_gain.reshape(1, -1), w_query, w_keyval, routes_t, gates_t
    )
    with jax.named_scope("qkv_exchange"):
        got = exchange(send.reshape(blocks, SEND_ROWS, LANES))
    part = suffix_attention(quarter, lengths[0], got)
    packed = prefix_pack(pieces, offset, got)
    with jax.named_scope("prefix_exchange"):
        prefix_got = exchange(packed.reshape(blocks, packed.shape[2], LANES))
    context = prefix_attention(quarter, lengths[0], got, prefix_got, part)
    with jax.named_scope("context_exchange"):
        ctx = exchange(context).reshape(HEADS, QUARTERS, 32, LANES)
    mixed, mixed_last, outgoing = mix(
        block, ctx, stream, prefix_got, got, w_out, moe_gain.reshape(1, -1), routes_t, own
    )
    with jax.named_scope("dispatch_exchange"):
        rows = exchange(outgoing.reshape(blocks, PART_ROWS, width))
    results = expert(rows.reshape(-1, width), own, other)
    with jax.named_scope("return_exchange"):
        returned = exchange(results.reshape(blocks, PART_ROWS, width)).reshape(-1, width)
    hidden, last_rows, norm_terms = combine(
        block, lengths[0], mixed, mixed_last, returned, routes_t, gates_t, final_gain.reshape(1, -1)
    )
    logits = jnp.dot(last_rows, unembed, preferred_element_type=f32)
    best = jnp.max(logits, axis=1)
    with jax.named_scope("final_exchange"):
        final = jnp.concatenate([norm_terms[:, :REQS], best[None, :]], axis=1)
        final = jnp.pad(final, ((0, 0), (0, LANES - 2 * REQS)))
        final = exchange(jnp.broadcast_to(final[None], (blocks, 1, LANES)))[:, 0, :]
    norm_sums = jnp.sum(final[:, :REQS], axis=0)
    greatest = jnp.max(final[:, REQS : 2 * REQS], axis=0)
    request_norm = jnp.sqrt(norm_sums / (lengths[0].astype(f32) * width))
    return (hidden[None], suffix_kv[None], request_norm[None], greatest[None])


def solution(mesh):
    placed = (
        P("grp", "blk", None),
        P("grp", None),
        P("grp"),
        P("grp", "blk", None),
        P("grp", "blk", None),
        P("grp", "blk", None),
        P(),
        P(),
        P(),
        P(),
        P(),
        P("blk", None, None),
        P("blk", None, None),
        P("blk", None, None),
        P(),
        P(None, "blk"),
    )
    return jax.shard_map(
        local,
        mesh=mesh,
        in_specs=placed,
        out_specs=(P("grp", "blk", None), P("grp", "blk", None), P("grp", None), P("grp", None)),
        check_vma=False,
    )
```

```python
import jax
import jax.numpy as jnp
from jax import lax
from jax.experimental import pallas as pl
from jax.experimental.pallas import tpu as pltpu
from jax.sharding import PartitionSpec as P

HEADS = 8
EXPERTS = 8
QUARTERS = 4
CAP = 40
SLOT_ROWS = 48
PART_ROWS = 24
PART_SLOTS = 20
SEND_ROWS = 176
REQS = 16
ROWS = 128
HALF = 64
LANES = 128
KEY_TILE = 1024
QUERY_TILE = 256
PREFIX_TILE = 1024
PREFIX_SUB = 128

epsilon = 1e-06
neg_big = -1e30
bf16 = jnp.bfloat16
f32 = jnp.float32


def rms_scale(values, gain_vector):
    return (
        values * lax.rsqrt(jnp.mean(values * values, axis=-1, keepdims=True) + epsilon) * gain_vector
    )


def lane_of(shape):
    return lax.broadcasted_iota(jnp.int32, shape, len(shape) - 1)


def head_split(first, second):
    low = lane_of(first.shape) < HALF
    axis = len(first.shape) - 1
    even = jnp.where(low, first, pltpu.roll(second, HALF, axis))
    odd = jnp.where(low, pltpu.roll(first, HALF, axis), second)
    return even, odd


def last_matrix(lengths_ref, positions):
    request = lax.broadcasted_iota(jnp.int32, positions.shape, 0)
    lasts = jnp.full(positions.shape, -1, jnp.int32)
    end = jnp.int32(0)
    for r in range(REQS):
        end = end + lengths_ref[r]
        lasts = jnp.where(request == r, end - 1, lasts)
    return (lasts == positions).astype(f32).astype(bf16)


def three_parts(values):
    high = values.astype(bf16).astype(f32)
    middle = (values - high).astype(bf16).astype(f32)
    low = (values - high - middle).astype(bf16).astype(f32)
    return high, middle, low


def in_hbm(*arrays):
    return tuple(pltpu.with_memory_space_constraint(one, pltpu.HBM) for one in arrays)


def project_kernel(
    block_ref, lengths_ref, tok_ref, gain_ref, wq_ref, wk_ref, wv_ref, routes_ref, gates_ref,
    kv_ref, send_ref, normed_ref, gate_ref,
):
    pair = pl.program_id(0)
    is_last = last_matrix(lengths_ref, block_ref[0] * ROWS + lane_of((REQS, ROWS)))

    @pl.when(pair == 0)
    def _():
        normed_ref[...] = rms_scale(tok_ref[...].astype(f32), gain_ref[...]).astype(bf16)
        row = lax.broadcasted_iota(jnp.int32, (LANES, ROWS), 0)
        named = row % EXPERTS
        weight = jnp.where(
            routes_ref[0:1, :] == named,
            gates_ref[0:1, :],
            jnp.where(routes_ref[1:2, :] == named, gates_ref[1:2, :], 0.0),
        )
        high, middle, low = three_parts(weight)
        piece = row // EXPERTS
        pieces = jnp.where(
            piece == 0, high, jnp.where(piece == 1, middle, jnp.where(piece == 2, low, 0.0))
        )
        gate_ref[...] = lax.dot_general(
            is_last, pieces.astype(bf16), (((1,), (1,)), ((), ())), preferred_element_type=f32
        ).astype(bf16)

    normed = normed_ref[...]
    query = jnp.dot(normed, wq_ref[...], preferred_element_type=f32).astype(bf16)
    key = jnp.dot(normed, wk_ref[...], preferred_element_type=f32).astype(bf16)
    value = jnp.dot(normed, wv_ref[...], preferred_element_type=f32).astype(bf16)
    column = pl.multiple_of(pair * LANES, LANES)
    kv_ref[:, pl.ds(column, LANES)] = key
    kv_ref[:, pl.ds(HEADS * HALF + column, LANES)] = value
    even, odd = head_split(key.astype(f32), value.astype(f32))
    even = even.astype(bf16)
    odd = odd.astype(bf16)
    wide = pl.multiple_of(pair * 2 * LANES, 2 * LANES)
    ends = jnp.dot(
        is_last, tok_ref[:, pl.ds(wide, 2 * LANES)], preferred_element_type=f32
    ).astype(bf16)
    scaled = query.astype(f32) * (HALF**-0.5)
    for quarter in range(QUARTERS):
        first = scaled[quarter * 32 : quarter * 32 + 16]
        second = scaled[quarter * 32 + 16 : quarter * 32 + 32]
        query_even, query_odd = head_split(first, second)
        send_ref[0, quarter, 0:ROWS, :] = even
        send_ref[1, quarter, 0:ROWS, :] = odd
        send_ref[0, quarter, ROWS : ROWS + 16, :] = query_even.astype(bf16)
        send_ref[1, quarter, ROWS : ROWS + 16, :] = query_odd.astype(bf16)
        for which in range(2):
            send_ref[which, quarter, ROWS + 16 : ROWS + 32, :] = ends[
                :, which * LANES : (which + 1) * LANES
            ]
            send_ref[which, quarter, ROWS + 32 : ROWS + 48, :] = gate_ref[...]


def project(block, lengths, stream, gain, w_query, w_keyval, routes_t, gates_t):
    width = stream.shape[1]
    return pl.pallas_call(
        project_kernel,
        grid_spec=pltpu.PrefetchScalarGridSpec(
            num_scalar_prefetch=2,
            grid=(HEADS // 2,),
            in_specs=[
                pl.BlockSpec((ROWS, width), lambda i, b, l: (0, 0)),
                pl.BlockSpec((1, width), lambda i, b, l: (0, 0)),
                pl.BlockSpec((width, LANES), lambda i, b, l: (0, i)),
                pl.BlockSpec((width, LANES), lambda i, b, l: (0, i)),
                pl.BlockSpec((width, LANES), lambda i, b, l: (0, i + HEADS // 2)),
                pl.BlockSpec((2, ROWS), lambda i, b, l: (0, 0)),
                pl.BlockSpec((2, ROWS), lambda i, b, l: (0, 0)),
            ],
            out_specs=[
                pl.BlockSpec((ROWS, 2 * HEADS * HALF), lambda i, b, l: (0, 0)),
                pl.BlockSpec((2, QUARTERS, SEND_ROWS, LANES), lambda i, b, l: (i, 0, 0, 0)),
            ],
            scratch_shapes=[pltpu.VMEM((ROWS, width), bf16), pltpu.VMEM((REQS, LANES), bf16)],
        ),
        out_shape=[
            jax.ShapeDtypeStruct((ROWS, 2 * HEADS * HALF), bf16),
            jax.ShapeDtypeStruct((HEADS, QUARTERS, SEND_ROWS, LANES), bf16),
        ],
        name="project",
    )(block, lengths, stream, gain, w_query, w_keyval, w_keyval, routes_t, gates_t)


def prefix_pack_kernel(offset_ref, ends_ref, *refs):
    pieces = refs[: len(refs) - 3]
    out_ref, prefix_v, sem = refs[len(refs) - 3 :]
    for k, piece in enumerate(pieces):

        @pl.when(offset_ref[0] == k)
        def _():
            copy = pltpu.make_async_copy(piece, prefix_v, sem)
            copy.start()
            copy.wait()

    rows = prefix_v.shape[0]
    for pair in range(HEADS // 2):
        key = prefix_v[:, pair * LANES : (pair + 1) * LANES].astype(f32)
        base = HEADS * HALF + pair * LANES
        value = prefix_v[:, base : base + LANES].astype(f32)
        even, odd = head_split(key, value)
        for quarter in range(QUARTERS):
            out_ref[2 * pair, quarter, 0:rows, :] = even.astype(bf16)
            out_ref[2 * pair + 1, quarter, 0:rows, :] = odd.astype(bf16)
    ends = jnp.sum(ends_ref[...].astype(f32), axis=0).astype(bf16)
    for head in range(HEADS):
        for quarter in range(QUARTERS):
            out_ref[head, quarter, rows : rows + REQS, :] = ends


def prefix_pack(pieces, offset, got):
    rows, width = pieces[0].shape
    return pl.pallas_call(
        prefix_pack_kernel,
        grid_spec=pltpu.PrefetchScalarGridSpec(
            num_scalar_prefetch=1,
            grid=(1,),
            in_specs=[
                pl.BlockSpec((got.shape[0], REQS, LANES), lambda i, owner: (0, 9, 0)),
            ]
            + [pl.BlockSpec(memory_space=pl.ANY)] * len(pieces),
            out_specs=pl.BlockSpec(
                (HEADS, QUARTERS, rows + REQS, LANES), lambda i, owner: (0, 0, 0, 0)
            ),
            scratch_shapes=[pltpu.VMEM((rows, width), bf16), pltpu.SemaphoreType.DMA(())],
        ),
        out_shape=jax.ShapeDtypeStruct((HEADS, QUARTERS, rows + REQS, LANES), bf16),
        name="prefix_pack",
    )(offset, *in_hbm(got, *pieces))


def query_tile(query_ref):
    packed = query_ref[...].reshape(QUERY_TILE // 2, LANES).astype(f32)
    low = lane_of(packed.shape) < HALF
    first = jnp.where(low, packed, 0.0)
    second = jnp.where(low, pltpu.roll(packed, HALF, 1), 0.0)
    return jnp.concatenate([first, second], axis=0).astype(bf16)


def offset_of(row):
    half_rows = QUERY_TILE // 2
    second = (row >= half_rows).astype(jnp.int32)
    within = row - second * half_rows
    return (within // 16) * ROWS + second * 16 + within % 16


def start_of(position, lengths_ref, zero):
    end = jnp.int32(0)
    start = zero
    for request in range(REQS):
        end = end + lengths_ref[request]
        start = jnp.where(position >= end, end, start)
    return start


def suffix_kernel(quarter_ref, lengths_ref, query_ref, got_ref, out_ref):
    tile = pl.program_id(0)
    blocks = QUERY_TILE // 32
    key_blocks = KEY_TILE // ROWS
    query = query_tile(query_ref)
    first_position = tile * blocks * ROWS + quarter_ref[0] * 32
    position = first_position + offset_of(lax.broadcasted_iota(jnp.int32, (QUERY_TILE, 1), 0))
    start = start_of(position, lengths_ref, jnp.zeros_like(position))
    lowest = start_of(first_position, lengths_ref, jnp.int32(0))
    span = blocks * ROWS
    last_tile = (tile * span + span - 1) // KEY_TILE

    def step(j, carry):
        acc, top, total = carry
        keys = got_ref[pl.ds(j * key_blocks, key_blocks), :, :].reshape(KEY_TILE, LANES)
        scores = lax.dot_general(
            query, keys, (((1,), (1,)), ((), ())), preferred_element_type=f32
        )
        key_position = j * KEY_TILE + lane_of(scores.shape)
        allowed = (key_position >= start) & (key_position <= position)
        scores = jnp.where(allowed, scores, neg_big)
        new_top = jnp.maximum(top, jnp.max(scores, axis=1, keepdims=True))
        shrink = jnp.exp(top - new_top)
        probs = jnp.exp(scores - new_top)
        total = total * shrink + jnp.sum(probs, axis=1, keepdims=True)
        acc = acc * shrink + jnp.dot(probs.astype(bf16), keys, preferred_element_type=f32)
        return acc, new_top, total

    acc, top, total = lax.fori_loop(
        lowest // KEY_TILE,
        last_tile + 1,
        step,
        (
            jnp.zeros((QUERY_TILE, LANES), f32),
            jnp.full((QUERY_TILE, 1), neg_big, f32),
            jnp.zeros((QUERY_TILE, 1), f32),
        ),
    )
    lane = lane_of(acc.shape)
    out_ref[...] = jnp.where(lane == 0, top, jnp.where(lane == 1, total, acc))


def suffix_attention(quarter, lengths, got):
    blocks = got.shape[0]
    queries = blocks * 32
    return pl.pallas_call(
        suffix_kernel,
        grid_spec=pltpu.PrefetchScalarGridSpec(
            num_scalar_prefetch=2,
            grid=(queries // QUERY_TILE,),
            in_specs=[
                pl.BlockSpec((QUERY_TILE // 32, 16, LANES), lambda i, q, l: (i, ROWS // 16, 0)),
                pl.BlockSpec((blocks, ROWS, LANES), lambda i, q, l: (0, 0, 0)),
            ],
            out_specs=pl.BlockSpec((QUERY_TILE, LANES), lambda i, q, l: (i, 0)),
        ),
        out_shape=pltpu.HBM((queries, LANES), f32),
        compiler_params=pltpu.CompilerParams(vmem_limit_bytes=14 << 20),
        name="suffix_attention",
    )(quarter, lengths, *in_hbm(got, got))


def prefix_kernel(quarter_ref, lengths_ref, query_ref, keys_ref, part_ref, out_ref, last_ref):
    tile = pl.program_id(0)
    tile_blocks = PREFIX_TILE // 32
    half_rows = PREFIX_TILE // 2
    packed = query_ref[...].reshape(half_rows, LANES).astype(f32)
    low = lane_of(packed.shape) < HALF
    query = jnp.concatenate(
        [jnp.where(low, packed, 0.0), jnp.where(low, pltpu.roll(packed, HALF, 1), 0.0)], axis=0
    ).astype(bf16)
    keys = keys_ref[...].reshape(-1, LANES)
    subs = PREFIX_TILE // PREFIX_SUB

    def score(sub):
        rows = slice(sub * PREFIX_SUB, (sub + 1) * PREFIX_SUB)
        return lax.dot_general(
            query[rows], keys, (((1,), (1,)), ((), ())), preferred_element_type=f32
        )

    def part_rows(sub):
        pieces = []
        per = QUERY_TILE // 2
        for start in range(sub * PREFIX_SUB, (sub + 1) * PREFIX_SUB, min(per, PREFIX_SUB)):
            second, rest = divmod(start, half_rows)
            group, inside = divmod(rest, per)
            first = group * QUERY_TILE + second * per + inside
            pieces.append(part_ref[first : first + min(per, PREFIX_SUB), :])
        return pieces[0] if len(pieces) == 1 else jnp.concatenate(pieces, axis=0)

    contexts = []
    scores = score(0)
    for sub in range(subs):
        following = score(sub + 1) if sub + 1 < subs else None
        part = part_rows(sub)
        part_top = part[:, 0:1]
        part_total = part[:, 1:2]
        top = jnp.maximum(part_top, jnp.max(scores, axis=1, keepdims=True))
        probs = jnp.exp(scores - top)
        shrink = jnp.exp(part_top - top)
        total = part_total * shrink + jnp.sum(probs, axis=1, keepdims=True)
        acc = part * shrink + jnp.dot(probs.astype(bf16), keys, preferred_element_type=f32)
        contexts.append(acc / total)
        scores = following
    context = contexts[0] if subs == 1 else jnp.concatenate(contexts, axis=0)
    packed = jnp.where(low, pltpu.roll(context[:half_rows], HALF, 1), context[half_rows:])
    out_ref[pl.ds(tile * tile_blocks, tile_blocks), 0:16, :] = packed.astype(bf16).reshape(
        tile_blocks, 16, LANES
    )
    row = lane_of((REQS, PREFIX_TILE))
    second = (row >= half_rows).astype(jnp.int32)
    within = row - second * half_rows
    positions = tile * tile_blocks * ROWS + quarter_ref[0] * 32
    positions = positions + (within // 16) * ROWS + second * 16 + within % 16
    is_last = last_matrix(lengths_ref, positions)
    ends = jnp.where(lane_of(context.shape) < HALF, 0.0, context).astype(bf16)
    ends = jnp.dot(is_last, ends, preferred_element_type=f32)

    @pl.when(tile == 0)
    def _():
        last_ref[...] = ends

    @pl.when(tile > 0)
    def _():
        last_ref[...] = last_ref[...] + ends

    @pl.when(tile == pl.num_programs(0) - 1)
    def _():
        every = last_ref[...].astype(bf16)
        for block in range(out_ref.shape[0]):
            out_ref[block, 16:32, :] = every


def prefix_attention(quarter, lengths, got, keys, part):
    blocks = got.shape[0]
    queries = blocks * 32
    rows = keys.shape[1] - REQS
    return pl.pallas_call(
        prefix_kernel,
        grid_spec=pltpu.PrefetchScalarGridSpec(
            num_scalar_prefetch=2,
            grid=(queries // PREFIX_TILE,),
            in_specs=[
                pl.BlockSpec((PREFIX_TILE // 32, 16, LANES), lambda i, q, l: (i, ROWS // 16, 0)),
                pl.BlockSpec((blocks, rows, LANES), lambda i, q, l: (0, 0, 0)),
                pl.BlockSpec((PREFIX_TILE, LANES), lambda i, q, l: (i, 0)),
            ],
            out_specs=pl.BlockSpec((blocks, 32, LANES), lambda i, q, l: (0, 0, 0)),
            scratch_shapes=[pltpu.VMEM((REQS, LANES), f32)],
        ),
        out_shape=jax.ShapeDtypeStruct((blocks, 32, LANES), bf16),
        compiler_params=pltpu.CompilerParams(vmem_limit_bytes=18 << 20),
        name="prefix_attention",
    )(quarter, lengths, *in_hbm(got, keys, part))


def gelu(v):
    scale = 0.7978845608028654
    half = 0.5 * v
    return half + half * jnp.tanh(v * (scale + (scale * 0.044715) * (v * v)))


def dot_nt(a, b):
    return lax.dot_general(a, b, (((1,), (1,)), ((), ())), preferred_element_type=f32)


def mix_kernel(
    block_ref, ctx_ref, tok_ref, tok_last_ref, gate_last_ref, wout_ref, gain_ref, routes_ref, g_ref, u_ref, d_ref,
    mixed_ref, mixed_last_ref, send_ref, g_v, u_v, d_v, send_v, sems, out_sems,
):
    copies = [
        pltpu.make_async_copy(source, place, sems.at[kind])
        for kind, (source, place) in enumerate(((g_ref, g_v), (u_ref, u_v), (d_ref, d_v)))
    ]
    for copy in copies:
        copy.start()
    tiles = []
    for pair in range(HEADS // 2):
        even = ctx_ref[2 * pair].astype(f32)
        odd = ctx_ref[2 * pair + 1].astype(f32)
        first, second = head_split(even[:, 0:16], odd[:, 0:16])
        both = jnp.stack([first, second], axis=1).reshape(ROWS, LANES)
        even_last = jnp.sum(even[:, 16:32], axis=0)
        odd_last = jnp.sum(odd[:, 16:32], axis=0)
        low = lane_of(even_last.shape) < HALF
        ends = jnp.where(low, pltpu.roll(even_last, HALF, 1), odd_last)
        tiles.append(jnp.concatenate([both, ends], axis=0).astype(bf16))
    context = jnp.concatenate(tiles, axis=1)
    lift = jnp.dot(context, wout_ref[...], preferred_element_type=f32)
    mixed = tok_ref[...].astype(f32) + lift[:ROWS]
    mixed_ref[...] = mixed
    routed = rms_scale(mixed, gain_ref[...]).astype(bf16)
    tok_last = jnp.concatenate([tok_last_ref[QUARTERS * j] for j in range(8)], axis=1)
    mixed_last = tok_last.astype(f32) + lift[ROWS:]
    mixed_last_ref[...] = mixed_last
    routed_last = rms_scale(mixed_last, gain_ref[...]).astype(bf16)
    expert_id = block_ref[0] // QUARTERS
    weights = jnp.sum(gate_last_ref[...].astype(f32), axis=0)
    lane = lane_of(weights.shape)
    mine = (lane % EXPERTS == expert_id) & (lane < 3 * EXPERTS)
    weight = jnp.sum(jnp.where(mine, weights, 0.0), axis=1, keepdims=True)
    copies[0].wait()
    copies[1].wait()
    act = (gelu(dot_nt(routed_last, g_v[...])) * dot_nt(routed_last, u_v[...])).astype(bf16)
    copies[2].wait()
    partial_last = weight * jnp.dot(act, d_v[...], preferred_element_type=f32)
    high = partial_last.astype(bf16)
    low_part = (partial_last - high.astype(f32)).astype(bf16)
    source = jnp.concatenate([routed, high, low_part], axis=0)
    columns = ROWS + 2 * REQS
    expert = lax.broadcasted_iota(jnp.int32, (EXPERTS, ROWS), 0)
    named = (routes_ref[0:1, :] == expert) | (routes_ref[1:2, :] == expert)
    earlier = (
        lax.broadcasted_iota(jnp.int32, (ROWS, ROWS), 0)
        < lax.broadcasted_iota(jnp.int32, (ROWS, ROWS), 1)
    ).astype(bf16)
    slots = jnp.dot(named.astype(f32).astype(bf16), earlier, preferred_element_type=f32)
    slots = jnp.where(named, slots, -1.0).astype(jnp.int32)
    place = slots + jnp.where(slots >= PART_SLOTS, PART_ROWS - PART_SLOTS, 0)
    place_id = lax.broadcasted_iota(jnp.int32, (SLOT_ROWS, ROWS), 0)
    extra_row = lax.broadcasted_iota(jnp.int32, (SLOT_ROWS, 2 * REQS), 0) % PART_ROWS
    extra_column = lane_of((SLOT_ROWS, 2 * REQS))
    sends = []
    for e in range(EXPERTS):
        pick = (place[e : e + 1, :] == place_id).astype(f32)
        for chip in range(2):
            row_last = 2 * e + chip
            extra = ((extra_row == PART_SLOTS) & (extra_column == row_last)) | (
                (extra_row == PART_SLOTS + 1) & (extra_column == REQS + row_last)
            )
            both = jnp.concatenate([pick, extra.astype(f32)], axis=1).astype(bf16)
            send_v[e, chip] = jnp.dot(both, source, preferred_element_type=f32).astype(bf16)
        send = pltpu.make_async_copy(send_v.at[e], send_ref.at[e], out_sems.at[e])
        send.start()
        sends.append(send)
    for send in sends:
        send.wait()


def mix(block, ctx, stream, prefix_got, got, w_out, gain, routes_t, own):
    width = stream.shape[1]
    blocks = got.shape[0]
    units = own[0].shape[0]
    hbm = pl.BlockSpec(memory_space=pl.ANY)

    def whole(shape):
        return pl.BlockSpec(shape, lambda i, b: (0,) * len(shape))

    return pl.pallas_call(
        mix_kernel,
        grid_spec=pltpu.PrefetchScalarGridSpec(
            num_scalar_prefetch=1,
            grid=(1,),
            in_specs=[
                whole(ctx.shape),
                whole(stream.shape),
                pl.BlockSpec((blocks, REQS, LANES), lambda i, b: (0, 4, 0)),
                pl.BlockSpec((blocks, REQS, LANES), lambda i, b: (0, 10, 0)),
                whole(w_out.shape),
                whole(gain.shape),
                whole(routes_t.shape),
                hbm,
                hbm,
                hbm,
            ],
            out_specs=[
                whole((ROWS, width)),
                whole((REQS, width)),
                pl.BlockSpec(memory_space=pltpu.HBM),
            ],
            scratch_shapes=[
                pltpu.VMEM((units, width), bf16),
                pltpu.VMEM((units, width), bf16),
                pltpu.VMEM((units, width), bf16),
                pltpu.VMEM((EXPERTS, 2, SLOT_ROWS, width), bf16),
                pltpu.SemaphoreType.DMA((3,)),
                pltpu.SemaphoreType.DMA((EXPERTS,)),
            ],
        ),
        out_shape=[
            pltpu.HBM((ROWS, width), f32),
            pltpu.HBM((REQS, width), f32),
            pltpu.HBM((EXPERTS, 2, SLOT_ROWS, width), bf16),
        ],
        compiler_params=pltpu.CompilerParams(vmem_limit_bytes=18 << 20),
        name="mix",
    )(block, ctx, stream, *in_hbm(prefix_got, got), w_out, gain, routes_t, *in_hbm(*own))


FFN_TILE = 256


def expert_kernel(
    x_ref, g0, u0, d0, g1, u1, d1, out_ref, gate_v, up_v, down_v, acc_v, out_v, sems, out_sems
):
    sources = ((g0, u0, d0), (g1, u1, d1))
    places = (gate_v, up_v, down_v)
    copies = [
        [
            pltpu.make_async_copy(sources[part][kind], places[kind].at[part], sems.at[part, kind])
            for kind in range(3)
        ]
        for part in range(2)
    ]
    for part in range(2):
        for kind in range(3):
            copies[part][kind].start()
    count = x_ref.shape[0]
    within = lane_of((16, count)) % PART_ROWS
    extra = ((within == PART_SLOTS) | (within == PART_SLOTS + 1)).astype(f32).astype(bf16)
    total = jnp.dot(extra, x_ref[...], preferred_element_type=f32)[0:1]
    high = total.astype(bf16).astype(f32)
    low = (total - high).astype(bf16).astype(f32)
    sends = []
    tiles = count // FFN_TILE
    work = [(part, tile) for part in range(2) for tile in range(tiles)]

    def span(tile):
        return slice(tile * FFN_TILE, (tile + 1) * FFN_TILE)

    def lift(part, tile):
        if tile == 0:
            copies[part][0].wait()
            copies[part][1].wait()
        x = x_ref[span(tile), :]
        return dot_nt(x, gate_v[part]), dot_nt(x, up_v[part])

    ready = lift(*work[0])
    for index, (part, tile) in enumerate(work):
        gate, up = ready
        if index + 1 < len(work):
            ready = lift(*work[index + 1])
        hidden = (gelu(gate) * up).astype(bf16)
        if tile == 0:
            copies[part][2].wait()
        down = jnp.dot(hidden, down_v[part], preferred_element_type=f32)
        if part == 0:
            acc_v[span(tile), :] = down
        else:
            row = tile * FFN_TILE + lax.broadcasted_iota(jnp.int32, (FFN_TILE, 1), 0)
            row = row % PART_ROWS
            result = acc_v[span(tile), :] + down
            result = jnp.where(row == PART_SLOTS, high, result)
            result = jnp.where(row == PART_SLOTS + 1, low, result)
            out_v[span(tile), :] = result.astype(bf16)
            send = pltpu.make_async_copy(
                out_v.at[pl.ds(tile * FFN_TILE, FFN_TILE), :],
                out_ref.at[pl.ds(tile * FFN_TILE, FFN_TILE), :],
                out_sems.at[tile],
            )
            send.start()
            sends.append(send)
    for send in sends:
        send.wait()


def expert(rows, own, other):
    count, width = rows.shape
    units = own[0].shape[0]
    hbm = pl.BlockSpec(memory_space=pl.ANY)
    vmem = pl.BlockSpec(memory_space=pltpu.VMEM)
    return pl.pallas_call(
        expert_kernel,
        in_specs=[vmem] + [hbm] * 6,
        out_specs=pl.BlockSpec(memory_space=pltpu.HBM),
        out_shape=pltpu.HBM((count, width), bf16),
        scratch_shapes=[
            pltpu.VMEM((2, units, width), bf16),
            pltpu.VMEM((2, units, width), bf16),
            pltpu.VMEM((2, units, width), bf16),
            pltpu.VMEM((count, width), f32),
            pltpu.VMEM((count, width), bf16),
            pltpu.SemaphoreType.DMA((2, 3)),
            pltpu.SemaphoreType.DMA((count // FFN_TILE,)),
        ],
        compiler_params=pltpu.CompilerParams(vmem_limit_bytes=26 << 20),
        name="expert",
    )(rows, *in_hbm(*own, *other))


def column_of(row):
    return jnp.transpose(jnp.broadcast_to(row, (ROWS, LANES)))


def combine_kernel(
    block_ref, lengths_ref, mixed_ref, mixed_last_ref, got_ref, routes_ref, gates_ref, gain_ref,
    hidden_ref, last_ref, norm_ref,
):
    got = got_ref[...]
    count = got.shape[0]
    request_row = lax.broadcasted_iota(jnp.int32, (REQS, count), 0)
    wanted = request_row * (2 * PART_ROWS) + PART_SLOTS
    source = lane_of((REQS, count))
    pick_last = ((source == wanted) | (source == wanted + 1)).astype(f32).astype(bf16)
    moe_last = jnp.dot(pick_last, got, preferred_element_type=f32)
    hidden_last = (mixed_last_ref[...] + moe_last).astype(bf16).astype(f32)
    last_ref[...] = rms_scale(hidden_last, gain_ref[...]).astype(bf16)
    first = column_of(routes_ref[0:1, :].astype(f32)).astype(jnp.int32)
    second = column_of(routes_ref[1:2, :].astype(f32)).astype(jnp.int32)
    lane = lane_of((ROWS, LANES))
    named = ((first == lane) | (second == lane)).astype(f32).astype(bf16)
    earlier = (
        lax.broadcasted_iota(jnp.int32, (ROWS, ROWS), 1)
        < lax.broadcasted_iota(jnp.int32, (ROWS, ROWS), 0)
    ).astype(bf16)
    slots = jnp.dot(earlier, named, preferred_element_type=f32)
    column = lane_of((ROWS, count))
    moe = None
    for which, chosen in enumerate((first, second)):
        slot = jnp.sum(jnp.where(chosen == lane, slots, 0.0), axis=1, keepdims=True)
        slot = slot.astype(jnp.int32)
        place = slot + jnp.where(slot >= PART_SLOTS, PART_ROWS - PART_SLOTS, 0)
        target = chosen[:, 0:1] * (2 * SLOT_ROWS) + place
        pick = ((column == target) | (column == target + SLOT_ROWS)).astype(f32).astype(bf16)
        picked = jnp.dot(pick, got, preferred_element_type=f32)
        term = column_of(gates_ref[which : which + 1, :])[:, 0:1] * picked
        moe = term if moe is None else moe + term
    hidden = (mixed_ref[...] + moe).astype(bf16)
    hidden_ref[...] = hidden
    wide = hidden.astype(f32)
    squares = jnp.sum(wide * wide, axis=1, keepdims=True)
    position = block_ref[0] * ROWS + lax.broadcasted_iota(jnp.int32, (ROWS, LANES), 0)
    starts = jnp.zeros((1, LANES), jnp.int32)
    ends = jnp.zeros((1, LANES), jnp.int32)
    lane_row = lane_of((1, LANES))
    end = jnp.int32(0)
    for r in range(REQS):
        starts = jnp.where(lane_row == r, end, starts)
        end = end + lengths_ref[r]
        ends = jnp.where(lane_row == r, end, ends)
    member = (position >= starts) & (position < ends)
    norm_ref[...] = jnp.sum(jnp.where(member, squares, 0.0), axis=0, keepdims=True)


def combine(block, lengths, mixed, mixed_last, got, routes, gates, gain):
    width = mixed.shape[1]
    vmem = pl.BlockSpec(memory_space=pltpu.VMEM)
    smem = pl.BlockSpec(memory_space=pltpu.SMEM)
    return pl.pallas_call(
        combine_kernel,
        in_specs=[smem, smem] + [vmem] * 6,
        out_specs=[vmem] * 3,
        out_shape=[
            jax.ShapeDtypeStruct((ROWS, width), bf16),
            jax.ShapeDtypeStruct((REQS, width), bf16),
            jax.ShapeDtypeStruct((1, LANES), f32),
        ],
        compiler_params=pltpu.CompilerParams(vmem_limit_bytes=16 << 20),
        name="combine",
    )(block, lengths, mixed, mixed_last, got, routes, gates, gain)


def exchange(rows):
    return lax.all_to_all(rows, "blk", split_axis=0, concat_axis=0, tiled=True)


def ring_pieces(piece):
    size = lax.axis_size("grp")

    def shift(one, by):
        return lax.ppermute(one, "grp", [(i, (i + by) % size) for i in range(size)])

    pieces = {0: piece}
    for by in (1, 2, -1):
        pieces[by % size] = shift(piece, by)
    pieces[6] = shift(pieces[7], -1)
    pieces[3] = shift(pieces[2], 1)
    pieces[4] = shift(pieces[2], 2)
    pieces[5] = shift(pieces[7], -2)
    return [pieces[k] for k in range(size)]


def local(
    tokens,
    lengths,
    owners,
    prefix_cache,
    routes,
    gates,
    attn_gain,
    w_query,
    w_keyval,
    w_out,
    moe_gain,
    w_gate,
    w_up,
    w_down,
    final_gain,
    unembed,
):
    blocks = lax.axis_size("blk")
    block_index = lax.axis_index("blk")
    width = tokens.shape[2]
    stream = tokens[0]
    block = block_index.astype(jnp.int32).reshape(1)
    quarter = block % QUARTERS
    swap = [(i, i ^ 1) for i in range(blocks)]
    with jax.named_scope("prefix_gather"):
        pieces = ring_pieces(prefix_cache[0])
        offset = (lax.axis_index("grp").astype(jnp.int32) - owners) % len(pieces)
    own = (w_gate[0].T, w_up[0].T, w_down[0])
    routes_t = routes[0].T
    gates_t = gates[0].T
    suffix_kv, send = project(
        block, lengths[0], stream, attn_gain.reshape(1, -1), w_query, w_keyval, routes_t, gates_t
    )
    with jax.named_scope("qkv_exchange"):
        got = exchange(send.reshape(blocks, SEND_ROWS, LANES))
    packed = prefix_pack(pieces, offset, got)
    with jax.named_scope("weight_swap"):
        packed, *ready = lax.optimization_barrier((packed, *own))
        other = [lax.ppermute(one, "blk", swap) for one in ready]
    with jax.named_scope("prefix_exchange"):
        prefix_got = exchange(packed.reshape(blocks, packed.shape[2], LANES))
    part = suffix_attention(quarter, lengths[0], got)
    part, *other = lax.optimization_barrier((part, *other))
    context = prefix_attention(quarter, lengths[0], got, prefix_got, part)
    with jax.named_scope("context_exchange"):
        ctx = exchange(context).reshape(HEADS, QUARTERS, 32, LANES)
    mixed, mixed_last, outgoing = mix(
        block, ctx, stream, prefix_got, got, w_out, moe_gain.reshape(1, -1), routes_t, own
    )
    with jax.named_scope("dispatch_exchange"):
        rows = exchange(outgoing.reshape(blocks, PART_ROWS, width))
    results = expert(rows.reshape(-1, width), own, other)
    with jax.named_scope("return_exchange"):
        returned = exchange(results.reshape(blocks, PART_ROWS, width)).reshape(-1, width)
    hidden, last_rows, norm_terms = combine(
        block, lengths[0], mixed, mixed_last, returned, routes_t, gates_t, final_gain.reshape(1, -1)
    )
    logits = jnp.dot(last_rows, unembed, preferred_element_type=f32)
    best = jnp.max(logits, axis=1)
    with jax.named_scope("final_exchange"):
        final = jnp.concatenate([norm_terms[:, :REQS], best[None, :]], axis=1)
        final = jnp.pad(final, ((0, 0), (0, LANES - 2 * REQS)))
        final = exchange(jnp.broadcast_to(final[None], (blocks, 1, LANES)))[:, 0, :]
    norm_sums = jnp.sum(final[:, :REQS], axis=0)
    greatest = jnp.max(final[:, REQS : 2 * REQS], axis=0)
    request_norm = jnp.sqrt(norm_sums / (lengths[0].astype(f32) * width))
    return (hidden[None], suffix_kv[None], request_norm[None], greatest[None])


def solution(mesh):
    placed = (
        P("grp", "blk", None),
        P("grp", None),
        P("grp"),
        P("grp", "blk", None),
        P("grp", "blk", None),
        P("grp", "blk", None),
        P(),
        P(),
        P(),
        P(),
        P(),
        P("blk", None, None),
        P("blk", None, None),
        P("blk", None, None),
        P(),
        P(None, "blk"),
    )
    return jax.shard_map(
        local,
        mesh=mesh,
        in_specs=placed,
        out_specs=(P("grp", "blk", None), P("grp", "blk", None), P("grp", None), P("grp", None)),
        check_vma=False,
    )
```

```python
import jax
import jax.numpy as jnp
from jax import lax
from jax.experimental import pallas as pl
from jax.experimental.pallas import tpu as pltpu
from jax.sharding import PartitionSpec as P

HEADS = 8
EXPERTS = 8
QUARTERS = 4
CAP = 40
SLOT_ROWS = 48
PART_ROWS = 24
PART_SLOTS = 20
SEND_ROWS = 176
PAIRS = 2
REQS = 16
ROWS = 128
HALF = 64
LANES = 128
KEY_TILE = 1024
QUERY_TILE = 256
PREFIX_TILE = 1024
PREFIX_SUB = 128

epsilon = 1e-06
neg_big = -1e30
bf16 = jnp.bfloat16
f32 = jnp.float32


def rms_scale(values, gain_vector):
    return (
        values * lax.rsqrt(jnp.mean(values * values, axis=-1, keepdims=True) + epsilon) * gain_vector
    )


def lane_of(shape):
    return lax.broadcasted_iota(jnp.int32, shape, len(shape) - 1)


def head_split(first, second):
    low = lane_of(first.shape) < HALF
    axis = len(first.shape) - 1
    even = jnp.where(low, first, pltpu.roll(second, HALF, axis))
    odd = jnp.where(low, pltpu.roll(first, HALF, axis), second)
    return even, odd


def last_matrix(lengths_ref, positions):
    request = lax.broadcasted_iota(jnp.int32, positions.shape, 0)
    lasts = jnp.full(positions.shape, -1, jnp.int32)
    end = jnp.int32(0)
    for r in range(REQS):
        end = end + lengths_ref[r]
        lasts = jnp.where(request == r, end - 1, lasts)
    return (lasts == positions).astype(f32).astype(bf16)


def three_parts(values):
    high = values.astype(bf16).astype(f32)
    middle = (values - high).astype(bf16).astype(f32)
    low = (values - high - middle).astype(bf16).astype(f32)
    return high, middle, low


def in_hbm(*arrays):
    return tuple(pltpu.with_memory_space_constraint(one, pltpu.HBM) for one in arrays)


def project_kernel(
    block_ref, lengths_ref, tok_ref, gain_ref, wq_ref, wk_ref, wv_ref, routes_ref, gates_ref,
    kv_ref, send_ref, normed_ref, gate_ref,
):
    step = pl.program_id(0)
    is_last = last_matrix(lengths_ref, block_ref[0] * ROWS + lane_of((REQS, ROWS)))

    @pl.when(step == 0)
    def _():
        normed_ref[...] = rms_scale(tok_ref[...].astype(f32), gain_ref[...]).astype(bf16)
        row = lax.broadcasted_iota(jnp.int32, (LANES, ROWS), 0)
        named = row % EXPERTS
        weight = jnp.where(
            routes_ref[0:1, :] == named,
            gates_ref[0:1, :],
            jnp.where(routes_ref[1:2, :] == named, gates_ref[1:2, :], 0.0),
        )
        high, middle, low = three_parts(weight)
        piece = row // EXPERTS
        pieces = jnp.where(
            piece == 0, high, jnp.where(piece == 1, middle, jnp.where(piece == 2, low, 0.0))
        )
        gate_ref[...] = lax.dot_general(
            is_last, pieces.astype(bf16), (((1,), (1,)), ((), ())), preferred_element_type=f32
        ).astype(bf16)

    normed = normed_ref[...]
    query = jnp.dot(normed, wq_ref[...], preferred_element_type=f32).astype(bf16)
    key = jnp.dot(normed, wk_ref[...], preferred_element_type=f32).astype(bf16)
    value = jnp.dot(normed, wv_ref[...], preferred_element_type=f32).astype(bf16)
    column = pl.multiple_of(step * PAIRS * LANES, PAIRS * LANES)
    kv_ref[:, pl.ds(column, PAIRS * LANES)] = key
    kv_ref[:, pl.ds(HEADS * HALF + column, PAIRS * LANES)] = value
    wide = pl.multiple_of(step * 2 * PAIRS * LANES, 2 * PAIRS * LANES)
    ends = jnp.dot(
        is_last, tok_ref[:, pl.ds(wide, 2 * PAIRS * LANES)], preferred_element_type=f32
    ).astype(bf16)
    scaled = query.astype(f32) * (HALF**-0.5)
    for pair in range(PAIRS):
        lanes = slice(pair * LANES, (pair + 1) * LANES)
        even, odd = head_split(key[:, lanes].astype(f32), value[:, lanes].astype(f32))
        even = even.astype(bf16)
        odd = odd.astype(bf16)
        for quarter in range(QUARTERS):
            first = scaled[quarter * 32 : quarter * 32 + 16, lanes]
            second = scaled[quarter * 32 + 16 : quarter * 32 + 32, lanes]
            query_even, query_odd = head_split(first, second)
            send_ref[2 * pair, quarter, 0:ROWS, :] = even
            send_ref[2 * pair + 1, quarter, 0:ROWS, :] = odd
            send_ref[2 * pair, quarter, ROWS : ROWS + 16, :] = query_even.astype(bf16)
            send_ref[2 * pair + 1, quarter, ROWS : ROWS + 16, :] = query_odd.astype(bf16)
            for which in range(2 * pair, 2 * pair + 2):
                send_ref[which, quarter, ROWS + 16 : ROWS + 32, :] = ends[
                    :, which * LANES : (which + 1) * LANES
                ]
                send_ref[which, quarter, ROWS + 32 : ROWS + 48, :] = gate_ref[...]


def project(block, lengths, stream, gain, w_query, w_keyval, routes_t, gates_t):
    width = stream.shape[1]
    return pl.pallas_call(
        project_kernel,
        grid_spec=pltpu.PrefetchScalarGridSpec(
            num_scalar_prefetch=2,
            grid=(HEADS // 2 // PAIRS,),
            in_specs=[
                pl.BlockSpec((ROWS, width), lambda i, b, l: (0, 0)),
                pl.BlockSpec((1, width), lambda i, b, l: (0, 0)),
                pl.BlockSpec((width, PAIRS * LANES), lambda i, b, l: (0, i)),
                pl.BlockSpec((width, PAIRS * LANES), lambda i, b, l: (0, i)),
                pl.BlockSpec((width, PAIRS * LANES), lambda i, b, l: (0, i + HEADS // 2 // PAIRS)),
                pl.BlockSpec((2, ROWS), lambda i, b, l: (0, 0)),
                pl.BlockSpec((2, ROWS), lambda i, b, l: (0, 0)),
            ],
            out_specs=[
                pl.BlockSpec((ROWS, 2 * HEADS * HALF), lambda i, b, l: (0, 0)),
                pl.BlockSpec((2 * PAIRS, QUARTERS, SEND_ROWS, LANES), lambda i, b, l: (i, 0, 0, 0)),
            ],
            scratch_shapes=[pltpu.VMEM((ROWS, width), bf16), pltpu.VMEM((REQS, LANES), bf16)],
        ),
        out_shape=[
            jax.ShapeDtypeStruct((ROWS, 2 * HEADS * HALF), bf16),
            jax.ShapeDtypeStruct((HEADS, QUARTERS, SEND_ROWS, LANES), bf16),
        ],
        compiler_params=pltpu.CompilerParams(vmem_limit_bytes=24 << 20),
        name="project",
    )(block, lengths, *in_hbm(stream, gain, w_query, w_keyval, w_keyval, routes_t, gates_t))


def prefix_pack_kernel(offset_ref, got_ref, *refs):
    pieces = refs[: len(refs) - 5]
    out_ref, prefix_v, ends_v, sem, ends_sem = refs[len(refs) - 5 :]
    ends_copy = pltpu.make_async_copy(
        got_ref.at[:, pl.ds(ROWS + 16, REQS), :], ends_v, ends_sem
    )
    ends_copy.start()
    for k, piece in enumerate(pieces):

        @pl.when(offset_ref[0] == k)
        def _():
            copy = pltpu.make_async_copy(piece, prefix_v, sem)
            copy.start()
            copy.wait()

    rows = prefix_v.shape[0]
    ends_copy.wait()
    ends = jnp.sum(ends_v[...].astype(f32), axis=0).astype(bf16)
    for head in range(HEADS):
        for quarter in range(QUARTERS):
            out_ref[head, quarter, rows : rows + REQS, :] = ends
    for pair in range(HEADS // 2):
        key = prefix_v[:, pair * LANES : (pair + 1) * LANES].astype(f32)
        base = HEADS * HALF + pair * LANES
        value = prefix_v[:, base : base + LANES].astype(f32)
        even, odd = head_split(key, value)
        for quarter in range(QUARTERS):
            out_ref[2 * pair, quarter, 0:rows, :] = even.astype(bf16)
            out_ref[2 * pair + 1, quarter, 0:rows, :] = odd.astype(bf16)


def prefix_pack(pieces, offset, got):
    rows, width = pieces[0].shape
    return pl.pallas_call(
        prefix_pack_kernel,
        grid_spec=pltpu.PrefetchScalarGridSpec(
            num_scalar_prefetch=1,
            grid=(1,),
            in_specs=[pl.BlockSpec(memory_space=pl.ANY)] * (1 + len(pieces)),
            out_specs=pl.BlockSpec(
                (HEADS, QUARTERS, rows + REQS, LANES), lambda i, owner: (0, 0, 0, 0)
            ),
            scratch_shapes=[
                pltpu.VMEM((rows, width), bf16),
                pltpu.VMEM((got.shape[0], REQS, LANES), bf16),
                pltpu.SemaphoreType.DMA(()),
                pltpu.SemaphoreType.DMA(()),
            ],
        ),
        out_shape=jax.ShapeDtypeStruct((HEADS, QUARTERS, rows + REQS, LANES), bf16),
        name="prefix_pack",
    )(offset, *in_hbm(got, *pieces))


def query_tile(query_ref):
    packed = query_ref[...].reshape(QUERY_TILE // 2, LANES).astype(f32)
    low = lane_of(packed.shape) < HALF
    first = jnp.where(low, packed, 0.0)
    second = jnp.where(low, pltpu.roll(packed, HALF, 1), 0.0)
    return jnp.concatenate([first, second], axis=0).astype(bf16)


def offset_of(row):
    half_rows = QUERY_TILE // 2
    second = (row >= half_rows).astype(jnp.int32)
    within = row - second * half_rows
    return (within // 16) * ROWS + second * 16 + within % 16


def start_of(position, lengths_ref, zero):
    end = jnp.int32(0)
    start = zero
    for request in range(REQS):
        end = end + lengths_ref[request]
        start = jnp.where(position >= end, end, start)
    return start


def suffix_kernel(quarter_ref, lengths_ref, query_ref, got_ref, out_ref):
    tile = pl.program_id(0)
    blocks = QUERY_TILE // 32
    key_blocks = KEY_TILE // ROWS
    query = query_tile(query_ref)
    first_position = tile * blocks * ROWS + quarter_ref[0] * 32
    position = first_position + offset_of(lax.broadcasted_iota(jnp.int32, (QUERY_TILE, 1), 0))
    start = start_of(position, lengths_ref, jnp.zeros_like(position))
    lowest = start_of(first_position, lengths_ref, jnp.int32(0))
    span = blocks * ROWS
    last_tile = (tile * span + span - 1) // KEY_TILE

    def step(j, carry):
        acc, top, total = carry
        keys = got_ref[pl.ds(j * key_blocks, key_blocks), :, :].reshape(KEY_TILE, LANES)
        scores = lax.dot_general(
            query, keys, (((1,), (1,)), ((), ())), preferred_element_type=f32
        )
        key_position = j * KEY_TILE + lane_of(scores.shape)
        allowed = (key_position >= start) & (key_position <= position)
        scores = jnp.where(allowed, scores, neg_big)
        new_top = jnp.maximum(top, jnp.max(scores, axis=1, keepdims=True))
        shrink = jnp.exp(top - new_top)
        probs = jnp.exp(scores - new_top)
        total = total * shrink + jnp.sum(probs, axis=1, keepdims=True)
        acc = acc * shrink + jnp.dot(probs.astype(bf16), keys, preferred_element_type=f32)
        return acc, new_top, total

    acc, top, total = lax.fori_loop(
        lowest // KEY_TILE,
        last_tile + 1,
        step,
        (
            jnp.zeros((QUERY_TILE, LANES), f32),
            jnp.full((QUERY_TILE, 1), neg_big, f32),
            jnp.zeros((QUERY_TILE, 1), f32),
        ),
    )
    lane = lane_of(acc.shape)
    out_ref[...] = jnp.where(lane == 0, top, jnp.where(lane == 1, total, acc))


def suffix_attention(quarter, lengths, got):
    blocks = got.shape[0]
    queries = blocks * 32
    return pl.pallas_call(
        suffix_kernel,
        grid_spec=pltpu.PrefetchScalarGridSpec(
            num_scalar_prefetch=2,
            grid=(queries // QUERY_TILE,),
            in_specs=[
                pl.BlockSpec((QUERY_TILE // 32, 16, LANES), lambda i, q, l: (i, ROWS // 16, 0)),
                pl.BlockSpec((blocks, ROWS, LANES), lambda i, q, l: (0, 0, 0)),
            ],
            out_specs=pl.BlockSpec((QUERY_TILE, LANES), lambda i, q, l: (i, 0)),
        ),
        out_shape=pltpu.HBM((queries, LANES), f32),
        compiler_params=pltpu.CompilerParams(vmem_limit_bytes=14 << 20),
        name="suffix_attention",
    )(quarter, lengths, *in_hbm(got, got))


def prefix_kernel(quarter_ref, lengths_ref, query_ref, keys_ref, part_ref, out_ref, last_ref):
    tile = pl.program_id(0)
    tile_blocks = PREFIX_TILE // 32
    half_rows = PREFIX_TILE // 2
    packed = query_ref[...].reshape(half_rows, LANES).astype(f32)
    low = lane_of(packed.shape) < HALF
    query = jnp.concatenate(
        [jnp.where(low, packed, 0.0), jnp.where(low, pltpu.roll(packed, HALF, 1), 0.0)], axis=0
    ).astype(bf16)
    keys = keys_ref[...].reshape(-1, LANES)
    subs = PREFIX_TILE // PREFIX_SUB

    def score(sub):
        rows = slice(sub * PREFIX_SUB, (sub + 1) * PREFIX_SUB)
        return lax.dot_general(
            query[rows], keys, (((1,), (1,)), ((), ())), preferred_element_type=f32
        )

    def part_rows(sub):
        pieces = []
        per = QUERY_TILE // 2
        for start in range(sub * PREFIX_SUB, (sub + 1) * PREFIX_SUB, min(per, PREFIX_SUB)):
            second, rest = divmod(start, half_rows)
            group, inside = divmod(rest, per)
            first = group * QUERY_TILE + second * per + inside
            pieces.append(part_ref[first : first + min(per, PREFIX_SUB), :])
        return pieces[0] if len(pieces) == 1 else jnp.concatenate(pieces, axis=0)

    contexts = []
    scores = score(0)
    for sub in range(subs):
        following = score(sub + 1) if sub + 1 < subs else None
        part = part_rows(sub)
        part_top = part[:, 0:1]
        part_total = part[:, 1:2]
        top = jnp.maximum(part_top, jnp.max(scores, axis=1, keepdims=True))
        probs = jnp.exp(scores - top)
        shrink = jnp.exp(part_top - top)
        total = part_total * shrink + jnp.sum(probs, axis=1, keepdims=True)
        acc = part * shrink + jnp.dot(probs.astype(bf16), keys, preferred_element_type=f32)
        contexts.append(acc / total)
        scores = following
    context = contexts[0] if subs == 1 else jnp.concatenate(contexts, axis=0)
    packed = jnp.where(low, pltpu.roll(context[:half_rows], HALF, 1), context[half_rows:])
    out_ref[pl.ds(tile * tile_blocks, tile_blocks), 0:16, :] = packed.astype(bf16).reshape(
        tile_blocks, 16, LANES
    )
    row = lane_of((REQS, PREFIX_TILE))
    second = (row >= half_rows).astype(jnp.int32)
    within = row - second * half_rows
    positions = tile * tile_blocks * ROWS + quarter_ref[0] * 32
    positions = positions + (within // 16) * ROWS + second * 16 + within % 16
    is_last = last_matrix(lengths_ref, positions)
    ends = jnp.where(lane_of(context.shape) < HALF, 0.0, context).astype(bf16)
    ends = jnp.dot(is_last, ends, preferred_element_type=f32)

    @pl.when(tile == 0)
    def _():
        last_ref[...] = ends

    @pl.when(tile > 0)
    def _():
        last_ref[...] = last_ref[...] + ends

    @pl.when(tile == pl.num_programs(0) - 1)
    def _():
        every = last_ref[...].astype(bf16)
        for block in range(out_ref.shape[0]):
            out_ref[block, 16:32, :] = every


def prefix_attention(quarter, lengths, got, keys, part):
    blocks = got.shape[0]
    queries = blocks * 32
    rows = keys.shape[1] - REQS
    return pl.pallas_call(
        prefix_kernel,
        grid_spec=pltpu.PrefetchScalarGridSpec(
            num_scalar_prefetch=2,
            grid=(queries // PREFIX_TILE,),
            in_specs=[
                pl.BlockSpec((PREFIX_TILE // 32, 16, LANES), lambda i, q, l: (i, ROWS // 16, 0)),
                pl.BlockSpec((blocks, rows, LANES), lambda i, q, l: (0, 0, 0)),
                pl.BlockSpec((PREFIX_TILE, LANES), lambda i, q, l: (i, 0)),
            ],
            out_specs=pl.BlockSpec((blocks, 32, LANES), lambda i, q, l: (0, 0, 0)),
            scratch_shapes=[pltpu.VMEM((REQS, LANES), f32)],
        ),
        out_shape=jax.ShapeDtypeStruct((blocks, 32, LANES), bf16),
        compiler_params=pltpu.CompilerParams(vmem_limit_bytes=18 << 20),
        name="prefix_attention",
    )(quarter, lengths, *in_hbm(got, keys, part))


def gelu(v):
    scale = 0.7978845608028654
    half = 0.5 * v
    return half + half * jnp.tanh(v * (scale + (scale * 0.044715) * (v * v)))


def dot_nt(a, b):
    return lax.dot_general(a, b, (((1,), (1,)), ((), ())), preferred_element_type=f32)


def mix_kernel(
    block_ref, ctx_ref, tok_ref, tok_last_ref, gate_last_ref, wout_ref, gain_ref, routes_ref, g_ref, u_ref, d_ref,
    mixed_ref, mixed_last_ref, send_ref, send_v, out_sems,
):
    tiles = []
    for pair in range(HEADS // 2):
        even = ctx_ref[2 * pair].astype(f32)
        odd = ctx_ref[2 * pair + 1].astype(f32)
        first, second = head_split(even[:, 0:16], odd[:, 0:16])
        both = jnp.stack([first, second], axis=1).reshape(ROWS, LANES)
        even_last = jnp.sum(even[:, 16:32], axis=0)
        odd_last = jnp.sum(odd[:, 16:32], axis=0)
        low = lane_of(even_last.shape) < HALF
        ends = jnp.where(low, pltpu.roll(even_last, HALF, 1), odd_last)
        tiles.append(jnp.concatenate([both, ends], axis=0).astype(bf16))
    context = jnp.concatenate(tiles, axis=1)
    lift = jnp.dot(context, wout_ref[...], preferred_element_type=f32)
    mixed = tok_ref[...].astype(f32) + lift[:ROWS]
    mixed_ref[...] = mixed
    routed = rms_scale(mixed, gain_ref[...]).astype(bf16)
    tok_last = jnp.concatenate([tok_last_ref[QUARTERS * j] for j in range(8)], axis=1)
    mixed_last = tok_last.astype(f32) + lift[ROWS:]
    mixed_last_ref[...] = mixed_last
    routed_last = rms_scale(mixed_last, gain_ref[...]).astype(bf16)
    expert_id = block_ref[0] // QUARTERS
    weights = jnp.sum(gate_last_ref[...].astype(f32), axis=0)
    lane = lane_of(weights.shape)
    mine = (lane % EXPERTS == expert_id) & (lane < 3 * EXPERTS)
    weight = jnp.sum(jnp.where(mine, weights, 0.0), axis=1, keepdims=True)
    act = (gelu(dot_nt(routed_last, g_ref[...])) * dot_nt(routed_last, u_ref[...])).astype(bf16)
    partial_last = weight * jnp.dot(act, d_ref[...], preferred_element_type=f32)
    high = partial_last.astype(bf16)
    low_part = (partial_last - high.astype(f32)).astype(bf16)
    source = jnp.concatenate([routed, high, low_part], axis=0)
    expert = lax.broadcasted_iota(jnp.int32, (EXPERTS, ROWS), 0)
    named = (routes_ref[0:1, :] == expert) | (routes_ref[1:2, :] == expert)
    earlier = (
        lax.broadcasted_iota(jnp.int32, (ROWS, ROWS), 0)
        < lax.broadcasted_iota(jnp.int32, (ROWS, ROWS), 1)
    ).astype(bf16)
    slots = jnp.dot(named.astype(f32).astype(bf16), earlier, preferred_element_type=f32)
    slots = jnp.where(named, slots, -1.0).astype(jnp.int32)
    place = slots + jnp.where(slots >= PART_SLOTS, PART_ROWS - PART_SLOTS, 0)
    place_id = lax.broadcasted_iota(jnp.int32, (SLOT_ROWS, ROWS), 0)
    extra_row = lax.broadcasted_iota(jnp.int32, (SLOT_ROWS, 2 * REQS), 0) % PART_ROWS
    extra_column = lane_of((SLOT_ROWS, 2 * REQS))
    picks = []
    for e in range(EXPERTS):
        pick = (place[e : e + 1, :] == place_id).astype(f32)
        for chip in range(2):
            row_last = 2 * e + chip
            extra = ((extra_row == PART_SLOTS) & (extra_column == row_last)) | (
                (extra_row == PART_SLOTS + 1) & (extra_column == REQS + row_last)
            )
            picks.append(jnp.concatenate([pick, extra.astype(f32)], axis=1).astype(bf16))
    sends = []
    per = len(picks) // MIX_PARTS
    rows = per * SLOT_ROWS
    for part in range(MIX_PARTS):
        chosen = jnp.concatenate(picks[part * per : (part + 1) * per], axis=0)
        send_v[part] = jnp.dot(chosen, source, preferred_element_type=f32).astype(bf16)
        send = pltpu.make_async_copy(
            send_v.at[part], send_ref.at[pl.ds(part * rows, rows), :], out_sems.at[part]
        )
        send.start()
        sends.append(send)
    for send in sends:
        send.wait()


MIX_PARTS = 2


def mix(block, ctx, stream, prefix_got, got, w_out, gain, routes_t, own):
    width = stream.shape[1]
    blocks = got.shape[0]
    units = own[0].shape[0]
    def whole(shape):
        return pl.BlockSpec(shape, lambda i, b: (0,) * len(shape))

    return pl.pallas_call(
        mix_kernel,
        grid_spec=pltpu.PrefetchScalarGridSpec(
            num_scalar_prefetch=1,
            grid=(1,),
            in_specs=[
                whole(ctx.shape),
                whole(stream.shape),
                pl.BlockSpec((blocks, REQS, LANES), lambda i, b: (0, 4, 0)),
                pl.BlockSpec((blocks, REQS, LANES), lambda i, b: (0, 10, 0)),
                whole(w_out.shape),
                whole(gain.shape),
                whole(routes_t.shape),
                whole((units, width)),
                whole((units, width)),
                whole((units, width)),
            ],
            out_specs=[
                whole((ROWS, width)),
                whole((REQS, width)),
                pl.BlockSpec(memory_space=pltpu.HBM),
            ],
            scratch_shapes=[
                pltpu.VMEM((MIX_PARTS, 2 * EXPERTS * SLOT_ROWS // MIX_PARTS, width), bf16),
                pltpu.SemaphoreType.DMA((MIX_PARTS,)),
            ],
        ),
        out_shape=[
            pltpu.HBM((ROWS, width), f32),
            pltpu.HBM((REQS, width), f32),
            pltpu.HBM((2 * EXPERTS * SLOT_ROWS, width), bf16),
        ],
        compiler_params=pltpu.CompilerParams(vmem_limit_bytes=18 << 20),
        name="mix",
    )(block, ctx, stream, *in_hbm(prefix_got, got), w_out, gain, routes_t, *own)


FFN_TILE = 256


def expert_kernel(
    x_ref, g0, u0, d0, g1, u1, d1, out_ref, acc_v, out_v, out_sems
):
    weights = ((g0, u0, d0), (g1, u1, d1))
    count = x_ref.shape[0]
    within = lane_of((16, count)) % PART_ROWS
    extra = ((within == PART_SLOTS) | (within == PART_SLOTS + 1)).astype(f32).astype(bf16)
    total = jnp.dot(extra, x_ref[...], preferred_element_type=f32)[0:1]
    high = total.astype(bf16).astype(f32)
    low = (total - high).astype(bf16).astype(f32)
    sends = []
    tiles = count // FFN_TILE
    work = [(part, tile) for part in range(2) for tile in range(tiles)]

    def span(tile):
        return slice(tile * FFN_TILE, (tile + 1) * FFN_TILE)

    def lift(part, tile):
        x = x_ref[span(tile), :]
        return dot_nt(x, weights[part][0][...]), dot_nt(x, weights[part][1][...])

    ready = lift(*work[0])
    for index, (part, tile) in enumerate(work):
        gate, up = ready
        if index + 1 < len(work):
            ready = lift(*work[index + 1])
        hidden = (gelu(gate) * up).astype(bf16)
        down = jnp.dot(hidden, weights[part][2][...], preferred_element_type=f32)
        if part == 0:
            acc_v[span(tile), :] = down
        else:
            row = tile * FFN_TILE + lax.broadcasted_iota(jnp.int32, (FFN_TILE, 1), 0)
            row = row % PART_ROWS
            result = acc_v[span(tile), :] + down
            result = jnp.where(row == PART_SLOTS, high, result)
            result = jnp.where(row == PART_SLOTS + 1, low, result)
            out_v[span(tile), :] = result.astype(bf16)
            send = pltpu.make_async_copy(
                out_v.at[pl.ds(tile * FFN_TILE, FFN_TILE), :],
                out_ref.at[pl.ds(tile * FFN_TILE, FFN_TILE), :],
                out_sems.at[tile],
            )
            send.start()
            sends.append(send)
    for send in sends:
        send.wait()


def expert(rows, own, other):
    count, width = rows.shape
    vmem = pl.BlockSpec(memory_space=pltpu.VMEM)
    return pl.pallas_call(
        expert_kernel,
        in_specs=[vmem] * 7,
        out_specs=pl.BlockSpec(memory_space=pltpu.HBM),
        out_shape=pltpu.HBM((count, width), bf16),
        scratch_shapes=[
            pltpu.VMEM((count, width), f32),
            pltpu.VMEM((count, width), bf16),
            pltpu.SemaphoreType.DMA((count // FFN_TILE,)),
        ],
        compiler_params=pltpu.CompilerParams(vmem_limit_bytes=26 << 20),
        name="expert",
    )(rows, *own, *other)


def column_of(row):
    return jnp.transpose(jnp.broadcast_to(row, (ROWS, LANES)))


def combine_kernel(
    block_ref, lengths_ref, mixed_ref, mixed_last_ref, got_ref, routes_ref, gates_ref, gain_ref,
    hidden_ref, last_ref, norm_ref,
):
    got = got_ref[...]
    count = got.shape[0]
    request_row = lax.broadcasted_iota(jnp.int32, (REQS, count), 0)
    wanted = request_row * (2 * PART_ROWS) + PART_SLOTS
    source = lane_of((REQS, count))
    pick_last = ((source == wanted) | (source == wanted + 1)).astype(f32).astype(bf16)
    first = column_of(routes_ref[0:1, :].astype(f32)).astype(jnp.int32)
    second = column_of(routes_ref[1:2, :].astype(f32)).astype(jnp.int32)
    lane = lane_of((ROWS, LANES))
    named = ((first == lane) | (second == lane)).astype(f32).astype(bf16)
    earlier = (
        lax.broadcasted_iota(jnp.int32, (ROWS, ROWS), 1)
        < lax.broadcasted_iota(jnp.int32, (ROWS, ROWS), 0)
    ).astype(bf16)
    slots = jnp.dot(earlier, named, preferred_element_type=f32)
    column = lane_of((ROWS, count))
    picks = [pick_last]
    for chosen in (first, second):
        slot = jnp.sum(jnp.where(chosen == lane, slots, 0.0), axis=1, keepdims=True)
        slot = slot.astype(jnp.int32)
        place = slot + jnp.where(slot >= PART_SLOTS, PART_ROWS - PART_SLOTS, 0)
        target = chosen[:, 0:1] * (2 * SLOT_ROWS) + place
        pick = ((column == target) | (column == target + SLOT_ROWS)).astype(f32).astype(bf16)
        picks.append(pick)
    picked = jnp.dot(jnp.concatenate(picks, axis=0), got, preferred_element_type=f32)
    hidden_last = (mixed_last_ref[...] + picked[:REQS]).astype(bf16).astype(f32)
    last_ref[...] = rms_scale(hidden_last, gain_ref[...]).astype(bf16)
    moe = column_of(gates_ref[0:1, :])[:, 0:1] * picked[REQS : REQS + ROWS]
    moe = moe + column_of(gates_ref[1:2, :])[:, 0:1] * picked[REQS + ROWS :]
    hidden = (mixed_ref[...] + moe).astype(bf16)
    hidden_ref[...] = hidden
    wide = hidden.astype(f32)
    squares = jnp.sum(wide * wide, axis=1, keepdims=True)
    position = block_ref[0] * ROWS + lax.broadcasted_iota(jnp.int32, (ROWS, LANES), 0)
    starts = jnp.zeros((1, LANES), jnp.int32)
    ends = jnp.zeros((1, LANES), jnp.int32)
    lane_row = lane_of((1, LANES))
    end = jnp.int32(0)
    for r in range(REQS):
        starts = jnp.where(lane_row == r, end, starts)
        end = end + lengths_ref[r]
        ends = jnp.where(lane_row == r, end, ends)
    member = (position >= starts) & (position < ends)
    norm_ref[...] = jnp.sum(jnp.where(member, squares, 0.0), axis=0, keepdims=True)


def combine(block, lengths, mixed, mixed_last, got, routes, gates, gain):
    width = mixed.shape[1]
    vmem = pl.BlockSpec(memory_space=pltpu.VMEM)
    smem = pl.BlockSpec(memory_space=pltpu.SMEM)
    return pl.pallas_call(
        combine_kernel,
        in_specs=[smem, smem] + [vmem] * 6,
        out_specs=[vmem] * 3,
        out_shape=[
            jax.ShapeDtypeStruct((ROWS, width), bf16),
            jax.ShapeDtypeStruct((REQS, width), bf16),
            jax.ShapeDtypeStruct((1, LANES), f32),
        ],
        compiler_params=pltpu.CompilerParams(vmem_limit_bytes=16 << 20),
        name="combine",
    )(block, lengths, mixed, mixed_last, got, routes, gates, gain)


def exchange(rows):
    return lax.all_to_all(rows, "blk", split_axis=0, concat_axis=0, tiled=True)


def ring_pieces(piece):
    size = lax.axis_size("grp")

    def shift(one, by):
        return lax.ppermute(one, "grp", [(i, (i + by) % size) for i in range(size)])

    pieces = {0: piece}
    for by in (1, 2, -1):
        pieces[by % size] = shift(piece, by)
    pieces[6] = shift(pieces[7], -1)
    pieces[3] = shift(pieces[2], 1)
    pieces[4] = shift(pieces[2], 2)
    pieces[5] = shift(pieces[7], -2)
    return [pieces[k] for k in range(size)]


def local(
    tokens,
    lengths,
    owners,
    prefix_cache,
    routes,
    gates,
    attn_gain,
    w_query,
    w_keyval,
    w_out,
    moe_gain,
    w_gate,
    w_up,
    w_down,
    final_gain,
    unembed,
):
    blocks = lax.axis_size("blk")
    block_index = lax.axis_index("blk")
    width = tokens.shape[2]
    stream = tokens[0]
    block = block_index.astype(jnp.int32).reshape(1)
    quarter = block % QUARTERS
    swap = [(i, i ^ 1) for i in range(blocks)]
    with jax.named_scope("prefix_gather"):
        pieces = ring_pieces(prefix_cache[0])
        offset = (lax.axis_index("grp").astype(jnp.int32) - owners) % len(pieces)
    own = (w_gate[0].T, w_up[0].T, w_down[0])
    routes_t = routes[0].T
    gates_t = gates[0].T
    suffix_kv, send = project(
        block, lengths[0], stream, attn_gain.reshape(1, -1), w_query, w_keyval, routes_t, gates_t
    )
    with jax.named_scope("qkv_exchange"):
        got = exchange(send.reshape(blocks, SEND_ROWS, LANES))
    packed = prefix_pack(pieces, offset, got)
    with jax.named_scope("weight_swap"):
        packed, *ready = lax.optimization_barrier((packed, *own))
        other = [lax.ppermute(one, "blk", swap) for one in ready]
    with jax.named_scope("prefix_exchange"):
        prefix_got = exchange(packed.reshape(blocks, packed.shape[2], LANES))
    part = suffix_attention(quarter, lengths[0], got)
    part, *other = lax.optimization_barrier((part, *other))
    context = prefix_attention(quarter, lengths[0], got, prefix_got, part)
    with jax.named_scope("context_exchange"):
        ctx = exchange(context).reshape(HEADS, QUARTERS, 32, LANES)
    mixed, mixed_last, outgoing = mix(
        block, ctx, stream, prefix_got, got, w_out, moe_gain.reshape(1, -1), routes_t, own
    )
    with jax.named_scope("dispatch_exchange"):
        rows = exchange(outgoing.reshape(blocks, PART_ROWS, width))
    results = expert(rows.reshape(-1, width), own, other)
    with jax.named_scope("return_exchange"):
        returned = exchange(results.reshape(blocks, PART_ROWS, width)).reshape(-1, width)
    hidden, last_rows, norm_terms = combine(
        block, lengths[0], mixed, mixed_last, returned, routes_t, gates_t, final_gain.reshape(1, -1)
    )
    logits = jnp.dot(last_rows, unembed, preferred_element_type=f32)
    best = jnp.max(logits, axis=1)
    with jax.named_scope("final_exchange"):
        final = jnp.concatenate([norm_terms[:, :REQS], best[None, :]], axis=1)
        final = jnp.pad(final, ((0, 0), (0, LANES - 2 * REQS)))
        final = exchange(jnp.broadcast_to(final[None], (blocks, 1, LANES)))[:, 0, :]
    norm_sums = jnp.sum(final[:, :REQS], axis=0)
    greatest = jnp.max(final[:, REQS : 2 * REQS], axis=0)
    request_norm = jnp.sqrt(norm_sums / (lengths[0].astype(f32) * width))
    return (hidden[None], suffix_kv[None], request_norm[None], greatest[None])


def solution(mesh):
    placed = (
        P("grp", "blk", None),
        P("grp", None),
        P("grp"),
        P("grp", "blk", None),
        P("grp", "blk", None),
        P("grp", "blk", None),
        P(),
        P(),
        P(),
        P(),
        P(),
        P("blk", None, None),
        P("blk", None, None),
        P("blk", None, None),
        P(),
        P(None, "blk"),
    )
    return jax.shard_map(
        local,
        mesh=mesh,
        in_specs=placed,
        out_specs=(P("grp", "blk", None), P("grp", "blk", None), P("grp", None), P("grp", None)),
        check_vma=False,
    )
```

```python
import jax
import jax.numpy as jnp
from jax import lax
from jax.experimental import pallas as pl
from jax.experimental.pallas import tpu as pltpu
from jax.sharding import PartitionSpec as P

HEADS = 8
EXPERTS = 8
QUARTERS = 4
CAP = 40
SLOT_ROWS = 48
PART_ROWS = 24
PART_SLOTS = 20
SEND_ROWS = 176
PAIRS = 2
REQS = 16
ROWS = 128
HALF = 64
LANES = 128
KEY_TILE = 1024
QUERY_TILE = 256
PREFIX_TILE = 1024
PREFIX_SUB = 128

epsilon = 1e-06
neg_big = -1e30
bf16 = jnp.bfloat16
f32 = jnp.float32


def rms_scale(values, gain_vector):
    return (
        values * lax.rsqrt(jnp.mean(values * values, axis=-1, keepdims=True) + epsilon) * gain_vector
    )


def lane_of(shape):
    return lax.broadcasted_iota(jnp.int32, shape, len(shape) - 1)


def head_split(first, second):
    low = lane_of(first.shape) < HALF
    axis = len(first.shape) - 1
    even = jnp.where(low, first, pltpu.roll(second, HALF, axis))
    odd = jnp.where(low, pltpu.roll(first, HALF, axis), second)
    return even, odd


def last_matrix(lengths_ref, positions):
    request = lax.broadcasted_iota(jnp.int32, positions.shape, 0)
    lasts = jnp.full(positions.shape, -1, jnp.int32)
    end = jnp.int32(0)
    for r in range(REQS):
        end = end + lengths_ref[r]
        lasts = jnp.where(request == r, end - 1, lasts)
    return (lasts == positions).astype(f32).astype(bf16)


def three_parts(values):
    high = values.astype(bf16).astype(f32)
    middle = (values - high).astype(bf16).astype(f32)
    low = (values - high - middle).astype(bf16).astype(f32)
    return high, middle, low


def in_hbm(*arrays):
    return tuple(pltpu.with_memory_space_constraint(one, pltpu.HBM) for one in arrays)


def project_kernel(
    block_ref, lengths_ref, tok_ref, gain_ref, wq_ref, wk_ref, wv_ref, routes_ref, gates_ref,
    kv_ref, send_ref, normed_ref, gate_ref,
):
    step = pl.program_id(0)
    is_last = last_matrix(lengths_ref, block_ref[0] * ROWS + lane_of((REQS, ROWS)))

    @pl.when(step == 0)
    def _():
        normed_ref[...] = rms_scale(tok_ref[...].astype(f32), gain_ref[...]).astype(bf16)
        row = lax.broadcasted_iota(jnp.int32, (LANES, ROWS), 0)
        named = row % EXPERTS
        weight = jnp.where(
            routes_ref[0:1, :] == named,
            gates_ref[0:1, :],
            jnp.where(routes_ref[1:2, :] == named, gates_ref[1:2, :], 0.0),
        )
        high, middle, low = three_parts(weight)
        piece = row // EXPERTS
        pieces = jnp.where(
            piece == 0, high, jnp.where(piece == 1, middle, jnp.where(piece == 2, low, 0.0))
        )
        gate_ref[...] = lax.dot_general(
            is_last, pieces.astype(bf16), (((1,), (1,)), ((), ())), preferred_element_type=f32
        ).astype(bf16)

    normed = normed_ref[...]
    query = jnp.dot(normed, wq_ref[...], preferred_element_type=f32).astype(bf16)
    key = jnp.dot(normed, wk_ref[...], preferred_element_type=f32).astype(bf16)
    value = jnp.dot(normed, wv_ref[...], preferred_element_type=f32).astype(bf16)
    column = pl.multiple_of(step * PAIRS * LANES, PAIRS * LANES)
    kv_ref[:, pl.ds(column, PAIRS * LANES)] = key
    kv_ref[:, pl.ds(HEADS * HALF + column, PAIRS * LANES)] = value
    wide = pl.multiple_of(step * 2 * PAIRS * LANES, 2 * PAIRS * LANES)
    ends = jnp.dot(
        is_last, tok_ref[:, pl.ds(wide, 2 * PAIRS * LANES)], preferred_element_type=f32
    ).astype(bf16)
    scaled = query.astype(f32) * (HALF**-0.5)
    for pair in range(PAIRS):
        lanes = slice(pair * LANES, (pair + 1) * LANES)
        even, odd = head_split(key[:, lanes].astype(f32), value[:, lanes].astype(f32))
        even = even.astype(bf16)
        odd = odd.astype(bf16)
        for quarter in range(QUARTERS):
            first = scaled[quarter * 32 : quarter * 32 + 16, lanes]
            second = scaled[quarter * 32 + 16 : quarter * 32 + 32, lanes]
            query_even, query_odd = head_split(first, second)
            send_ref[2 * pair, quarter, 0:ROWS, :] = even
            send_ref[2 * pair + 1, quarter, 0:ROWS, :] = odd
            send_ref[2 * pair, quarter, ROWS : ROWS + 16, :] = query_even.astype(bf16)
            send_ref[2 * pair + 1, quarter, ROWS : ROWS + 16, :] = query_odd.astype(bf16)
            for which in range(2 * pair, 2 * pair + 2):
                send_ref[which, quarter, ROWS + 16 : ROWS + 32, :] = ends[
                    :, which * LANES : (which + 1) * LANES
                ]
                send_ref[which, quarter, ROWS + 32 : ROWS + 48, :] = gate_ref[...]


def project(block, lengths, stream, gain, w_query, w_keyval, routes_t, gates_t):
    width = stream.shape[1]
    return pl.pallas_call(
        project_kernel,
        grid_spec=pltpu.PrefetchScalarGridSpec(
            num_scalar_prefetch=2,
            grid=(HEADS // 2 // PAIRS,),
            in_specs=[
                pl.BlockSpec((ROWS, width), lambda i, b, l: (0, 0)),
                pl.BlockSpec((1, width), lambda i, b, l: (0, 0)),
                pl.BlockSpec((width, PAIRS * LANES), lambda i, b, l: (0, i)),
                pl.BlockSpec((width, PAIRS * LANES), lambda i, b, l: (0, i)),
                pl.BlockSpec((width, PAIRS * LANES), lambda i, b, l: (0, i + HEADS // 2 // PAIRS)),
                pl.BlockSpec((2, ROWS), lambda i, b, l: (0, 0)),
                pl.BlockSpec((2, ROWS), lambda i, b, l: (0, 0)),
            ],
            out_specs=[
                pl.BlockSpec((ROWS, 2 * HEADS * HALF), lambda i, b, l: (0, 0)),
                pl.BlockSpec((2 * PAIRS, QUARTERS, SEND_ROWS, LANES), lambda i, b, l: (i, 0, 0, 0)),
            ],
            scratch_shapes=[pltpu.VMEM((ROWS, width), bf16), pltpu.VMEM((REQS, LANES), bf16)],
        ),
        out_shape=[
            jax.ShapeDtypeStruct((ROWS, 2 * HEADS * HALF), bf16),
            jax.ShapeDtypeStruct((HEADS, QUARTERS, SEND_ROWS, LANES), bf16),
        ],
        compiler_params=pltpu.CompilerParams(vmem_limit_bytes=24 << 20),
        name="project",
    )(block, *in_hbm(lengths, stream, gain, w_query, w_keyval, w_keyval, routes_t, gates_t))


def prefix_pack_kernel(offset_ref, got_ref, *refs):
    pieces = refs[: len(refs) - 5]
    out_ref, prefix_v, ends_v, sem, ends_sem = refs[len(refs) - 5 :]
    ends_copy = pltpu.make_async_copy(
        got_ref.at[:, pl.ds(ROWS + 16, REQS), :], ends_v, ends_sem
    )
    ends_copy.start()
    for k, piece in enumerate(pieces):

        @pl.when(offset_ref[0] == k)
        def _():
            copy = pltpu.make_async_copy(piece, prefix_v, sem)
            copy.start()
            copy.wait()

    rows = prefix_v.shape[0]
    ends_copy.wait()
    ends = jnp.sum(ends_v[...].astype(f32), axis=0).astype(bf16)
    for head in range(HEADS):
        for quarter in range(QUARTERS):
            out_ref[head, quarter, rows : rows + REQS, :] = ends
    for pair in range(HEADS // 2):
        key = prefix_v[:, pair * LANES : (pair + 1) * LANES].astype(f32)
        base = HEADS * HALF + pair * LANES
        value = prefix_v[:, base : base + LANES].astype(f32)
        even, odd = head_split(key, value)
        for quarter in range(QUARTERS):
            out_ref[2 * pair, quarter, 0:rows, :] = even.astype(bf16)
            out_ref[2 * pair + 1, quarter, 0:rows, :] = odd.astype(bf16)


def prefix_pack(pieces, offset, got):
    rows, width = pieces[0].shape
    return pl.pallas_call(
        prefix_pack_kernel,
        grid_spec=pltpu.PrefetchScalarGridSpec(
            num_scalar_prefetch=1,
            grid=(1,),
            in_specs=[pl.BlockSpec(memory_space=pl.ANY)] * (1 + len(pieces)),
            out_specs=pl.BlockSpec(
                (HEADS, QUARTERS, rows + REQS, LANES), lambda i, owner: (0, 0, 0, 0)
            ),
            scratch_shapes=[
                pltpu.VMEM((rows, width), bf16),
                pltpu.VMEM((got.shape[0], REQS, LANES), bf16),
                pltpu.SemaphoreType.DMA(()),
                pltpu.SemaphoreType.DMA(()),
            ],
        ),
        out_shape=jax.ShapeDtypeStruct((HEADS, QUARTERS, rows + REQS, LANES), bf16),
        name="prefix_pack",
    )(offset, *in_hbm(got, *pieces))


def query_tile(query_ref):
    packed = query_ref[...].reshape(QUERY_TILE // 2, LANES).astype(f32)
    low = lane_of(packed.shape) < HALF
    first = jnp.where(low, packed, 0.0)
    second = jnp.where(low, pltpu.roll(packed, HALF, 1), 0.0)
    return jnp.concatenate([first, second], axis=0).astype(bf16)


def offset_of(row):
    half_rows = QUERY_TILE // 2
    second = (row >= half_rows).astype(jnp.int32)
    within = row - second * half_rows
    return (within // 16) * ROWS + second * 16 + within % 16


def start_of(position, lengths_ref, zero):
    end = jnp.int32(0)
    start = zero
    for request in range(REQS):
        end = end + lengths_ref[request]
        start = jnp.where(position >= end, end, start)
    return start


def suffix_kernel(quarter_ref, lengths_ref, query_ref, got_ref, out_ref):
    tile = pl.program_id(0)
    blocks = QUERY_TILE // 32
    key_blocks = KEY_TILE // ROWS
    query = query_tile(query_ref)
    first_position = tile * blocks * ROWS + quarter_ref[0] * 32
    position = first_position + offset_of(lax.broadcasted_iota(jnp.int32, (QUERY_TILE, 1), 0))
    start = start_of(position, lengths_ref, jnp.zeros_like(position))
    lowest = start_of(first_position, lengths_ref, jnp.int32(0))
    span = blocks * ROWS
    last_tile = (tile * span + span - 1) // KEY_TILE

    def step(j, carry):
        acc, top, total = carry
        keys = got_ref[pl.ds(j * key_blocks, key_blocks), :, :].reshape(KEY_TILE, LANES)
        scores = lax.dot_general(
            query, keys, (((1,), (1,)), ((), ())), preferred_element_type=f32
        )
        key_position = j * KEY_TILE + lane_of(scores.shape)
        allowed = (key_position >= start) & (key_position <= position)
        scores = jnp.where(allowed, scores, neg_big)
        new_top = jnp.maximum(top, jnp.max(scores, axis=1, keepdims=True))
        shrink = jnp.exp(top - new_top)
        probs = jnp.exp(scores - new_top)
        total = total * shrink + jnp.sum(probs, axis=1, keepdims=True)
        acc = acc * shrink + jnp.dot(probs.astype(bf16), keys, preferred_element_type=f32)
        return acc, new_top, total

    acc, top, total = lax.fori_loop(
        lowest // KEY_TILE,
        last_tile + 1,
        step,
        (
            jnp.zeros((QUERY_TILE, LANES), f32),
            jnp.full((QUERY_TILE, 1), neg_big, f32),
            jnp.zeros((QUERY_TILE, 1), f32),
        ),
    )
    lane = lane_of(acc.shape)
    out_ref[...] = jnp.where(lane == 0, top, jnp.where(lane == 1, total, acc))


def suffix_attention(quarter, lengths, got):
    blocks = got.shape[0]
    queries = blocks * 32
    return pl.pallas_call(
        suffix_kernel,
        grid_spec=pltpu.PrefetchScalarGridSpec(
            num_scalar_prefetch=2,
            grid=(queries // QUERY_TILE,),
            in_specs=[
                pl.BlockSpec((QUERY_TILE // 32, 16, LANES), lambda i, q, l: (i, ROWS // 16, 0)),
                pl.BlockSpec((blocks, ROWS, LANES), lambda i, q, l: (0, 0, 0)),
            ],
            out_specs=pl.BlockSpec((QUERY_TILE, LANES), lambda i, q, l: (i, 0)),
        ),
        out_shape=pltpu.HBM((queries, LANES), f32),
        compiler_params=pltpu.CompilerParams(vmem_limit_bytes=14 << 20),
        name="suffix_attention",
    )(quarter, lengths, *in_hbm(got, got))


def prefix_kernel(quarter_ref, lengths_ref, query_ref, keys_ref, part_ref, out_ref, last_ref):
    tile = pl.program_id(0)
    tile_blocks = PREFIX_TILE // 32
    half_rows = PREFIX_TILE // 2
    packed = query_ref[...].reshape(half_rows, LANES).astype(f32)
    low = lane_of(packed.shape) < HALF
    query = jnp.concatenate(
        [jnp.where(low, packed, 0.0), jnp.where(low, pltpu.roll(packed, HALF, 1), 0.0)], axis=0
    ).astype(bf16)
    keys = keys_ref[...].reshape(-1, LANES)
    subs = PREFIX_TILE // PREFIX_SUB

    def score(sub):
        rows = slice(sub * PREFIX_SUB, (sub + 1) * PREFIX_SUB)
        return lax.dot_general(
            query[rows], keys, (((1,), (1,)), ((), ())), preferred_element_type=f32
        )

    def part_rows(sub):
        pieces = []
        per = QUERY_TILE // 2
        for start in range(sub * PREFIX_SUB, (sub + 1) * PREFIX_SUB, min(per, PREFIX_SUB)):
            second, rest = divmod(start, half_rows)
            group, inside = divmod(rest, per)
            first = group * QUERY_TILE + second * per + inside
            pieces.append(part_ref[first : first + min(per, PREFIX_SUB), :])
        return pieces[0] if len(pieces) == 1 else jnp.concatenate(pieces, axis=0)

    contexts = []
    scores = score(0)
    for sub in range(subs):
        following = score(sub + 1) if sub + 1 < subs else None
        part = part_rows(sub)
        part_top = part[:, 0:1]
        part_total = part[:, 1:2]
        top = jnp.maximum(part_top, jnp.max(scores, axis=1, keepdims=True))
        probs = jnp.exp(scores - top)
        shrink = jnp.exp(part_top - top)
        total = part_total * shrink + jnp.sum(probs, axis=1, keepdims=True)
        acc = part * shrink + jnp.dot(probs.astype(bf16), keys, preferred_element_type=f32)
        contexts.append(acc / total)
        scores = following
    context = contexts[0] if subs == 1 else jnp.concatenate(contexts, axis=0)
    packed = jnp.where(low, pltpu.roll(context[:half_rows], HALF, 1), context[half_rows:])
    out_ref[pl.ds(tile * tile_blocks, tile_blocks), 0:16, :] = packed.astype(bf16).reshape(
        tile_blocks, 16, LANES
    )
    row = lane_of((REQS, PREFIX_TILE))
    second = (row >= half_rows).astype(jnp.int32)
    within = row - second * half_rows
    positions = tile * tile_blocks * ROWS + quarter_ref[0] * 32
    positions = positions + (within // 16) * ROWS + second * 16 + within % 16
    is_last = last_matrix(lengths_ref, positions)
    ends = jnp.where(lane_of(context.shape) < HALF, 0.0, context).astype(bf16)
    ends = jnp.dot(is_last, ends, preferred_element_type=f32)

    @pl.when(tile == 0)
    def _():
        last_ref[...] = ends

    @pl.when(tile > 0)
    def _():
        last_ref[...] = last_ref[...] + ends

    @pl.when(tile == pl.num_programs(0) - 1)
    def _():
        every = last_ref[...].astype(bf16)
        for block in range(out_ref.shape[0]):
            out_ref[block, 16:32, :] = every


def prefix_attention(quarter, lengths, got, keys, part):
    blocks = got.shape[0]
    queries = blocks * 32
    rows = keys.shape[1] - REQS
    return pl.pallas_call(
        prefix_kernel,
        grid_spec=pltpu.PrefetchScalarGridSpec(
            num_scalar_prefetch=2,
            grid=(queries // PREFIX_TILE,),
            in_specs=[
                pl.BlockSpec((PREFIX_TILE // 32, 16, LANES), lambda i, q, l: (i, ROWS // 16, 0)),
                pl.BlockSpec((blocks, rows, LANES), lambda i, q, l: (0, 0, 0)),
                pl.BlockSpec((PREFIX_TILE, LANES), lambda i, q, l: (i, 0)),
            ],
            out_specs=pl.BlockSpec((blocks, 32, LANES), lambda i, q, l: (0, 0, 0)),
            scratch_shapes=[pltpu.VMEM((REQS, LANES), f32)],
        ),
        out_shape=jax.ShapeDtypeStruct((blocks, 32, LANES), bf16),
        compiler_params=pltpu.CompilerParams(vmem_limit_bytes=18 << 20),
        name="prefix_attention",
    )(quarter, lengths, *in_hbm(got, keys, part))


def gelu(v):
    scale = 0.7978845608028654
    half = 0.5 * v
    return half + half * jnp.tanh(v * (scale + (scale * 0.044715) * (v * v)))


def dot_nt(a, b):
    return lax.dot_general(a, b, (((1,), (1,)), ((), ())), preferred_element_type=f32)


def mix_kernel(
    block_ref, ctx_ref, tok_ref, tok_last_ref, gate_last_ref, wout_ref, gain_ref, routes_ref, g_ref, u_ref, d_ref,
    mixed_ref, mixed_last_ref, send_ref, wout_v, send_v, wout_sem, out_sems,
):
    lift_copy = pltpu.make_async_copy(wout_ref, wout_v, wout_sem)
    lift_copy.start()
    tiles = []
    for pair in range(HEADS // 2):
        even = ctx_ref[2 * pair].astype(f32)
        odd = ctx_ref[2 * pair + 1].astype(f32)
        first, second = head_split(even[:, 0:16], odd[:, 0:16])
        both = jnp.stack([first, second], axis=1).reshape(ROWS, LANES)
        even_last = jnp.sum(even[:, 16:32], axis=0)
        odd_last = jnp.sum(odd[:, 16:32], axis=0)
        low = lane_of(even_last.shape) < HALF
        ends = jnp.where(low, pltpu.roll(even_last, HALF, 1), odd_last)
        tiles.append(jnp.concatenate([both, ends], axis=0).astype(bf16))
    context = jnp.concatenate(tiles, axis=1)
    lift_copy.wait()
    lift = jnp.dot(context, wout_v[...], preferred_element_type=f32)
    mixed = tok_ref[...].astype(f32) + lift[:ROWS]
    mixed_ref[...] = mixed
    routed = rms_scale(mixed, gain_ref[...]).astype(bf16)
    tok_last = jnp.concatenate([tok_last_ref[QUARTERS * j] for j in range(8)], axis=1)
    mixed_last = tok_last.astype(f32) + lift[ROWS:]
    mixed_last_ref[...] = mixed_last
    routed_last = rms_scale(mixed_last, gain_ref[...]).astype(bf16)
    expert_id = block_ref[0] // QUARTERS
    weights = jnp.sum(gate_last_ref[...].astype(f32), axis=0)
    lane = lane_of(weights.shape)
    mine = (lane % EXPERTS == expert_id) & (lane < 3 * EXPERTS)
    weight = jnp.sum(jnp.where(mine, weights, 0.0), axis=1, keepdims=True)
    act = (gelu(dot_nt(routed_last, g_ref[...])) * dot_nt(routed_last, u_ref[...])).astype(bf16)
    partial_last = weight * jnp.dot(act, d_ref[...], preferred_element_type=f32)
    high = partial_last.astype(bf16)
    low_part = (partial_last - high.astype(f32)).astype(bf16)
    source = jnp.concatenate([routed, high, low_part], axis=0)
    expert = lax.broadcasted_iota(jnp.int32, (EXPERTS, ROWS), 0)
    named = (routes_ref[0:1, :] == expert) | (routes_ref[1:2, :] == expert)
    earlier = (
        lax.broadcasted_iota(jnp.int32, (ROWS, ROWS), 0)
        < lax.broadcasted_iota(jnp.int32, (ROWS, ROWS), 1)
    ).astype(bf16)
    slots = jnp.dot(named.astype(f32).astype(bf16), earlier, preferred_element_type=f32)
    slots = jnp.where(named, slots, -1.0).astype(jnp.int32)
    place = slots + jnp.where(slots >= PART_SLOTS, PART_ROWS - PART_SLOTS, 0)
    place_id = lax.broadcasted_iota(jnp.int32, (SLOT_ROWS, ROWS), 0)
    extra_row = lax.broadcasted_iota(jnp.int32, (SLOT_ROWS, 2 * REQS), 0) % PART_ROWS
    extra_column = lane_of((SLOT_ROWS, 2 * REQS))
    picks = []
    for e in range(EXPERTS):
        pick = (place[e : e + 1, :] == place_id).astype(f32)
        for chip in range(2):
            row_last = 2 * e + chip
            extra = ((extra_row == PART_SLOTS) & (extra_column == row_last)) | (
                (extra_row == PART_SLOTS + 1) & (extra_column == REQS + row_last)
            )
            picks.append(jnp.concatenate([pick, extra.astype(f32)], axis=1).astype(bf16))
    sends = []
    per = len(picks) // MIX_PARTS
    rows = per * SLOT_ROWS
    for part in range(MIX_PARTS):
        chosen = jnp.concatenate(picks[part * per : (part + 1) * per], axis=0)
        send_v[part] = jnp.dot(chosen, source, preferred_element_type=f32).astype(bf16)
        send = pltpu.make_async_copy(
            send_v.at[part], send_ref.at[pl.ds(part * rows, rows), :], out_sems.at[part]
        )
        send.start()
        sends.append(send)
    for send in sends:
        send.wait()


MIX_PARTS = 2


def mix(block, ctx, stream, prefix_got, got, w_out, gain, routes_t, own):
    width = stream.shape[1]
    blocks = got.shape[0]
    units = own[0].shape[0]
    def whole(shape):
        return pl.BlockSpec(shape, lambda i, b: (0,) * len(shape))

    return pl.pallas_call(
        mix_kernel,
        grid_spec=pltpu.PrefetchScalarGridSpec(
            num_scalar_prefetch=1,
            grid=(1,),
            in_specs=[
                whole(ctx.shape),
                whole(stream.shape),
                pl.BlockSpec((blocks, REQS, LANES), lambda i, b: (0, 4, 0)),
                pl.BlockSpec((blocks, REQS, LANES), lambda i, b: (0, 10, 0)),
                pl.BlockSpec(memory_space=pl.ANY),
                whole(gain.shape),
                whole(routes_t.shape),
                whole((units, width)),
                whole((units, width)),
                whole((units, width)),
            ],
            out_specs=[
                whole((ROWS, width)),
                whole((REQS, width)),
                pl.BlockSpec(memory_space=pltpu.HBM),
            ],
            scratch_shapes=[
                pltpu.VMEM(w_out.shape, bf16),
                pltpu.VMEM((MIX_PARTS, 2 * EXPERTS * SLOT_ROWS // MIX_PARTS, width), bf16),
                pltpu.SemaphoreType.DMA(()),
                pltpu.SemaphoreType.DMA((MIX_PARTS,)),
            ],
        ),
        out_shape=[
            pltpu.HBM((ROWS, width), f32),
            pltpu.HBM((REQS, width), f32),
            pltpu.HBM((2 * EXPERTS * SLOT_ROWS, width), bf16),
        ],
        compiler_params=pltpu.CompilerParams(vmem_limit_bytes=18 << 20),
        name="mix",
    )(block, ctx, stream, *in_hbm(prefix_got, got, w_out), gain, routes_t, *own)


FFN_TILE = 256


def expert_kernel(
    x_ref, g0, u0, d0, g1, u1, d1, out_ref, acc_v, out_v, out_sems
):
    weights = ((g0, u0, d0), (g1, u1, d1))
    count = x_ref.shape[0]
    within = lane_of((16, count)) % PART_ROWS
    extra = ((within == PART_SLOTS) | (within == PART_SLOTS + 1)).astype(f32).astype(bf16)
    total = jnp.dot(extra, x_ref[...], preferred_element_type=f32)[0:1]
    high = total.astype(bf16).astype(f32)
    low = (total - high).astype(bf16).astype(f32)
    sends = []
    tiles = count // FFN_TILE
    work = [(part, tile) for part in range(2) for tile in range(tiles)]

    def span(tile):
        return slice(tile * FFN_TILE, (tile + 1) * FFN_TILE)

    def lift(part, tile):
        x = x_ref[span(tile), :]
        return dot_nt(x, weights[part][0][...]), dot_nt(x, weights[part][1][...])

    ready = lift(*work[0])
    for index, (part, tile) in enumerate(work):
        gate, up = ready
        if index + 1 < len(work):
            ready = lift(*work[index + 1])
        hidden = (gelu(gate) * up).astype(bf16)
        down = jnp.dot(hidden, weights[part][2][...], preferred_element_type=f32)
        if part == 0:
            acc_v[span(tile), :] = down
        else:
            row = tile * FFN_TILE + lax.broadcasted_iota(jnp.int32, (FFN_TILE, 1), 0)
            row = row % PART_ROWS
            result = acc_v[span(tile), :] + down
            result = jnp.where(row == PART_SLOTS, high, result)
            result = jnp.where(row == PART_SLOTS + 1, low, result)
            out_v[span(tile), :] = result.astype(bf16)
            send = pltpu.make_async_copy(
                out_v.at[pl.ds(tile * FFN_TILE, FFN_TILE), :],
                out_ref.at[pl.ds(tile * FFN_TILE, FFN_TILE), :],
                out_sems.at[tile],
            )
            send.start()
            sends.append(send)
    for send in sends:
        send.wait()


def expert(rows, own, other):
    count, width = rows.shape
    vmem = pl.BlockSpec(memory_space=pltpu.VMEM)
    return pl.pallas_call(
        expert_kernel,
        in_specs=[vmem] * 7,
        out_specs=pl.BlockSpec(memory_space=pltpu.HBM),
        out_shape=pltpu.HBM((count, width), bf16),
        scratch_shapes=[
            pltpu.VMEM((count, width), f32),
            pltpu.VMEM((count, width), bf16),
            pltpu.SemaphoreType.DMA((count // FFN_TILE,)),
        ],
        compiler_params=pltpu.CompilerParams(vmem_limit_bytes=26 << 20),
        name="expert",
    )(rows, *own, *other)


def column_of(row):
    return jnp.transpose(jnp.broadcast_to(row, (ROWS, LANES)))


def combine_kernel(
    block_ref, lengths_ref, mixed_ref, mixed_last_ref, got_ref, routes_ref, gates_ref, gain_ref,
    unembed_ref, hidden_ref, packet_ref,
):
    got = got_ref[...]
    count = got.shape[0]
    request_row = lax.broadcasted_iota(jnp.int32, (REQS, count), 0)
    wanted = request_row * (2 * PART_ROWS) + PART_SLOTS
    source = lane_of((REQS, count))
    pick_last = ((source == wanted) | (source == wanted + 1)).astype(f32).astype(bf16)
    first = column_of(routes_ref[0:1, :].astype(f32)).astype(jnp.int32)
    second = column_of(routes_ref[1:2, :].astype(f32)).astype(jnp.int32)
    lane = lane_of((ROWS, LANES))
    named = ((first == lane) | (second == lane)).astype(f32).astype(bf16)
    earlier = (
        lax.broadcasted_iota(jnp.int32, (ROWS, ROWS), 1)
        < lax.broadcasted_iota(jnp.int32, (ROWS, ROWS), 0)
    ).astype(bf16)
    slots = jnp.dot(earlier, named, preferred_element_type=f32)
    column = lane_of((ROWS, count))
    picks = [pick_last]
    for chosen in (first, second):
        slot = jnp.sum(jnp.where(chosen == lane, slots, 0.0), axis=1, keepdims=True)
        slot = slot.astype(jnp.int32)
        place = slot + jnp.where(slot >= PART_SLOTS, PART_ROWS - PART_SLOTS, 0)
        target = chosen[:, 0:1] * (2 * SLOT_ROWS) + place
        pick = ((column == target) | (column == target + SLOT_ROWS)).astype(f32).astype(bf16)
        picks.append(pick)
    picked = jnp.dot(jnp.concatenate(picks, axis=0), got, preferred_element_type=f32)
    hidden_last = (mixed_last_ref[...] + picked[:REQS]).astype(bf16).astype(f32)
    last_rows = rms_scale(hidden_last, gain_ref[...]).astype(bf16)
    best = jnp.max(dot_nt(last_rows, unembed_ref[...]), axis=1, keepdims=True)
    request = lax.broadcasted_iota(jnp.int32, (REQS, LANES), 0)
    best = jnp.where(lane_of((REQS, LANES)) == request + REQS, best, 0.0)
    best = jnp.sum(best, axis=0, keepdims=True)
    moe = column_of(gates_ref[0:1, :])[:, 0:1] * picked[REQS : REQS + ROWS]
    moe = moe + column_of(gates_ref[1:2, :])[:, 0:1] * picked[REQS + ROWS :]
    hidden = (mixed_ref[...] + moe).astype(bf16)
    hidden_ref[...] = hidden
    wide = hidden.astype(f32)
    squares = jnp.sum(wide * wide, axis=1, keepdims=True)
    position = block_ref[0] * ROWS + lax.broadcasted_iota(jnp.int32, (ROWS, LANES), 0)
    starts = jnp.zeros((1, LANES), jnp.int32)
    ends = jnp.zeros((1, LANES), jnp.int32)
    lane_row = lane_of((1, LANES))
    end = jnp.int32(0)
    for r in range(REQS):
        starts = jnp.where(lane_row == r, end, starts)
        end = end + lengths_ref[r]
        ends = jnp.where(lane_row == r, end, ends)
    member = (position >= starts) & (position < ends)
    packet_ref[...] = best + jnp.sum(jnp.where(member, squares, 0.0), axis=0, keepdims=True)


def combine(block, lengths, mixed, mixed_last, got, routes, gates, gain, unembed):
    width = mixed.shape[1]
    vmem = pl.BlockSpec(memory_space=pltpu.VMEM)
    smem = pl.BlockSpec(memory_space=pltpu.SMEM)
    return pl.pallas_call(
        combine_kernel,
        in_specs=[smem, smem] + [vmem] * 7,
        out_specs=[vmem] * 2,
        out_shape=[
            jax.ShapeDtypeStruct((ROWS, width), bf16),
            jax.ShapeDtypeStruct((1, LANES), f32),
        ],
        compiler_params=pltpu.CompilerParams(vmem_limit_bytes=16 << 20),
        name="combine",
    )(block, lengths, mixed, mixed_last, got, routes, gates, gain, unembed)


def exchange(rows):
    return lax.all_to_all(rows, "blk", split_axis=0, concat_axis=0, tiled=True)


def ring_pieces(piece):
    size = lax.axis_size("grp")

    def shift(one, by):
        return lax.ppermute(one, "grp", [(i, (i + by) % size) for i in range(size)])

    pieces = {0: piece}
    for by in (1, 2, -1):
        pieces[by % size] = shift(piece, by)
    pieces[6] = shift(pieces[7], -1)
    pieces[3] = shift(pieces[2], 1)
    pieces[4] = shift(pieces[2], 2)
    pieces[5] = shift(pieces[7], -2)
    return [pieces[k] for k in range(size)]


def local(
    tokens,
    lengths,
    owners,
    prefix_cache,
    routes,
    gates,
    attn_gain,
    w_query,
    w_keyval,
    w_out,
    moe_gain,
    w_gate,
    w_up,
    w_down,
    final_gain,
    unembed,
):
    blocks = lax.axis_size("blk")
    block_index = lax.axis_index("blk")
    width = tokens.shape[2]
    stream = tokens[0]
    block = block_index.astype(jnp.int32).reshape(1)
    quarter = block % QUARTERS
    swap = [(i, i ^ 1) for i in range(blocks)]
    with jax.named_scope("prefix_gather"):
        pieces = ring_pieces(prefix_cache[0])
        offset = (lax.axis_index("grp").astype(jnp.int32) - owners) % len(pieces)
    own = (w_gate[0].T, w_up[0].T, w_down[0])
    routes_t = routes[0].T
    gates_t = gates[0].T
    suffix_kv, send = project(
        block, lengths[0], stream, attn_gain.reshape(1, -1), w_query, w_keyval, routes_t, gates_t
    )
    with jax.named_scope("qkv_exchange"):
        got = exchange(send.reshape(blocks, SEND_ROWS, LANES))
    packed = prefix_pack(pieces, offset, got)
    with jax.named_scope("weight_swap"):
        packed, *ready = lax.optimization_barrier((packed, *own))
        other = [lax.ppermute(one, "blk", swap) for one in ready]
    with jax.named_scope("prefix_exchange"):
        prefix_got = exchange(packed.reshape(blocks, packed.shape[2], LANES))
    part = suffix_attention(quarter, lengths[0], got)
    part, *other = lax.optimization_barrier((part, *other))
    context = prefix_attention(quarter, lengths[0], got, prefix_got, part)
    with jax.named_scope("context_exchange"):
        ctx = exchange(context).reshape(HEADS, QUARTERS, 32, LANES)
    mixed, mixed_last, outgoing = mix(
        block, ctx, stream, prefix_got, got, w_out, moe_gain.reshape(1, -1), routes_t, own
    )
    with jax.named_scope("dispatch_exchange"):
        rows = exchange(outgoing.reshape(blocks, PART_ROWS, width))
    results = expert(rows.reshape(-1, width), own, other)
    with jax.named_scope("return_exchange"):
        returned = exchange(results.reshape(blocks, PART_ROWS, width)).reshape(-1, width)
    hidden, packet = combine(
        block,
        lengths[0],
        mixed,
        mixed_last,
        returned,
        routes_t,
        gates_t,
        final_gain.reshape(1, -1),
        unembed.T,
    )
    with jax.named_scope("final_exchange"):
        final = exchange(jnp.broadcast_to(packet[None], (blocks, 1, LANES)))[:, 0, :]
    norm_sums = jnp.sum(final[:, :REQS], axis=0)
    greatest = jnp.max(final[:, REQS : 2 * REQS], axis=0)
    request_norm = jnp.sqrt(norm_sums / (lengths[0].astype(f32) * width))
    return (hidden[None], suffix_kv[None], request_norm[None], greatest[None])


def solution(mesh):
    placed = (
        P("grp", "blk", None),
        P("grp", None),
        P("grp"),
        P("grp", "blk", None),
        P("grp", "blk", None),
        P("grp", "blk", None),
        P(),
        P(),
        P(),
        P(),
        P(),
        P("blk", None, None),
        P("blk", None, None),
        P("blk", None, None),
        P(),
        P(None, "blk"),
    )
    return jax.shard_map(
        local,
        mesh=mesh,
        in_specs=placed,
        out_specs=(P("grp", "blk", None), P("grp", "blk", None), P("grp", None), P("grp", None)),
        check_vma=False,
    )
```
